128 devices in a mesh: segment: 4 (over y), tensor: 16 (over z, x), dp: 2 (over core).
Axes of the slice: x: 4, y: 4, z: 4, core: 2. Of those that a mesh axis runs over, the one named last changes fastest.
Arguments:
- tokens: bfloat16 [2, 256, 8192], P('dp', 'tensor'), may hold values from -6 to 6
- cotangent: bfloat16 [2, 256, 8192], P('dp', 'tensor'), may hold values from -1.1953125 to 1.1953125
- sequence_job: int32 [2], P('dp'), may hold values from 0 to 31
- section_layer_list: int32 [4], replicated, may hold values from 0 to 1, as said below
- section_norm_gain: bfloat16 [4, 8192], P('segment'), may hold values from 0.099609375 to 1.8984375
- query_matrix: bfloat16 [4, 8192, 4096], P('segment', None, 'tensor'), may hold values from -0.0625 to 0.0625
- key_matrix: bfloat16 [4, 8192, 512], P('segment', None, 'tensor'), may hold values from -0.0625 to 0.0625
- value_matrix: bfloat16 [4, 8192, 512], P('segment', None, 'tensor'), may hold values from -0.0625 to 0.0625
- output_matrix: bfloat16 [4, 4096, 8192], P('segment', 'tensor'), may hold values from -0.09375 to 0.09375
- adapter_down_all: bfloat16 [4, 8192, 512], P('segment', 'tensor'), may hold values from -0.0625 to 0.0625
- adapter_up_all: bfloat16 [4, 512, 4096], P('segment', None, 'tensor'), may hold values from -0.09375 to 0.09375
Outputs:
- grad_down: float32 [4, 8192, 512], P('segment', 'tensor')
- grad_up: float32 [4, 512, 4096], P('segment', None, 'tensor')
The draws below stay inside these ranges and needn't reach their ends.
Inputs may be any that keep to these rules, and one draw needn't show every extreme that they name: `section_layer_list`: at least one section applies no layer and at least one applies one; each of the others applies none or one.
All inputs are finite; a program needn't handle non-finite values.
Results may differ from the reference program's by a relative error of at most 0.035.
Values may be sent and summed in bfloat16 or wider, within the bound.
A program may use at most 192 MiB of HBM per device.

```python
import math
import jax
import jax.numpy as jnp
from jax import lax

MODEL_WIDTH = 8192
QUERY_HEADS = 32
KV_HEADS = 4
HEAD_SIZE = 128
ADAPTER_RANK = 16
ADAPTER_JOBS = 32
SEQUENCE_TOKENS = 256
NBLK = 2
N_SEGMENT = 4
N_TENSOR = 16


def draw_section_layer_list(key, part):
    bit_key = jax.random.fold_in(key, 11)
    order_key = jax.random.fold_in(key, 23)
    bits = jax.random.randint(bit_key, (N_SEGMENT,), 0, 2, dtype=jnp.int32)
    order = jax.random.permutation(order_key, N_SEGMENT)
    bits = bits.at[order[0]].set(0)
    bits = bits.at[order[1]].set(1)
    return bits.astype(jnp.int32)


def steps_of(stream_key, shape, pieces, low, top_value):
    gain, own = 1.0, jax.random.fold_in(stream_key, 6)
    for axis_at, shards_of in pieces:
        steps = jnp.exp(jax.random.uniform(jax.random.fold_in(own, axis_at), (shards_of,), jnp.float32, low / len(pieces), top_value / len(pieces)))
        gain = gain * jnp.repeat(steps, shape[axis_at] // shards_of).reshape([-1 if axis == axis_at else 1 for axis in range(len(shape))])
    return gain


def bell_draw(key, extent, width, most, shards=(), kind=jnp.bfloat16):
    entries = width * jax.random.normal(key, extent, jnp.float32)
    if shards:
        entries = entries * steps_of(key, extent, shards, -0.22, 0.18)
    return jnp.clip(entries, -most, most).astype(kind)


def setup_inputs(seed: int = 0) -> dict:
    key_list = jax.random.split(jax.random.key(seed), 12)
    return {
        "tokens": bell_draw(key_list[0], (NBLK, SEQUENCE_TOKENS, MODEL_WIDTH), 1.0, 6.0, ((0, 2), (1, 16))),
        "cotangent": bell_draw(key_list[1], (NBLK, SEQUENCE_TOKENS, MODEL_WIDTH), 0.2, 1.1953125, ((0, 2), (1, 16))),
        "sequence_job": jax.random.randint(key_list[2], (NBLK,), 0, ADAPTER_JOBS).astype(jnp.int32),
        "section_layer_list": draw_section_layer_list(jax.random.fold_in(key_list[11], 71), 0),
        "section_norm_gain": jnp.clip(1.0 + 0.18 * jax.random.normal(key_list[4], (N_SEGMENT, MODEL_WIDTH), jnp.float32), 0.099609375, 1.8984375).astype(jnp.bfloat16),
        "query_matrix": bell_draw(key_list[5], (N_SEGMENT, MODEL_WIDTH, QUERY_HEADS * HEAD_SIZE), MODEL_WIDTH ** -0.5, 0.0625, ((0, 4), (2, 16))),
        "key_matrix": bell_draw(key_list[6], (N_SEGMENT, MODEL_WIDTH, KV_HEADS * HEAD_SIZE), MODEL_WIDTH ** -0.5, 0.0625, ((0, 4), (2, 16))),
        "value_matrix": bell_draw(key_list[7], (N_SEGMENT, MODEL_WIDTH, KV_HEADS * HEAD_SIZE), MODEL_WIDTH ** -0.5, 0.0625, ((0, 4), (2, 16))),
        "output_matrix": bell_draw(key_list[8], (N_SEGMENT, QUERY_HEADS * HEAD_SIZE, MODEL_WIDTH), (QUERY_HEADS * HEAD_SIZE) ** -0.5, 0.09375, ((0, 4), (1, 16))),
        "adapter_down_all": bell_draw(key_list[9], (N_SEGMENT, MODEL_WIDTH, ADAPTER_JOBS * ADAPTER_RANK), MODEL_WIDTH ** -0.5, 0.0625, ((0, 4), (1, 16))),
        "adapter_up_all": bell_draw(key_list[10], (N_SEGMENT, ADAPTER_JOBS * ADAPTER_RANK, QUERY_HEADS * HEAD_SIZE), (QUERY_HEADS * HEAD_SIZE) ** -0.5, 0.09375, ((0, 4), (2, 16))),
    }


ADAPTER_SCALE = 2.0
EPSILON = 1e-05

def rotate(inputs, head_count):
    sequence_count, row_count, width_all = inputs.shape
    head_dim = width_all // head_count
    half_dim = head_dim // 2
    shaped = inputs.reshape(sequence_count, row_count, head_count, head_dim)
    positions = jnp.arange(row_count, dtype=jnp.float32)
    exponent = jnp.arange(half_dim, dtype=jnp.float32) * (2.0 / head_dim)
    frequency = jnp.exp(-math.log(10000.0) * exponent)
    angles = positions[:, None] * frequency[None, :]
    cosine_table = jnp.cos(angles)[None, :, None, :]
    sine_table = jnp.sin(angles)[None, :, None, :]
    first_half = shaped[..., :half_dim]
    second_half = shaped[..., half_dim:]
    turned = jnp.concatenate([first_half * cosine_table - second_half * sine_table, second_half * cosine_table + first_half * sine_table], axis=-1)
    return turned.reshape(sequence_count, row_count, width_all)

def attend(query_rows, key_rows, value_rows, head_dim):
    sequence_count, row_count, query_span_width = query_rows.shape
    head_count = query_span_width // head_dim
    key_heads = key_rows.shape[-1] // head_dim
    group_size = head_count // key_heads
    rotated_queries = rotate(query_rows, head_count).reshape(sequence_count, row_count, key_heads, group_size, head_dim)
    rotated_keys = rotate(key_rows, key_heads).reshape(sequence_count, row_count, key_heads, head_dim)
    value_heads = value_rows.reshape(sequence_count, row_count, key_heads, head_dim)
    scores = jnp.einsum('bqhgd,bshd->bhgqs', rotated_queries, rotated_keys) / math.sqrt(head_dim)
    causal = jnp.arange(row_count)[:, None] >= jnp.arange(row_count)[None, :]
    scores = jnp.where(causal, scores, -1e+30)
    weights = jnp.exp(scores)
    probability = weights / lax.optimization_barrier(jnp.sum(weights, axis=-1, keepdims=True))
    output = jnp.einsum('bhgqs,bshd->bqhgd', probability, value_heads)
    return output.reshape(sequence_count, row_count, query_span_width)

def reference(tokens, cotangent, sequence_job, section_layer_list, section_norm_gain, query_matrix, key_matrix, value_matrix, output_matrix, adapter_down_all, adapter_up_all):
    sequence_count = tokens.shape[0]
    query_span_width = QUERY_HEADS * HEAD_SIZE
    key_width = KV_HEADS * HEAD_SIZE
    q_cols = query_span_width // N_TENSOR
    k_cols = key_width // N_TENSOR
    width_columns = MODEL_WIDTH // N_TENSOR
    onehot = (sequence_job[:, None] == jnp.arange(ADAPTER_JOBS, dtype=jnp.int32)[None, :]).astype(jnp.float32)
    hidden = tokens
    stored = []
    for relay_section in range(N_SEGMENT):
        stream = hidden.astype(jnp.float32)
        inverse = lax.rsqrt(lax.optimization_barrier(jnp.mean(stream * stream, axis=-1, keepdims=True)) + EPSILON)
        gain_row = section_norm_gain[relay_section].astype(jnp.float32)
        normed = (stream * inverse * gain_row).astype(jnp.bfloat16)
        flattened_rows = normed.reshape(sequence_count * SEQUENCE_TOKENS, MODEL_WIDTH)
        query_rows = jnp.dot(flattened_rows, query_matrix[relay_section], preferred_element_type=jnp.float32).reshape(sequence_count, SEQUENCE_TOKENS, query_span_width)
        key_rows = jnp.dot(flattened_rows, key_matrix[relay_section], preferred_element_type=jnp.float32).reshape(sequence_count, SEQUENCE_TOKENS, key_width)
        value_rows = jnp.dot(flattened_rows, value_matrix[relay_section], preferred_element_type=jnp.float32).reshape(sequence_count, SEQUENCE_TOKENS, key_width)
        every_job = jnp.dot(flattened_rows, adapter_down_all[relay_section], preferred_element_type=jnp.float32).reshape(sequence_count, SEQUENCE_TOKENS, ADAPTER_JOBS, ADAPTER_RANK)
        reduced_rank = lax.optimization_barrier(jnp.sum(every_job * onehot[:, None, :, None], axis=2))
        picked_up = adapter_up_all[relay_section].reshape(ADAPTER_JOBS, ADAPTER_RANK, query_span_width)[sequence_job].astype(jnp.float32)
        query_rows = query_rows + ADAPTER_SCALE * jnp.einsum('aqw,awy->aqy', reduced_rank, picked_up)
        attended = attend(query_rows, key_rows, value_rows, HEAD_SIZE).astype(jnp.bfloat16)
        flat_attended = attended.reshape(sequence_count * SEQUENCE_TOKENS, query_span_width)
        summed = jnp.zeros((sequence_count * SEQUENCE_TOKENS, MODEL_WIDTH), jnp.float32)
        for member in range(N_TENSOR):
            partial_addend = jnp.dot(flat_attended[:, member * q_cols:(member + 1) * q_cols], output_matrix[relay_section][member * q_cols:(member + 1) * q_cols], preferred_element_type=jnp.float32)
            summed = summed + lax.optimization_barrier(partial_addend.astype(jnp.bfloat16)).astype(jnp.float32)
        updated = (stream + summed.reshape(sequence_count, SEQUENCE_TOKENS, MODEL_WIDTH)).astype(jnp.bfloat16)
        applies = section_layer_list[relay_section] > 0
        stored.append((stream, inverse, normed, query_rows, key_rows, value_rows, reduced_rank, picked_up))
        hidden = jnp.where(applies, updated, hidden)
    gradient = cotangent.astype(jnp.float32)
    grads_down = [None] * N_SEGMENT
    grads_up = [None] * N_SEGMENT
    for relay_section in reversed(range(N_SEGMENT)):
        stream, inverse, normed, query_rows, key_rows, value_rows, reduced_rank, picked_up = stored[relay_section]
        applies = section_layer_list[relay_section] > 0
        flat_grad = gradient.astype(jnp.bfloat16).reshape(sequence_count * SEQUENCE_TOKENS, MODEL_WIDTH)
        grad_attended = jnp.dot(flat_grad, output_matrix[relay_section].T, preferred_element_type=jnp.float32).reshape(sequence_count, SEQUENCE_TOKENS, query_span_width)
        unused, pullback = jax.vjp(lambda first_in, second_in, third_in: attend(first_in, second_in, third_in, HEAD_SIZE), query_rows, key_rows, value_rows)
        query_gradient, key_gradient, value_gradient = pullback(grad_attended)
        shared_up_adapter = ADAPTER_SCALE * jnp.einsum('mxh,mxi->mhi', reduced_rank, query_gradient)
        grad_up = jnp.einsum('bj,bkc->jkc', onehot, shared_up_adapter).reshape(ADAPTER_JOBS * ADAPTER_RANK, query_span_width)
        reduced_gradient = ADAPTER_SCALE * jnp.einsum('ehy,ety->eht', query_gradient, picked_up)
        share_down = jnp.einsum('brd,brk->bdk', normed.astype(jnp.float32), reduced_gradient)
        grad_down = jnp.einsum('bj,bdk->djk', onehot, share_down).reshape(MODEL_WIDTH, ADAPTER_JOBS * ADAPTER_RANK)
        picked_down = adapter_down_all[relay_section].reshape(MODEL_WIDTH, ADAPTER_JOBS, ADAPTER_RANK)[:, sequence_job, :].astype(jnp.float32)
        query_bf = query_gradient.astype(jnp.bfloat16).reshape(sequence_count * SEQUENCE_TOKENS, query_span_width)
        keys_bf = key_gradient.astype(jnp.bfloat16).reshape(sequence_count * SEQUENCE_TOKENS, key_width)
        values_bf = value_gradient.astype(jnp.bfloat16).reshape(sequence_count * SEQUENCE_TOKENS, key_width)
        grad_norm = jnp.zeros((sequence_count * SEQUENCE_TOKENS, MODEL_WIDTH), jnp.float32)
        for member in range(N_TENSOR):
            q_low, q_high = (member * q_cols, (member + 1) * q_cols)
            k_low, k_high = (member * k_cols, (member + 1) * k_cols)
            width_lower, width_upper = (member * width_columns, (member + 1) * width_columns)
            partial_addend = jnp.dot(query_bf[:, q_low:q_high], query_matrix[relay_section][:, q_low:q_high].T, preferred_element_type=jnp.float32)
            partial_addend = partial_addend + jnp.dot(keys_bf[:, k_low:k_high], key_matrix[relay_section][:, k_low:k_high].T, preferred_element_type=jnp.float32)
            partial_addend = partial_addend + jnp.dot(values_bf[:, k_low:k_high], value_matrix[relay_section][:, k_low:k_high].T, preferred_element_type=jnp.float32)
            adapter_addend = jnp.einsum('hem,uhm->heu', reduced_gradient, picked_down[width_lower:width_upper]).reshape(sequence_count * SEQUENCE_TOKENS, width_columns)
            partial_addend = partial_addend.at[:, width_lower:width_upper].add(adapter_addend)
            grad_norm = grad_norm + lax.optimization_barrier(partial_addend.astype(jnp.bfloat16)).astype(jnp.float32)
        grad_norm = grad_norm.reshape(sequence_count, SEQUENCE_TOKENS, MODEL_WIDTH)
        gained = grad_norm * section_norm_gain[relay_section].astype(jnp.float32)
        grad_hidden = inverse * gained - stream * inverse ** 3 * lax.optimization_barrier(jnp.mean(gained * stream, axis=-1, keepdims=True))
        gradient = jnp.where(applies, gradient + grad_hidden, gradient)
        grads_down[relay_section] = jnp.where(applies, grad_down, jnp.zeros_like(grad_down))
        grads_up[relay_section] = jnp.where(applies, grad_up, jnp.zeros_like(grad_up))
        gradient = lax.optimization_barrier(gradient.astype(jnp.bfloat16)).astype(jnp.float32)
    return (jnp.stack(grads_down), jnp.stack(grads_up))
```

```python
import functools
import math

import jax
import jax.numpy as jnp
from jax import lax
from jax.experimental import pallas as pl
from jax.experimental.pallas import tpu as pltpu
from jax.sharding import Mesh
from jax.sharding import PartitionSpec as P

HEAD_SIZE = 128
ADAPTER_RANK = 16
ADAPTER_JOBS = 32
ADAPTER_SCALE = 2.0
EPSILON = 1e-05
SIDE = 4
ROWS = 16
TOKENS = SIDE * SIDE * ROWS
KV_PART = 32
LOW_LANE = 2 * KV_PART
GATHER_CHUNKS = 4
SCATTER_CHUNKS = 8
SEG, Z, X = "segment", "tensor_0", "tensor_1"
TENSOR = (Z, X)
MESH = pl.DeviceIdType.MESH
BF16, F32 = jnp.bfloat16, jnp.float32
VMEM_LIMIT = 60 * 1024 * 1024


def dot(a, b, dims=((1,), (0,))):
    return lax.dot_general(a, b, (dims, ((), ())), preferred_element_type=F32)


def step_of(axis, offset):
    return lax.rem(lax.axis_index(axis) + (offset + SIDE), SIDE)


def remote(src, dst, send_sem, recv_sem, axis, offset):
    return pltpu.make_async_remote_copy(
        src_ref=src,
        dst_ref=dst,
        send_sem=send_sem,
        recv_sem=recv_sem,
        device_id={axis: step_of(axis, offset)},
        device_id_type=MESH,
    )


def greet(partners):
    barrier = pltpu.get_barrier_semaphore()
    for axis, offset in partners:
        pl.semaphore_signal(
            barrier, inc=1, device_id={axis: step_of(axis, offset)}, device_id_type=MESH
        )
    pl.semaphore_wait(barrier, len(partners))


NEAR = [(Z, 1), (Z, -1), (X, 1), (X, -1)]


def order_of(chunk):
    return (Z, X) if chunk % 2 == 0 else (X, Z)


def blocks(ref, axis, place, columns):
    if axis == Z:
        return ref.at[place, :, :, columns]
    return ref.at[:, place, :, columns]


def gather_all(held, send, recv, consume):
    width = held.shape[-1]
    size = width // GATHER_CHUNKS
    me = {Z: lax.axis_index(Z), X: lax.axis_index(X)}
    started = []

    def columns(chunk, half=None):
        if half is None:
            return pl.ds(chunk * size, size)
        return pl.ds(chunk * size + half * (size // 2), size // 2)

    def go(chunk, slot, src, axis, offset):
        copy = remote(src, src, send.at[chunk, slot], recv.at[chunk, slot], axis, offset)
        copy.start()
        started.append(copy)

    def arrived(chunk, slot, where, axis, offset):
        remote(where, where, send.at[chunk, slot], recv.at[chunk, slot], axis, offset).wait_recv()

    def one(first, offset, cols):
        place = step_of(first, offset)
        z, x = (place, me[X]) if first == Z else (me[Z], place)
        return held.at[z, x, :, cols]

    def stage0(chunk):
        first, _ = order_of(chunk)
        own = one(first, 0, columns(chunk))
        go(chunk, 0, own, first, 1)
        go(chunk, 1, own, first, -1)

    def stage1(chunk):
        first, _ = order_of(chunk)
        arrived(chunk, 0, one(first, -1, columns(chunk)), first, 1)
        go(chunk, 2, one(first, -1, columns(chunk, 0)), first, 1)
        arrived(chunk, 1, one(first, 1, columns(chunk)), first, -1)
        go(chunk, 3, one(first, 1, columns(chunk, 1)), first, -1)

    def stage2(chunk):
        first, second = order_of(chunk)
        arrived(chunk, 2, one(first, 2, columns(chunk, 0)), first, 1)
        arrived(chunk, 3, one(first, 2, columns(chunk, 1)), first, -1)
        group = blocks(held, second, me[second], columns(chunk))
        go(chunk, 4, group, second, 1)
        go(chunk, 5, group, second, -1)

    def stage3(chunk):
        _, second = order_of(chunk)
        low, high = step_of(second, -1), step_of(second, 1)
        arrived(chunk, 4, blocks(held, second, low, columns(chunk)), second, 1)
        go(chunk, 6, blocks(held, second, low, columns(chunk, 0)), second, 1)
        arrived(chunk, 5, blocks(held, second, high, columns(chunk)), second, -1)
        go(chunk, 7, blocks(held, second, high, columns(chunk, 1)), second, -1)

    def stage4(chunk):
        _, second = order_of(chunk)
        far = step_of(second, 2)
        arrived(chunk, 6, blocks(held, second, far, columns(chunk, 0)), second, 1)
        arrived(chunk, 7, blocks(held, second, far, columns(chunk, 1)), second, -1)
        consume(chunk, chunk * size, size)

    stages = [stage1, stage2, stage3, stage4]
    for chunk in range(GATHER_CHUNKS):
        stage0(chunk)
    for turn in range(GATHER_CHUNKS + len(stages) - 1):
        for place, stage in enumerate(stages):
            chunk = turn - place
            if 0 <= chunk < GATHER_CHUNKS:
                stage(chunk)
    for copy in started:
        copy.wait_send()


def scatter_sum(part, mid, land1, land2, land3, land4, send, recv, term, finish):
    width = part.shape[-1]
    size = width // SCATTER_CHUNKS
    half = size // 2
    me = {Z: lax.axis_index(Z), X: lax.axis_index(X)}
    started = []

    def columns(chunk, part_of=None):
        if part_of is None:
            return pl.ds(chunk * size, size)
        return pl.ds(chunk * size + part_of * half, half)

    def go(chunk, slot, src, dst, axis, offset):
        copy = remote(src, dst, send.at[chunk, slot], recv.at[chunk, slot], axis, offset)
        copy.start()
        started.append(copy)

    def arrived(chunk, slot, where, axis, offset):
        remote(where, where, send.at[chunk, slot], recv.at[chunk, slot], axis, offset).wait_recv()

    def add_into(target, landed):
        target[...] = (target[...].astype(F32) + landed[...].astype(F32)).astype(BF16)

    def stage0(chunk):
        first, _ = order_of(chunk)
        part[:, :, :, columns(chunk)] = (
            term(chunk * size, size).astype(BF16).reshape(SIDE, SIDE, ROWS, size)
        )
        far = step_of(first, 2)
        go(chunk, 0, blocks(part, first, far, columns(chunk, 0)), land1.at[chunk, 0], first, 1)
        go(chunk, 1, blocks(part, first, far, columns(chunk, 1)), land1.at[chunk, 1], first, -1)

    def stage1(chunk):
        first, _ = order_of(chunk)
        for slot, offset in ((0, 1), (1, -1)):
            arrived(chunk, slot, land1.at[chunk, slot], first, offset)
            near = step_of(first, offset)
            add_into(blocks(part, first, near, columns(chunk, slot)), land1.at[chunk, slot])
            go(
                chunk,
                2 + slot,
                blocks(part, first, near, columns(chunk)),
                land2.at[chunk, slot],
                first,
                offset,
            )

    def stage2(chunk):
        first, second = order_of(chunk)
        arrived(chunk, 2, land2.at[chunk, 0], first, 1)
        arrived(chunk, 3, land2.at[chunk, 1], first, -1)
        own = blocks(part, first, me[first], columns(chunk))
        mid[chunk] = (
            own[...].astype(F32) + land2[chunk, 0].astype(F32) + land2[chunk, 1].astype(F32)
        ).astype(BF16)
        far = step_of(second, 2)
        go(chunk, 4, mid.at[chunk, far, :, pl.ds(0, half)], land3.at[chunk, 0], second, 1)
        go(chunk, 5, mid.at[chunk, far, :, pl.ds(half, half)], land3.at[chunk, 1], second, -1)

    def stage3(chunk):
        _, second = order_of(chunk)
        for slot, offset in ((0, 1), (1, -1)):
            arrived(chunk, 4 + slot, land3.at[chunk, slot], second, offset)
            near = step_of(second, offset)
            add_into(mid.at[chunk, near, :, pl.ds(slot * half, half)], land3.at[chunk, slot])
            go(chunk, 6 + slot, mid.at[chunk, near], land4.at[chunk, slot], second, offset)

    def stage4(chunk):
        _, second = order_of(chunk)
        arrived(chunk, 6, land4.at[chunk, 0], second, 1)
        arrived(chunk, 7, land4.at[chunk, 1], second, -1)
        total = (
            mid[chunk, me[second]].astype(F32)
            + land4[chunk, 0].astype(F32)
            + land4[chunk, 1].astype(F32)
        )
        finish(chunk, chunk * size, size, total)

    stages = [stage0, stage1, stage2, stage3, stage4]
    for turn in range(SCATTER_CHUNKS + len(stages) - 1):
        for place, stage in enumerate(stages):
            chunk = turn - place
            if 0 <= chunk < SCATTER_CHUNKS:
                stage(chunk)
    for copy in started:
        copy.wait_send()


def scatter_scratch(width):
    size = width // SCATTER_CHUNKS
    return [
        pltpu.VMEM((SIDE, SIDE, ROWS, width), BF16),
        pltpu.VMEM((SCATTER_CHUNKS, SIDE, ROWS, size), BF16),
        pltpu.VMEM((SCATTER_CHUNKS, 2, SIDE, ROWS, size // 2), BF16),
        pltpu.VMEM((SCATTER_CHUNKS, 2, SIDE, ROWS, size), BF16),
        pltpu.VMEM((SCATTER_CHUNKS, 2, ROWS, size // 2), BF16),
        pltpu.VMEM((SCATTER_CHUNKS, 2, ROWS, size), BF16),
        pltpu.SemaphoreType.DMA((SCATTER_CHUNKS, 8)),
        pltpu.SemaphoreType.DMA((SCATTER_CHUNKS, 8)),
    ]


def gather_scratch(width):
    return [
        pltpu.VMEM((SIDE, SIDE, ROWS, width), BF16),
        pltpu.SemaphoreType.DMA((GATHER_CHUNKS, 8)),
        pltpu.SemaphoreType.DMA((GATHER_CHUNKS, 8)),
    ]


def spread(all_planes, columns, send, recv, started):
    planes = lax.axis_size(SEG)
    mine = lax.axis_index(SEG)
    for distance in range(1, planes):
        copy = pltpu.make_async_remote_copy(
            src_ref=all_planes.at[mine, :, columns],
            dst_ref=all_planes.at[mine, :, columns],
            send_sem=send.at[distance],
            recv_sem=recv.at[distance],
            device_id={SEG: lax.rem(mine + distance, planes)},
            device_id_type=MESH,
        )
        copy.start()
        started.append(copy)


def spread_wait(all_planes, columns, send, recv):
    planes = lax.axis_size(SEG)
    mine = lax.axis_index(SEG)
    for distance in range(1, planes):
        there = all_planes.at[lax.rem(mine + planes - distance, planes), :, columns]
        pltpu.make_async_remote_copy(
            src_ref=there,
            dst_ref=there,
            send_sem=send.at[distance],
            recv_sem=recv.at[distance],
            device_id={SEG: lax.rem(mine + distance, planes)},
            device_id_type=MESH,
        ).wait_recv()


def plane_partners():
    return lax.axis_size(SEG)


def greet_all(axes_of_x, with_planes):
    barrier = pltpu.get_barrier_semaphore()
    partners = list(NEAR)
    if axes_of_x:
        partners.append((X, 2))
    count = len(partners)
    for axis, offset in partners:
        pl.semaphore_signal(
            barrier, inc=1, device_id={axis: step_of(axis, offset)}, device_id_type=MESH
        )
    if with_planes:
        planes = lax.axis_size(SEG)
        mine = lax.axis_index(SEG)
        for distance in range(1, planes):
            pl.semaphore_signal(
                barrier,
                inc=1,
                device_id={SEG: lax.rem(mine + distance, planes)},
                device_id_type=MESH,
            )
        count += planes - 1
    pl.semaphore_wait(barrier, count)


def turned(value, cosine, sine):
    return value * cosine + pltpu.roll(value, HEAD_SIZE // 2, 1) * sine


def turned_back(value, cosine, sine):
    return value * cosine + pltpu.roll(value * sine, HEAD_SIZE // 2, 1)


def probabilities(query, key):
    scores = dot(query, key, ((1,), (1,))) * (1.0 / math.sqrt(HEAD_SIZE))
    row = lax.broadcasted_iota(jnp.int32, scores.shape, 0)
    column = lax.broadcasted_iota(jnp.int32, scores.shape, 1)
    weights = jnp.exp(jnp.where(row >= column, scores, -1e30))
    return weights / jnp.sum(weights, axis=-1, keepdims=True)


def project_kernel(
    hidden, gain, query_hbm, side_hbm, up, pick, cosine, sine,
    query_out, key_out, value_out, side_out, piece_out,
    held, send, recv, query_w, side_w, w_sem, query_sum, side_sum, trade, trade_send, trade_recv,
):
    width = held.shape[-1]
    size = width // GATHER_CHUNKS
    loads = []
    for chunk in range(GATHER_CHUNKS):
        rows = pl.ds(chunk * size, size)
        pair = (
            pltpu.make_async_copy(query_hbm.at[rows], query_w.at[rows], w_sem.at[chunk, 0]),
            pltpu.make_async_copy(side_hbm.at[rows], side_w.at[rows], w_sem.at[chunk, 1]),
        )
        for copy in pair:
            copy.start()
        loads.append(pair)
    stream = hidden[...].astype(F32)
    inverse = lax.rsqrt(jnp.mean(stream * stream, axis=-1, keepdims=True) + EPSILON)
    held[lax.axis_index(Z), lax.axis_index(X)] = (stream * inverse * gain[...]).astype(BF16)
    query_sum[...] = jnp.zeros_like(query_sum)
    side_sum[...] = jnp.zeros_like(side_sum)
    greet_all(True, False)

    def consume(chunk, first, extent):
        for copy in loads[chunk]:
            copy.wait()
        tile = min(512, extent)

        def body(i, carry):
            at = pl.multiple_of(first + i * tile, tile)
            rows = held[:, :, :, pl.ds(at, tile)].reshape(TOKENS, tile)
            query_sum[...] += dot(rows, query_w[pl.ds(at, tile), :])
            side_sum[...] += dot(rows, side_w[pl.ds(at, tile), :])
            return carry

        lax.fori_loop(0, extent // tile, body, 0)

    gather_all(held, send, recv, consume)
    mine = lax.axis_index(X)
    side = side_sum[...].astype(BF16)
    side_out[...] = side
    trade[mine] = side
    copies = []
    for distance in range(1, SIDE):
        copy = remote(
            trade.at[mine], trade.at[mine], trade_send.at[distance], trade_recv.at[distance], X, distance
        )
        copy.start()
        copies.append(copy)
    query = query_sum[...] + ADAPTER_SCALE * dot(side, up[...])
    for head in range(query.shape[1] // HEAD_SIZE):
        lanes = slice(head * HEAD_SIZE, (head + 1) * HEAD_SIZE)
        query_out[:, lanes] = turned(query[:, lanes], cosine[...], sine[...]).astype(BF16)
    piece = width // (SIDE * SIDE)
    first = (lax.axis_index(Z) * SIDE + mine) * piece
    piece_out[...] = held[:, :, :, pl.ds(pl.multiple_of(first, piece), piece)].reshape(TOKENS, piece)
    for distance in range(1, SIDE):
        there = trade.at[step_of(X, -distance)]
        remote(there, there, trade_send.at[distance], trade_recv.at[distance], X, distance).wait_recv()
    for copy in copies:
        copy.wait_send()
    both = dot(trade[0], pick[0])
    for place in range(1, SIDE):
        both += dot(trade[place], pick[place])
    key_out[...] = turned(both[:, :HEAD_SIZE], cosine[...], sine[...]).astype(BF16)
    value_out[...] = both[:, HEAD_SIZE:].astype(BF16)


def extend_kernel(
    owner, hidden, query, key, value, out_hbm,
    hidden_out,
    part, mid, land1, land2, land3, land4, send, recv, out_w, w_sem, attended, planes, p_send, p_recv,
):
    width = part.shape[-1]
    size = width // SCATTER_CHUNKS
    loads = []
    for chunk in range(SCATTER_CHUNKS):
        cols = pl.ds(chunk * size, size)
        copy = pltpu.make_async_copy(out_hbm.at[:, cols], out_w.at[:, cols], w_sem.at[chunk])
        copy.start()
        loads.append(copy)
    for head in range(query.shape[1] // HEAD_SIZE):
        lanes = slice(head * HEAD_SIZE, (head + 1) * HEAD_SIZE)
        weights = probabilities(query[:, lanes], key[...]).astype(BF16)
        attended[:, lanes] = dot(weights, value[...]).astype(BF16)
    greet_all(False, True)
    mine = lax.axis_index(SEG)
    started = []

    def term(first, extent):
        loads[first // size].wait()
        return dot(attended[...], out_w[:, pl.ds(first, extent)])

    def finish(chunk, first, extent, total):
        cols = pl.ds(first, extent)
        planes[mine, :, cols] = (hidden[:, cols].astype(F32) + total).astype(BF16)
        spread(planes, cols, p_send.at[chunk], p_recv.at[chunk], started)

    scatter_sum(part, mid, land1, land2, land3, land4, send, recv, term, finish)
    for chunk in range(SCATTER_CHUNKS):
        spread_wait(planes, pl.ds(chunk * size, size), p_send.at[chunk], p_recv.at[chunk])
    for copy in started:
        copy.wait_send()
    hidden_out[...] = planes[owner[0]]


def reverse_kernel(
    gradient, query, key, value, side, out_hbm, up, cosine, sine,
    query_grad_out, pair_grad_out, low_out, up_out,
    held, send, recv, out_w, w_sem, back,
):
    width = held.shape[-1]
    size = width // GATHER_CHUNKS
    loads = []
    for chunk in range(GATHER_CHUNKS):
        cols = pl.ds(chunk * size, size)
        copy = pltpu.make_async_copy(out_hbm.at[:, cols], out_w.at[:, cols], w_sem.at[chunk])
        copy.start()
        loads.append(copy)
    held[lax.axis_index(Z), lax.axis_index(X)] = gradient[...]
    back[...] = jnp.zeros_like(back)
    greet_all(False, False)

    def consume(chunk, first, extent):
        loads[chunk].wait()
        tile = min(512, extent)

        def body(i, carry):
            at = pl.multiple_of(first + i * tile, tile)
            rows = held[:, :, :, pl.ds(at, tile)].reshape(TOKENS, tile)
            back[...] += dot(rows, out_w[:, pl.ds(at, tile)], ((1,), (1,)))
            return carry

        lax.fori_loop(0, extent // tile, body, 0)

    gather_all(held, send, recv, consume)
    scale = 1.0 / math.sqrt(HEAD_SIZE)
    key_grad = jnp.zeros((TOKENS, HEAD_SIZE), F32)
    value_grad = jnp.zeros((TOKENS, HEAD_SIZE), F32)
    for head in range(query.shape[1] // HEAD_SIZE):
        lanes = slice(head * HEAD_SIZE, (head + 1) * HEAD_SIZE)
        weights = probabilities(query[:, lanes], key[...])
        out_grad = back[:, lanes].astype(BF16)
        value_grad += dot(weights.astype(BF16), out_grad, ((0,), (0,)))
        weight_grad = dot(out_grad, value[...], ((1,), (1,)))
        mean = jnp.sum(weight_grad * weights, axis=-1, keepdims=True)
        score_grad = (weights * (weight_grad - mean) * scale).astype(BF16)
        query_grad = turned_back(dot(score_grad, key[...]), cosine[...], sine[...])
        query_grad_out[:, lanes] = query_grad.astype(BF16)
        key_grad += dot(score_grad, query[:, lanes], ((0,), (0,)))
    pair_grad_out[:, :HEAD_SIZE] = turned_back(key_grad, cosine[...], sine[...]).astype(BF16)
    pair_grad_out[:, HEAD_SIZE:] = value_grad.astype(BF16)
    query_grad = query_grad_out[...]
    low_out[...] = ADAPTER_SCALE * dot(query_grad, up[...], ((1,), (1,)))
    up_out[...] = ADAPTER_SCALE * dot(side[...], query_grad, ((0,), (0,)))


def return_kernel(
    owner, gradient, hidden, gain, query_grad, pair_grad, low, query_hbm, side_hbm, pick,
    gradient_out,
    part, mid, land1, land2, land3, land4, send, recv,
    query_w, side_w, w_sem, side_grad, trade, trade_send, trade_recv,
    normed_grad, planes, p_send, p_recv, means, m_send, m_recv,
):
    width = part.shape[-1]
    size = width // SCATTER_CHUNKS
    loads = []
    for chunk in range(SCATTER_CHUNKS):
        rows = pl.ds(chunk * size, size)
        pair = (
            pltpu.make_async_copy(query_hbm.at[rows], query_w.at[rows], w_sem.at[chunk, 0]),
            pltpu.make_async_copy(side_hbm.at[rows], side_w.at[rows], w_sem.at[chunk, 1]),
        )
        for copy in pair:
            copy.start()
        loads.append(pair)
    x_index = lax.axis_index(X)
    for place in range(SIDE):
        trade[0, place] = dot(pair_grad[...], pick[place], ((1,), (1,))).astype(BF16)
    stream = hidden[...].astype(F32)
    inverse = lax.rsqrt(jnp.mean(stream * stream, axis=-1, keepdims=True) + EPSILON)
    greet_all(True, True)
    copies = []
    for distance in range(1, SIDE):
        copy = remote(
            trade.at[0, step_of(X, distance)],
            trade.at[1, distance],
            trade_send.at[distance],
            trade_recv.at[distance],
            X,
            distance,
        )
        copy.start()
        copies.append(copy)
    total = trade[0, x_index].astype(F32) + low[...]
    for distance in range(1, SIDE):
        there = trade.at[1, distance]
        remote(there, there, trade_send.at[distance], trade_recv.at[distance], X, distance).wait_recv()
        total += trade[1, distance].astype(F32)
    side_grad[...] = total.astype(BF16)
    mine = lax.axis_index(SEG)
    started = []
    sums = []

    def term(first, extent):
        for copy in loads[first // size]:
            copy.wait()
        rows = pl.ds(first, extent)
        return dot(query_grad[...], query_w[rows, :], ((1,), (1,))) + dot(
            side_grad[...], side_w[rows, :], ((1,), (1,))
        )

    def finish(chunk, first, extent, total):
        cols = pl.ds(first, extent)
        gained = total * gain[:, cols]
        sums.append(jnp.sum(gained * hidden[:, cols].astype(F32), axis=-1, keepdims=True))
        planes[mine, :, cols] = (inverse * gained).astype(BF16)
        spread(planes, cols, p_send.at[chunk], p_recv.at[chunk], started)

    scatter_sum(part, mid, land1, land2, land3, land4, send, recv, term, finish)
    mean = sum(sums) / width
    means[mine] = jnp.broadcast_to(mean, (ROWS, HEAD_SIZE))
    spread(means, slice(None), m_send, m_recv, started)
    for chunk in range(SCATTER_CHUNKS):
        spread_wait(planes, pl.ds(chunk * size, size), p_send.at[chunk], p_recv.at[chunk])
    spread_wait(means, slice(None), m_send, m_recv)
    for copy in copies + started:
        copy.wait_send()
    mean = means[owner[0]][:, :1]
    gradient_out[...] = (
        gradient[...].astype(F32)
        + planes[owner[0]].astype(F32)
        - stream * (inverse * inverse * inverse * mean)
    ).astype(BF16)


def in_vmem(count):
    return [pl.BlockSpec(memory_space=pltpu.VMEM)] * count


ANYWHERE = pl.BlockSpec(memory_space=pl.ANY)
SCALAR = pl.BlockSpec(memory_space=pltpu.SMEM)


def params(number):
    return pltpu.CompilerParams(
        collective_id=number, has_side_effects=True, vmem_limit_bytes=VMEM_LIMIT
    )


def shaped(shape, dtype=BF16):
    return jax.ShapeDtypeStruct(shape, dtype)


def project(hidden, gain, query_w, side_w, up, pick, cosine, sine):
    width, columns = query_w.shape
    return pl.pallas_call(
        project_kernel,
        out_shape=(
            shaped((TOKENS, columns)),
            shaped((TOKENS, HEAD_SIZE)),
            shaped((TOKENS, HEAD_SIZE)),
            shaped((TOKENS, HEAD_SIZE)),
            shaped((TOKENS, width // (SIDE * SIDE))),
        ),
        in_specs=in_vmem(2) + [ANYWHERE] * 2 + in_vmem(4),
        out_specs=tuple(in_vmem(5)),
        scratch_shapes=[
            *gather_scratch(width),
            pltpu.VMEM((width, columns), BF16),
            pltpu.VMEM((width, HEAD_SIZE), BF16),
            pltpu.SemaphoreType.DMA((GATHER_CHUNKS, 2)),
            pltpu.VMEM((TOKENS, columns), F32),
            pltpu.VMEM((TOKENS, HEAD_SIZE), F32),
            pltpu.VMEM((SIDE, TOKENS, HEAD_SIZE), BF16),
            pltpu.SemaphoreType.DMA((SIDE,)),
            pltpu.SemaphoreType.DMA((SIDE,)),
        ],
        compiler_params=params(1),
        name="project",
    )(hidden, gain, query_w, side_w, up, pick, cosine, sine)


def extend(owner, hidden, query, key, value, out_w, planes):
    columns, width = out_w.shape
    return pl.pallas_call(
        extend_kernel,
        out_shape=shaped((ROWS, width)),
        in_specs=[SCALAR, *in_vmem(4), ANYWHERE],
        out_specs=in_vmem(1)[0],
        scratch_shapes=[
            *scatter_scratch(width),
            pltpu.VMEM((columns, width), BF16),
            pltpu.SemaphoreType.DMA((SCATTER_CHUNKS,)),
            pltpu.VMEM((TOKENS, columns), BF16),
            pltpu.VMEM((planes, ROWS, width), BF16),
            pltpu.SemaphoreType.DMA((SCATTER_CHUNKS, planes)),
            pltpu.SemaphoreType.DMA((SCATTER_CHUNKS, planes)),
        ],
        compiler_params=params(2),
        name="extend",
    )(owner, hidden, query, key, value, out_w)


def reverse(gradient, query, key, value, side, out_w, up, cosine, sine):
    columns, width = out_w.shape
    return pl.pallas_call(
        reverse_kernel,
        out_shape=(
            shaped((TOKENS, columns)),
            shaped((TOKENS, 2 * HEAD_SIZE)),
            shaped((TOKENS, HEAD_SIZE), F32),
            shaped((HEAD_SIZE, columns), F32),
        ),
        in_specs=[*in_vmem(5), ANYWHERE, *in_vmem(3)],
        out_specs=tuple(in_vmem(4)),
        scratch_shapes=[
            *gather_scratch(width),
            pltpu.VMEM((columns, width), BF16),
            pltpu.SemaphoreType.DMA((GATHER_CHUNKS,)),
            pltpu.VMEM((TOKENS, columns), F32),
        ],
        compiler_params=params(3),
        name="reverse",
    )(gradient, query, key, value, side, out_w, up, cosine, sine)


def send_back(owner, gradient, hidden, gain, query_grad, pair_grad, low, query_w, side_w, pick, planes):
    width, columns = query_w.shape
    return pl.pallas_call(
        return_kernel,
        out_shape=shaped((ROWS, width)),
        in_specs=[SCALAR, *in_vmem(6), ANYWHERE, ANYWHERE, *in_vmem(1)],
        out_specs=in_vmem(1)[0],
        scratch_shapes=[
            *scatter_scratch(width),
            pltpu.VMEM((width, columns), BF16),
            pltpu.VMEM((width, HEAD_SIZE), BF16),
            pltpu.SemaphoreType.DMA((SCATTER_CHUNKS, 2)),
            pltpu.VMEM((TOKENS, HEAD_SIZE), BF16),
            pltpu.VMEM((2, SIDE, TOKENS, HEAD_SIZE), BF16),
            pltpu.SemaphoreType.DMA((SIDE,)),
            pltpu.SemaphoreType.DMA((SIDE,)),
            pltpu.VMEM((ROWS, HEAD_SIZE), F32),
            pltpu.VMEM((planes, ROWS, width), BF16),
            pltpu.SemaphoreType.DMA((SCATTER_CHUNKS, planes)),
            pltpu.SemaphoreType.DMA((SCATTER_CHUNKS, planes)),
            pltpu.VMEM((planes, ROWS, HEAD_SIZE), F32),
            pltpu.SemaphoreType.DMA((planes,)),
            pltpu.SemaphoreType.DMA((planes,)),
        ],
        compiler_params=params(4),
        name="send_back",
    )(owner, gradient, hidden, gain, query_grad, pair_grad, low, query_w, side_w, pick)


def turn_tables():
    positions = jnp.arange(TOKENS, dtype=F32)
    exponent = jnp.arange(HEAD_SIZE // 2, dtype=F32) * (2.0 / HEAD_SIZE)
    angles = positions[:, None] * jnp.exp(-math.log(10000.0) * exponent)[None, :]
    cosine, sine = jnp.cos(angles), jnp.sin(angles)
    return (
        jnp.concatenate([cosine, cosine], axis=1),
        jnp.concatenate([-sine, sine], axis=1),
    )


def pick_table():
    place = jnp.arange(SIDE)[:, None, None]
    row = jnp.arange(HEAD_SIZE)[None, :, None]
    column = jnp.arange(2 * HEAD_SIZE)[None, None, :]
    keys = (row < KV_PART) & (column == place * KV_PART + row)
    values = (
        (row >= KV_PART)
        & (row < 2 * KV_PART)
        & (column == HEAD_SIZE + place * KV_PART + row - KV_PART)
    )
    return (keys | values).astype(BF16)


def shards(
    tokens,
    cotangent,
    sequence_job,
    section_layer_list,
    section_norm_gain,
    query_matrix,
    key_matrix,
    value_matrix,
    output_matrix,
    adapter_down_all,
    adapter_up_all,
):
    segments = lax.axis_size(SEG)
    replicas = lax.axis_size("dp")
    segment_index = lax.axis_index(SEG)
    gain = section_norm_gain.astype(F32)
    query_w = query_matrix[0]
    out_w = output_matrix[0]
    width, columns = query_w.shape
    piece_width = adapter_down_all.shape[1]
    job = sequence_job[0]
    jobs_width = ADAPTER_JOBS * ADAPTER_RANK
    first = job * ADAPTER_RANK
    down_here = lax.dynamic_slice(adapter_down_all[0], (0, first), (piece_width, ADAPTER_RANK))
    down = lax.all_gather(down_here, TENSOR, axis=0, tiled=True)
    side_w = jnp.concatenate(
        [
            key_matrix[0],
            value_matrix[0],
            down,
            jnp.zeros((width, HEAD_SIZE - LOW_LANE - ADAPTER_RANK), BF16),
        ],
        axis=1,
    )
    up_here = lax.dynamic_slice(adapter_up_all[0], (first, 0), (ADAPTER_RANK, columns))
    up = jnp.pad(up_here, ((LOW_LANE, HEAD_SIZE - LOW_LANE - ADAPTER_RANK), (0, 0)))
    cosine, sine = turn_tables()
    pick = pick_table()

    active = section_layer_list > 0
    rank = jnp.cumsum(active.astype(jnp.int32)) - 1
    places = jnp.arange(segments, dtype=jnp.int32)
    layers = jnp.sum(active.astype(jnp.int32))
    turns = max(segments - 1, 1)
    owners = [
        jnp.sum(jnp.where(active & (rank == turn), places, 0)).astype(jnp.int32)
        for turn in range(turns)
    ]
    ending = cotangent[0]

    def run(turn, hidden):
        owner = owners[turn]
        owner_here = owner == segment_index
        owner = owner[None]
        query, key, value, side, piece = project(
            hidden, gain, query_w, side_w, up, pick, cosine, sine
        )
        nothing = (
            jnp.zeros((TOKENS, piece_width), BF16),
            jnp.zeros((TOKENS, HEAD_SIZE), F32),
            jnp.zeros((HEAD_SIZE, columns), F32),
        )

        def onward(start):
            following = extend(owner, start, query, key, value, out_w, segments)
            return run(turn + 1, following)

        if turn + 1 < turns:
            gradient, totals = lax.cond(
                layers > turn + 1, onward, lambda start: (ending, nothing), hidden
            )
        else:
            gradient, totals = ending, nothing
        query_grad, pair_grad, low, grad_up = reverse(
            gradient, query, key, value, side, out_w, up, cosine, sine
        )
        totals = jax.tree.map(
            lambda new, old: jnp.where(owner_here, new, old), (piece, low, grad_up), totals
        )
        if turn > 0:
            gradient = send_back(
                owner, gradient, hidden, gain, query_grad, pair_grad, low,
                query_w, side_w, pick, segments,
            )
        return gradient, totals

    _, (piece, low, grad_up) = run(0, tokens[0])
    low = lax.psum(low[:, LOW_LANE : LOW_LANE + ADAPTER_RANK], TENSOR)
    grad_up = grad_up[LOW_LANE : LOW_LANE + ADAPTER_RANK]
    grad_down = lax.dot_general(
        low.astype(BF16), piece, (((0,), (0,)), ((), ())), preferred_element_type=F32
    )
    mine = jnp.concatenate([grad_up, grad_down], axis=1)
    place = (jnp.arange(jobs_width)[None, :] == first + jnp.arange(ADAPTER_RANK)[:, None]).astype(F32)
    shares = lax.all_gather(
        jnp.concatenate([mine, place], axis=1).astype(BF16), "dp", axis=0, tiled=True
    ).astype(F32)
    places_all = shares[:, columns + piece_width :]
    grad_up = lax.dot_general(
        places_all, shares[:, :columns], (((0,), (0,)), ((), ())), precision="highest"
    )
    grad_down = lax.dot_general(
        shares[:, columns : columns + piece_width], places_all, (((0,), (0,)), ((), ())), precision="highest"
    )
    return (grad_down[None], grad_up[None])


def solution(mesh):
    split = Mesh(
        mesh.devices.reshape(mesh.shape["segment"], SIDE, SIDE, mesh.shape["dp"]),
        (SEG, Z, X, "dp"),
    )
    return jax.shard_map(
        shards,
        mesh=split,
        in_specs=(
            P("dp", TENSOR, None),
            P("dp", TENSOR, None),
            P("dp"),
            P(),
            P(SEG, None),
            P(SEG, None, TENSOR),
            P(SEG, None, TENSOR),
            P(SEG, None, TENSOR),
            P(SEG, TENSOR, None),
            P(SEG, TENSOR, None),
            P(SEG, None, TENSOR),
        ),
        out_specs=(P(SEG, TENSOR, None), P(SEG, None, TENSOR)),
        check_vma=False,
    )
```

```python
import functools
import math

import jax
import jax.numpy as jnp
from jax import lax
from jax.experimental import pallas as pl
from jax.experimental.pallas import tpu as pltpu
from jax.sharding import Mesh
from jax.sharding import PartitionSpec as P

HEAD_SIZE = 128
ADAPTER_RANK = 16
ADAPTER_JOBS = 32
ADAPTER_SCALE = 2.0
EPSILON = 1e-05
SIDE = 4
ROWS = 16
TOKENS = SIDE * SIDE * ROWS
KV_PART = 32
LOW_LANE = 2 * KV_PART
GATHER_CHUNKS = 4
SCATTER_CHUNKS = 4
SEG, Z, X = "segment", "tensor_0", "tensor_1"
TENSOR = (Z, X)
MESH = pl.DeviceIdType.MESH
BF16, F32 = jnp.bfloat16, jnp.float32
VMEM_LIMIT = 60 * 1024 * 1024


def dot(a, b, dims=((1,), (0,))):
    return lax.dot_general(a, b, (dims, ((), ())), preferred_element_type=F32)


def step_of(axis, offset):
    return lax.rem(lax.axis_index(axis) + (offset + SIDE), SIDE)


def remote(src, dst, send_sem, recv_sem, axis, offset):
    return pltpu.make_async_remote_copy(
        src_ref=src,
        dst_ref=dst,
        send_sem=send_sem,
        recv_sem=recv_sem,
        device_id={axis: step_of(axis, offset)},
        device_id_type=MESH,
    )


NEAR = [(Z, 1), (Z, -1), (X, 1), (X, -1)]


def greet(partners, planes):
    barrier = pltpu.get_barrier_semaphore()
    for axis, offset in partners:
        pl.semaphore_signal(
            barrier, inc=1, device_id={axis: step_of(axis, offset)}, device_id_type=MESH
        )
    mine = lax.axis_index(SEG)
    for distance in range(1, planes):
        there = lax.rem(mine + distance, planes)
        pl.semaphore_signal(barrier, inc=1, device_id={SEG: there}, device_id_type=MESH)
    pl.semaphore_wait(barrier, len(partners) + planes - 1)


def order_of(chunk):
    return (Z, X) if chunk % 2 == 0 else (X, Z)


def blocks(ref, axis, place, columns):
    if axis == Z:
        return ref.at[place, :, :, columns]
    return ref.at[:, place, :, columns]


def gather_stages(held, start, size, order, send, recv, started):
    first, second = order
    me = {Z: lax.axis_index(Z), X: lax.axis_index(X)}
    whole = pl.ds(start, size)
    halves = (pl.ds(start, size // 2), pl.ds(start + size // 2, size // 2))

    def go(slot, src, axis, offset):
        copy = remote(src, src, send.at[slot], recv.at[slot], axis, offset)
        copy.start()
        started.append(copy)

    def arrived(slot, where, axis, offset):
        remote(where, where, send.at[slot], recv.at[slot], axis, offset).wait_recv()

    def one(offset, columns):
        place = step_of(first, offset)
        z, x = (place, me[X]) if first == Z else (me[Z], place)
        return held.at[z, x, :, columns]

    def group(offset, columns):
        return blocks(held, second, step_of(second, offset), columns)

    def stage0():
        go(0, one(0, whole), first, 1)
        go(1, one(0, whole), first, -1)

    def stage1():
        arrived(0, one(-1, whole), first, 1)
        go(2, one(-1, halves[0]), first, 1)
        arrived(1, one(1, whole), first, -1)
        go(3, one(1, halves[1]), first, -1)

    def stage2():
        arrived(2, one(2, halves[0]), first, 1)
        arrived(3, one(2, halves[1]), first, -1)
        go(4, group(0, whole), second, 1)
        go(5, group(0, whole), second, -1)

    def stage3():
        arrived(4, group(-1, whole), second, 1)
        go(6, group(-1, halves[0]), second, 1)
        arrived(5, group(1, whole), second, -1)
        go(7, group(1, halves[1]), second, -1)

    def stage4():
        arrived(6, group(2, halves[0]), second, 1)
        arrived(7, group(2, halves[1]), second, -1)

    return stage0, stage1, stage2, stage3, stage4


def gather_chunks(held, send, recv, started):
    size = held.shape[-1] // GATHER_CHUNKS
    return [
        gather_stages(
            held, chunk * size, size, order_of(chunk), send.at[chunk], recv.at[chunk], started
        )
        for chunk in range(GATHER_CHUNKS)
    ]


def gather_scratch(width, chunks=GATHER_CHUNKS):
    return [
        pltpu.VMEM((SIDE, SIDE, ROWS, width), BF16),
        pltpu.SemaphoreType.DMA((chunks, 8)),
        pltpu.SemaphoreType.DMA((chunks, 8)),
    ]


def load_columns(source, target, sem, chunks):
    size = target.shape[1] // chunks
    loads = []
    for chunk in range(chunks):
        at = pl.ds(chunk * size, size)
        copy = pltpu.make_async_copy(source.at[:, at], target.at[:, at], sem.at[chunk])
        copy.start()
        loads.append(copy)
    return loads


def load_rows(source, target, sem, chunks):
    size = target.shape[0] // chunks
    loads = []
    for chunk in range(chunks):
        at = pl.ds(chunk * size, size)
        copy = pltpu.make_async_copy(source.at[at], target.at[at], sem.at[chunk])
        copy.start()
        loads.append(copy)
    return loads


def inverse_of(stream):
    return lax.rsqrt(jnp.mean(stream * stream, axis=-1, keepdims=True) + EPSILON)


def over_tiles(first, extent, body):
    tile = min(512, extent)

    def step(i, carry):
        body(pl.multiple_of(first + i * tile, tile), tile)
        return carry

    lax.fori_loop(0, extent // tile, step, 0)


def rows_of(held, at, tile):
    return held[:, :, :, pl.ds(at, tile)].reshape(TOKENS, tile)


def scatter_sum(part, mid, land1, land2, land3, land4, send, recv, term, finish, started):
    width = part.shape[-1]
    size = width // SCATTER_CHUNKS
    half = size // 2
    me = {Z: lax.axis_index(Z), X: lax.axis_index(X)}

    def columns(chunk, part_of=None):
        if part_of is None:
            return pl.ds(chunk * size, size)
        return pl.ds(chunk * size + part_of * half, half)

    def go(chunk, slot, src, dst, axis, offset):
        copy = remote(src, dst, send.at[chunk, slot], recv.at[chunk, slot], axis, offset)
        copy.start()
        started.append(copy)

    def arrived(chunk, slot, where, axis, offset):
        remote(where, where, send.at[chunk, slot], recv.at[chunk, slot], axis, offset).wait_recv()

    def add_into(target, landed):
        target[...] = (target[...].astype(F32) + landed[...].astype(F32)).astype(BF16)

    def stage0(chunk):
        first, _ = order_of(chunk)
        part[:, :, :, columns(chunk)] = (
            term(chunk * size, size).astype(BF16).reshape(SIDE, SIDE, ROWS, size)
        )
        far = step_of(first, 2)
        go(chunk, 0, blocks(part, first, far, columns(chunk, 0)), land1.at[chunk, 0], first, 1)
        go(chunk, 1, blocks(part, first, far, columns(chunk, 1)), land1.at[chunk, 1], first, -1)

    def stage1(chunk):
        first, _ = order_of(chunk)
        for slot, offset in ((0, 1), (1, -1)):
            arrived(chunk, slot, land1.at[chunk, slot], first, offset)
            near = step_of(first, offset)
            add_into(blocks(part, first, near, columns(chunk, slot)), land1.at[chunk, slot])
            go(
                chunk,
                2 + slot,
                blocks(part, first, near, columns(chunk)),
                land2.at[chunk, slot],
                first,
                offset,
            )

    def stage2(chunk):
        first, second = order_of(chunk)
        arrived(chunk, 2, land2.at[chunk, 0], first, 1)
        arrived(chunk, 3, land2.at[chunk, 1], first, -1)
        own = blocks(part, first, me[first], columns(chunk))
        mid[chunk] = (
            own[...].astype(F32) + land2[chunk, 0].astype(F32) + land2[chunk, 1].astype(F32)
        ).astype(BF16)
        far = step_of(second, 2)
        go(chunk, 4, mid.at[chunk, far, :, pl.ds(0, half)], land3.at[chunk, 0], second, 1)
        go(chunk, 5, mid.at[chunk, far, :, pl.ds(half, half)], land3.at[chunk, 1], second, -1)

    def stage3(chunk):
        _, second = order_of(chunk)
        for slot, offset in ((0, 1), (1, -1)):
            arrived(chunk, 4 + slot, land3.at[chunk, slot], second, offset)
            near = step_of(second, offset)
            add_into(mid.at[chunk, near, :, pl.ds(slot * half, half)], land3.at[chunk, slot])
            go(chunk, 6 + slot, mid.at[chunk, near], land4.at[chunk, slot], second, offset)

    def stage4(chunk):
        _, second = order_of(chunk)
        arrived(chunk, 6, land4.at[chunk, 0], second, 1)
        arrived(chunk, 7, land4.at[chunk, 1], second, -1)
        total = (
            mid[chunk, me[second]].astype(F32)
            + land4[chunk, 0].astype(F32)
            + land4[chunk, 1].astype(F32)
        )
        finish(chunk, chunk * size, size, total)

    stages = [stage0, stage1, stage2, stage3, stage4]
    pairs = SCATTER_CHUNKS // 2
    for turn in range(pairs + len(stages) - 1):
        for place, stage in enumerate(stages):
            pair = turn - place
            if 0 <= pair < pairs:
                stage(2 * pair)
                stage(2 * pair + 1)


def scatter_scratch(width):
    size = width // SCATTER_CHUNKS
    return [
        pltpu.VMEM((SIDE, SIDE, ROWS, width), BF16),
        pltpu.VMEM((SCATTER_CHUNKS, SIDE, ROWS, size), BF16),
        pltpu.VMEM((SCATTER_CHUNKS, 2, SIDE, ROWS, size // 2), BF16),
        pltpu.VMEM((SCATTER_CHUNKS, 2, SIDE, ROWS, size), BF16),
        pltpu.VMEM((SCATTER_CHUNKS, 2, ROWS, size // 2), BF16),
        pltpu.VMEM((SCATTER_CHUNKS, 2, ROWS, size), BF16),
        pltpu.SemaphoreType.DMA((SCATTER_CHUNKS, 8)),
        pltpu.SemaphoreType.DMA((SCATTER_CHUNKS, 8)),
    ]


def spread(all_planes, columns, send, recv, started):
    planes = lax.axis_size(SEG)
    mine = lax.axis_index(SEG)
    for distance in range(1, planes):
        copy = pltpu.make_async_remote_copy(
            src_ref=all_planes.at[mine, :, columns],
            dst_ref=all_planes.at[mine, :, columns],
            send_sem=send.at[distance],
            recv_sem=recv.at[distance],
            device_id={SEG: lax.rem(mine + distance, planes)},
            device_id_type=MESH,
        )
        copy.start()
        started.append(copy)


def spread_wait(all_planes, columns, send, recv):
    planes = lax.axis_size(SEG)
    mine = lax.axis_index(SEG)
    for distance in range(1, planes):
        there = all_planes.at[lax.rem(mine + planes - distance, planes), :, columns]
        pltpu.make_async_remote_copy(
            src_ref=there,
            dst_ref=there,
            send_sem=send.at[distance],
            recv_sem=recv.at[distance],
            device_id={SEG: lax.rem(mine + distance, planes)},
            device_id_type=MESH,
        ).wait_recv()


def turned(value, cosine, sine):
    return value * cosine + pltpu.roll(value, HEAD_SIZE // 2, 1) * sine


def turned_back(value, cosine, sine):
    return value * cosine + pltpu.roll(value * sine, HEAD_SIZE // 2, 1)


def probabilities(query, key):
    scores = dot(query, key, ((1,), (1,))) * (1.0 / math.sqrt(HEAD_SIZE))
    row = lax.broadcasted_iota(jnp.int32, scores.shape, 0)
    column = lax.broadcasted_iota(jnp.int32, scores.shape, 1)
    weights = jnp.exp(jnp.where(row >= column, scores, -1e30))
    return weights / jnp.sum(weights, axis=-1, keepdims=True)


def trade_start(trade, send, recv, source, target):
    copies = []
    for distance in range(1, SIDE):
        copy = remote(
            source(distance), target(distance), send.at[distance], recv.at[distance], X, distance
        )
        copy.start()
        copies.append(copy)
    return copies


def project_sums(held, first, extent, query_w, side_w, query_sum, side_sum):
    def body(at, tile):
        rows = rows_of(held, at, tile)
        query_sum[...] += dot(rows, query_w[pl.ds(at, tile), :])
        side_sum[...] += dot(rows, side_w[:, pl.ds(at, tile)], ((1,), (1,)))

    over_tiles(first, extent, body)


def project_start(side_sum, trade, send, recv, side_out):
    mine = lax.axis_index(X)
    side = side_sum[...].astype(BF16)
    side_out[...] = side
    trade[mine] = side
    return trade_start(
        trade, send, recv, lambda distance: trade.at[mine], lambda distance: trade.at[mine]
    )


def project_local(held, query_sum, side_out, up, cosine, sine, query_out, piece_out):
    query = query_sum[...] + ADAPTER_SCALE * dot(side_out[...], up[...])
    for head in range(query.shape[1] // HEAD_SIZE):
        lanes = slice(head * HEAD_SIZE, (head + 1) * HEAD_SIZE)
        query_out[:, lanes] = turned(query[:, lanes], cosine[...], sine[...]).astype(BF16)
    piece = held.shape[-1] // (SIDE * SIDE)
    first = (lax.axis_index(Z) * SIDE + lax.axis_index(X)) * piece
    piece_out[...] = rows_of(held, pl.multiple_of(first, piece), piece)


def project_end(trade, send, recv, copies, pick, cosine, sine, key_out, value_out):
    for distance in range(1, SIDE):
        there = trade.at[step_of(X, -distance)]
        remote(there, there, send.at[distance], recv.at[distance], X, distance).wait_recv()
    for copy in copies:
        copy.wait_send()
    both = dot(trade[0], pick[0])
    for place in range(1, SIDE):
        both += dot(trade[place], pick[place])
    key_out[...] = turned(both[:, :HEAD_SIZE], cosine[...], sine[...]).astype(BF16)
    value_out[...] = both[:, HEAD_SIZE:].astype(BF16)


def back_sums(held, first, extent, out_w, back_sum):
    def body(at, tile):
        back_sum[...] += dot(rows_of(held, at, tile), out_w[:, pl.ds(at, tile)], ((1,), (1,)))

    over_tiles(first, extent, body)


def start_kernel(
    job, hidden, ending, gain, query_hbm, key_hbm, value_hbm, out_hbm, down, up_table, pick, cosine, sine,
    query_out, key_out, value_out, side_out, piece_out, back_out, side_w, up_out,
    held, send, recv, held_back, send_back, recv_back, held_down, send_down, recv_down,
    query_w, q_sem, s_sem, out_w, o_sem, query_sum, side_sum, back_sum, trade, trade_send, trade_recv,
):
    size = held.shape[-1] // GATHER_CHUNKS
    narrow = [
        pltpu.make_async_copy(key_hbm, side_w.at[pl.ds(0, KV_PART)], s_sem.at[0]),
        pltpu.make_async_copy(value_hbm, side_w.at[pl.ds(KV_PART, KV_PART)], s_sem.at[1]),
    ]
    for copy in narrow:
        copy.start()
    query_loads = load_rows(query_hbm, query_w, q_sem, GATHER_CHUNKS)
    out_loads = load_columns(out_hbm, out_w, o_sem, GATHER_CHUNKS)
    z, x = lax.axis_index(Z), lax.axis_index(X)
    held_back[z, x] = ending[...]
    stream = hidden[...].astype(F32)
    held[z, x] = (stream * inverse_of(stream) * gain[...]).astype(BF16)
    tables = (ADAPTER_RANK, down.shape[1])
    picked = (
        lax.broadcasted_iota(jnp.int32, tables, 1)
        == lax.broadcasted_iota(jnp.int32, tables, 0) + job[0] * ADAPTER_RANK
    ).astype(BF16)
    held_down[z, x] = dot(picked, down[...], ((1,), (1,))).astype(BF16)
    greet(NEAR + [(X, 2)], 1)
    started = []
    first = gather_stages(
        held_down, 0, held_down.shape[-1], (Z, X), send_down.at[0], recv_down.at[0], started
    )
    ahead = gather_chunks(held, send, recv, started)
    behind = gather_chunks(held_back, send_back, recv_back, started)
    for chunk in [first, *ahead, *behind]:
        chunk[0]()
    up_out[...] = jnp.zeros_like(up_out)
    up_out[pl.ds(LOW_LANE, ADAPTER_RANK), :] = dot(picked, up_table[...]).astype(BF16)
    tail = HEAD_SIZE - LOW_LANE - ADAPTER_RANK
    side_w[pl.ds(LOW_LANE + ADAPTER_RANK, tail), :] = jnp.zeros((tail, side_w.shape[1]), BF16)
    query_sum[...] = jnp.zeros_like(query_sum)
    side_sum[...] = jnp.zeros_like(side_sum)
    back_sum[...] = jnp.zeros_like(back_sum)
    for chunk in [first, *ahead, *behind]:
        chunk[1]()
    for chunk in [first, *ahead]:
        chunk[2]()
    for chunk in [first, *ahead]:
        chunk[3]()
    for chunk in behind:
        chunk[2]()
    first[4]()
    piece = held_down.shape[-1]
    for place in range(SIDE * SIDE):
        side_w[pl.ds(LOW_LANE, ADAPTER_RANK), pl.ds(place * piece, piece)] = held_down[
            place // SIDE, place % SIDE
        ]
    for copy in narrow:
        copy.wait()
    for place, chunk in enumerate(ahead):
        chunk[4]()
        query_loads[place].wait()
        project_sums(held, place * size, size, query_w, side_w, query_sum, side_sum)
    copies = project_start(side_sum, trade, trade_send, trade_recv, side_out)
    for chunk in behind:
        chunk[3]()
    project_local(held, query_sum, side_out, up_out, cosine, sine, query_out, piece_out)
    project_end(trade, trade_send, trade_recv, copies, pick, cosine, sine, key_out, value_out)
    for place, chunk in enumerate(behind):
        chunk[4]()
        out_loads[place].wait()
        back_sums(held_back, place * size, size, out_w, back_sum)
    back_out[...] = back_sum[...].astype(BF16)
    for copy in started:
        copy.wait_send()


def advance_kernel(
    owner, hidden, query, key, value, gain, query_hbm, side_hbm, out_hbm, up, pick, cosine, sine,
    hidden_out, query_out, key_out, value_out, side_out, piece_out,
    part, mid, land1, land2, land3, land4, send, recv,
    held, send_held, recv_held,
    query_w, q_sem, side_w, s_sem, out_w, o_sem, attended, planes, p_send, p_recv,
    query_sum, side_sum, trade, trade_send, trade_recv,
):
    width = part.shape[-1]
    size = width // SCATTER_CHUNKS
    out_loads = load_columns(out_hbm, out_w, o_sem, SCATTER_CHUNKS)
    query_loads = load_rows(query_hbm, query_w, q_sem, GATHER_CHUNKS)
    side_loads = load_columns(side_hbm, side_w, s_sem, GATHER_CHUNKS)
    for head in range(query.shape[1] // HEAD_SIZE):
        lanes = slice(head * HEAD_SIZE, (head + 1) * HEAD_SIZE)
        weights = probabilities(query[:, lanes], key[...]).astype(BF16)
        attended[:, lanes] = dot(weights, value[...]).astype(BF16)
    query_sum[...] = jnp.zeros_like(query_sum)
    side_sum[...] = jnp.zeros_like(side_sum)
    greet(NEAR + [(X, 2)], planes.shape[0])
    mine = lax.axis_index(SEG)
    started = []

    def term(first, extent):
        out_loads[first // size].wait()
        return dot(attended[...], out_w[:, pl.ds(first, extent)])

    def finish(chunk, first, extent, total):
        cols = pl.ds(first, extent)
        planes[mine, :, cols] = (hidden[:, cols].astype(F32) + total).astype(BF16)
        spread(planes, cols, p_send.at[chunk], p_recv.at[chunk], started)

    scatter_sum(part, mid, land1, land2, land3, land4, send, recv, term, finish, started)
    for chunk in range(SCATTER_CHUNKS):
        spread_wait(planes, pl.ds(chunk * size, size), p_send.at[chunk], p_recv.at[chunk])
    following = planes[owner[0]]
    hidden_out[...] = following
    stream = following.astype(F32)
    held[lax.axis_index(Z), lax.axis_index(X)] = (stream * inverse_of(stream) * gain[...]).astype(BF16)
    ahead = gather_chunks(held, send_held, recv_held, started)
    for stage in range(4):
        for chunk in ahead:
            chunk[stage]()
    size = width // GATHER_CHUNKS
    for place, chunk in enumerate(ahead):
        chunk[4]()
        query_loads[place].wait()
        side_loads[place].wait()
        project_sums(held, place * size, size, query_w, side_w, query_sum, side_sum)
    copies = project_start(side_sum, trade, trade_send, trade_recv, side_out)
    project_local(held, query_sum, side_out, up, cosine, sine, query_out, piece_out)
    project_end(trade, trade_send, trade_recv, copies, pick, cosine, sine, key_out, value_out)
    for copy in started:
        copy.wait_send()


def attention_reverse(query, key, value, back, cosine, sine, query_grad_ref, pair_grad_ref=None):
    scale = 1.0 / math.sqrt(HEAD_SIZE)
    key_grad = jnp.zeros((TOKENS, HEAD_SIZE), F32)
    value_grad = jnp.zeros((TOKENS, HEAD_SIZE), F32)
    for head in range(query.shape[1] // HEAD_SIZE):
        lanes = slice(head * HEAD_SIZE, (head + 1) * HEAD_SIZE)
        weights = probabilities(query[:, lanes], key[...])
        out_grad = back[:, lanes]
        weight_grad = dot(out_grad, value[...], ((1,), (1,)))
        mean = jnp.sum(weight_grad * weights, axis=-1, keepdims=True)
        score_grad = (weights * (weight_grad - mean) * scale).astype(BF16)
        query_grad = turned_back(dot(score_grad, key[...]), cosine[...], sine[...])
        query_grad_ref[:, lanes] = query_grad.astype(BF16)
        if pair_grad_ref is not None:
            value_grad += dot(weights.astype(BF16), out_grad, ((0,), (0,)))
            key_grad += dot(score_grad, query[:, lanes], ((0,), (0,)))
    if pair_grad_ref is not None:
        pair_grad_ref[:, :HEAD_SIZE] = turned_back(key_grad, cosine[...], sine[...]).astype(BF16)
        pair_grad_ref[:, HEAD_SIZE:] = value_grad.astype(BF16)


LOW_ROWS = slice(LOW_LANE, LOW_LANE + ADAPTER_RANK)


def adapter_shares(query_grad, side, up):
    low = ADAPTER_SCALE * dot(up, query_grad, ((1,), (1,)))
    grad_up = ADAPTER_SCALE * dot(side, query_grad, ((0,), (0,)))
    return low[LOW_ROWS], grad_up[LOW_ROWS]


def retreat_kernel(
    flags, ending, gradient, hidden, gain, query, key, value, side, back, piece, old_piece, old_low, old_up,
    query_hbm, side_hbm, out_hbm, up, pick, cosine, sine,
    gradient_out, back_out, piece_out, low_out, up_out,
    part, mid, land1, land2, land3, land4, send, recv,
    held, send_held, recv_held,
    query_w, q_sem, side_w, s_sem, out_w, o_sem, query_grad, pair_grad, side_grad,
    trade, trade_send, trade_recv, planes, p_send, p_recv, means, m_send, m_recv, back_sum,
):
    width = part.shape[-1]
    size = width // SCATTER_CHUNKS
    query_loads = load_rows(query_hbm, query_w, q_sem, SCATTER_CHUNKS)
    side_loads = load_columns(side_hbm, side_w, s_sem, SCATTER_CHUNKS)
    out_loads = load_columns(out_hbm, out_w, o_sem, GATHER_CHUNKS)
    attention_reverse(query, key, value, back, cosine, sine, query_grad, pair_grad)
    for place in range(SIDE):
        trade[0, place] = dot(pair_grad[...], pick[place], ((1,), (1,))).astype(BF16)
    greet(NEAR + [(X, 2)], planes.shape[0])
    copies = trade_start(
        trade,
        trade_send,
        trade_recv,
        lambda distance: trade.at[0, step_of(X, distance)],
        lambda distance: trade.at[1, distance],
    )
    mine_here = flags[1] != 0
    low, grad_up = adapter_shares(query_grad[...], side[...], up[...])
    low_out[...] = jnp.where(mine_here, low, old_low[...])
    up_out[...] = jnp.where(mine_here, grad_up, old_up[...])
    piece_out[...] = jnp.where(mine_here, piece[...].astype(F32), old_piece[...].astype(F32)).astype(BF16)
    back_sum[...] = jnp.zeros_like(back_sum)
    stream = hidden[...].astype(F32)
    inverse = inverse_of(stream)
    total = trade[0, lax.axis_index(X)].astype(F32)
    total += ADAPTER_SCALE * dot(query_grad[...], up[...], ((1,), (1,)))
    for distance in range(1, SIDE):
        there = trade.at[1, distance]
        remote(there, there, trade_send.at[distance], trade_recv.at[distance], X, distance).wait_recv()
        total += trade[1, distance].astype(F32)
    side_grad[...] = total.astype(BF16)
    mine = lax.axis_index(SEG)
    started = []
    sums = []

    def term(first, extent):
        query_loads[first // size].wait()
        side_loads[first // size].wait()
        at = pl.ds(first, extent)
        return dot(query_grad[...], query_w[at, :], ((1,), (1,))) + dot(side_grad[...], side_w[:, at])

    def finish(chunk, first, extent, total):
        cols = pl.ds(first, extent)
        gained = total * gain[:, cols]
        sums.append(jnp.sum(gained * hidden[:, cols].astype(F32), axis=-1, keepdims=True))
        planes[mine, :, cols] = (inverse * gained).astype(BF16)
        spread(planes, cols, p_send.at[chunk], p_recv.at[chunk], started)

    scatter_sum(part, mid, land1, land2, land3, land4, send, recv, term, finish, started)
    means[mine] = jnp.broadcast_to(sum(sums) / width, (ROWS, HEAD_SIZE))
    spread(means, slice(None), m_send, m_recv, started)
    for chunk in range(SCATTER_CHUNKS):
        spread_wait(planes, pl.ds(chunk * size, size), p_send.at[chunk], p_recv.at[chunk])
    spread_wait(means, slice(None), m_send, m_recv)
    owner = flags[0]
    mean = means[owner][:, :1]
    before = jnp.where(flags[2] != 0, ending[...].astype(F32), gradient[...].astype(F32))
    following = (
        before + planes[owner].astype(F32) - stream * (inverse * inverse * inverse * mean)
    ).astype(BF16)
    gradient_out[...] = following
    held[lax.axis_index(Z), lax.axis_index(X)] = following
    ahead = gather_chunks(held, send_held, recv_held, started)
    for stage in range(4):
        for chunk in ahead:
            chunk[stage]()
    size = width // GATHER_CHUNKS
    for place, chunk in enumerate(ahead):
        chunk[4]()
        out_loads[place].wait()
        back_sums(held, place * size, size, out_w, back_sum)
    back_out[...] = back_sum[...].astype(BF16)
    for copy in copies + started:
        copy.wait_send()


def end_kernel(
    flags, query, key, value, side, back, piece, old_piece, old_low, old_up, up, cosine, sine,
    box_out,
    query_grad, lows_z, lows_x, low_send, low_recv, box, box_send, box_recv,
):
    attention_reverse(query, key, value, back, cosine, sine, query_grad)
    mine_here = flags[1] != 0
    low, grad_up = adapter_shares(query_grad[...], side[...], up[...])
    z, x = lax.axis_index(Z), lax.axis_index(X)
    lows_z[z] = jnp.where(mine_here, low, old_low[...])
    replicas = box.shape[0]
    barrier = pltpu.get_barrier_semaphore()
    around = [(axis, distance) for axis in TENSOR for distance in range(1, SIDE)]
    for axis, offset in around:
        pl.semaphore_signal(
            barrier, inc=1, device_id={axis: step_of(axis, offset)}, device_id_type=MESH
        )
    replica = lax.axis_index("dp")
    if replicas > 1:
        pl.semaphore_signal(barrier, inc=1, device_id={"dp": 1 - replica}, device_id_type=MESH)
    pl.semaphore_wait(barrier, len(around) + replicas - 1)
    copies = []

    def share(lows, axis, place, row):
        for distance in range(1, SIDE):
            copy = remote(
                lows.at[place], lows.at[place], low_send.at[row, distance], low_recv.at[row, distance],
                axis, distance,
            )
            copy.start()
            copies.append(copy)

    def shared(lows, axis, row):
        for distance in range(1, SIDE):
            there = lows.at[step_of(axis, -distance)]
            remote(
                there, there, low_send.at[row, distance], low_recv.at[row, distance], axis, distance
            ).wait_recv()
        return lows[0] + lows[1] + lows[2] + lows[3]

    share(lows_z, Z, z, 0)
    columns, width = query.shape[1], piece.shape[1]
    active = flags[2] != 0
    grad_up = jnp.where(mine_here, grad_up, old_up[...])
    box[replica, :, pl.ds(0, columns)] = jnp.where(active, grad_up, 0.0).astype(BF16)
    spot = box.shape[2] - columns - width
    jobs = (ADAPTER_RANK, spot)
    box[replica, :, pl.ds(columns + width, spot)] = (
        lax.broadcasted_iota(jnp.int32, jobs, 1)
        == lax.broadcasted_iota(jnp.int32, jobs, 0) + flags[3] * ADAPTER_RANK
    ).astype(BF16)
    chosen = jnp.where(mine_here, piece[...].astype(F32), old_piece[...].astype(F32)).astype(BF16)
    lows_x[x] = shared(lows_z, Z, 0)
    share(lows_x, X, x, 1)
    low = shared(lows_x, X, 1).astype(BF16)
    box[replica, :, pl.ds(columns, width)] = jnp.where(active, dot(low, chosen), 0.0).astype(BF16)
    if replicas > 1:
        copy = pltpu.make_async_remote_copy(
            src_ref=box.at[replica],
            dst_ref=box.at[replica],
            send_sem=box_send,
            recv_sem=box_recv,
            device_id={"dp": 1 - replica},
            device_id_type=MESH,
        )
        copy.start()
        there = box.at[1 - replica]
        pltpu.make_async_remote_copy(
            src_ref=there,
            dst_ref=there,
            send_sem=box_send,
            recv_sem=box_recv,
            device_id={"dp": 1 - replica},
            device_id_type=MESH,
        ).wait_recv()
        copy.wait_send()
    for copy in copies:
        copy.wait_send()
    box_out[...] = box[...]


ANYWHERE = pl.BlockSpec(memory_space=pl.ANY)
SCALAR = pl.BlockSpec(memory_space=pltpu.SMEM)
INSIDE = pl.BlockSpec(memory_space=pltpu.VMEM)
SPECS = {"s": SCALAR, "a": ANYWHERE, "v": INSIDE}


def shaped(shape, dtype=BF16):
    return jax.ShapeDtypeStruct(shape, dtype)


def call(kernel, number, places, outputs, scratch, *operands):
    return pl.pallas_call(
        kernel,
        out_shape=tuple(outputs),
        in_specs=[SPECS[place] for place in places],
        out_specs=tuple(INSIDE for _ in outputs),
        scratch_shapes=scratch,
        compiler_params=pltpu.CompilerParams(
            collective_id=number, has_side_effects=True, vmem_limit_bytes=VMEM_LIMIT
        ),
        name=kernel.__name__,
    )(*operands)


def dma(*shape):
    return pltpu.SemaphoreType.DMA(shape)


def projections(width, columns):
    return [
        shaped((TOKENS, columns)),
        shaped((TOKENS, HEAD_SIZE)),
        shaped((TOKENS, HEAD_SIZE)),
        shaped((TOKENS, HEAD_SIZE)),
        shaped((TOKENS, width // (SIDE * SIDE))),
    ]


def start(job, hidden, ending, gain, query_w, key_w, value_w, out_w, down, up_table, pick, cosine, sine):
    width, columns = query_w.shape
    return call(
        start_kernel, 1, "svvv" + "aaaa" + "vvvvv",
        [
            *projections(width, columns),
            shaped((TOKENS, columns)),
            shaped((HEAD_SIZE, width)),
            shaped((HEAD_SIZE, columns)),
        ],
        [
            *gather_scratch(width),
            *gather_scratch(width),
            *gather_scratch(down.shape[0], 1),
            pltpu.VMEM((width, columns), BF16),
            dma(GATHER_CHUNKS),
            dma(2),
            pltpu.VMEM((columns, width), BF16),
            dma(GATHER_CHUNKS),
            pltpu.VMEM((TOKENS, columns), F32),
            pltpu.VMEM((TOKENS, HEAD_SIZE), F32),
            pltpu.VMEM((TOKENS, columns), F32),
            pltpu.VMEM((SIDE, TOKENS, HEAD_SIZE), BF16),
            dma(SIDE),
            dma(SIDE),
        ],
        job, hidden, ending, gain, query_w, key_w, value_w, out_w, down, up_table, pick, cosine, sine,
    )


def advance(owner, hidden, query, key, value, gain, query_w, side_w, out_w, up, pick, cosine, sine, planes):
    width, columns = query_w.shape
    return call(
        advance_kernel, 2, "svvvvv" + "aaa" + "vvvv",
        [shaped((ROWS, width)), *projections(width, columns)],
        [
            *scatter_scratch(width),
            *gather_scratch(width),
            pltpu.VMEM((width, columns), BF16),
            dma(GATHER_CHUNKS),
            pltpu.VMEM((HEAD_SIZE, width), BF16),
            dma(GATHER_CHUNKS),
            pltpu.VMEM((columns, width), BF16),
            dma(SCATTER_CHUNKS),
            pltpu.VMEM((TOKENS, columns), BF16),
            pltpu.VMEM((planes, ROWS, width), BF16),
            dma(SCATTER_CHUNKS, planes),
            dma(SCATTER_CHUNKS, planes),
            pltpu.VMEM((TOKENS, columns), F32),
            pltpu.VMEM((TOKENS, HEAD_SIZE), F32),
            pltpu.VMEM((SIDE, TOKENS, HEAD_SIZE), BF16),
            dma(SIDE),
            dma(SIDE),
        ],
        owner, hidden, query, key, value, gain, query_w, side_w, out_w, up, pick, cosine, sine,
    )


def retreat(flags, ending, gradient, hidden, gain, kept, back, old, query_w, side_w, out_w, up, pick, cosine, sine, planes):
    width, columns = query_w.shape
    query, key, value, side, piece = kept
    return call(
        retreat_kernel, 3, "s" + "v" * 13 + "aaa" + "vvvv",
        [
            shaped((ROWS, width)),
            shaped((TOKENS, columns)),
            shaped(piece.shape),
            shaped((ADAPTER_RANK, TOKENS), F32),
            shaped((ADAPTER_RANK, columns), F32),
        ],
        [
            *scatter_scratch(width),
            *gather_scratch(width),
            pltpu.VMEM((width, columns), BF16),
            dma(SCATTER_CHUNKS),
            pltpu.VMEM((HEAD_SIZE, width), BF16),
            dma(SCATTER_CHUNKS),
            pltpu.VMEM((columns, width), BF16),
            dma(GATHER_CHUNKS),
            pltpu.VMEM((TOKENS, columns), BF16),
            pltpu.VMEM((TOKENS, 2 * HEAD_SIZE), BF16),
            pltpu.VMEM((TOKENS, HEAD_SIZE), BF16),
            pltpu.VMEM((2, SIDE, TOKENS, HEAD_SIZE), BF16),
            dma(SIDE),
            dma(SIDE),
            pltpu.VMEM((planes, ROWS, width), BF16),
            dma(SCATTER_CHUNKS, planes),
            dma(SCATTER_CHUNKS, planes),
            pltpu.VMEM((planes, ROWS, HEAD_SIZE), F32),
            dma(planes),
            dma(planes),
            pltpu.VMEM((TOKENS, columns), F32),
        ],
        flags, ending, gradient, hidden, gain, *kept[:4], back, piece, *old,
        query_w, side_w, out_w, up, pick, cosine, sine,
    )


def end(flags, kept, back, old, up, cosine, sine, replicas):
    query, key, value, side, piece = kept
    columns, width = query.shape[1], piece.shape[1]
    box = (replicas, ADAPTER_RANK, columns + width + ADAPTER_JOBS * ADAPTER_RANK)
    return call(
        end_kernel, 4, "s" + "v" * 12,
        [shaped(box)],
        [
            pltpu.VMEM((TOKENS, columns), BF16),
            pltpu.VMEM((SIDE, ADAPTER_RANK, TOKENS), F32),
            pltpu.VMEM((SIDE, ADAPTER_RANK, TOKENS), F32),
            dma(2, SIDE),
            dma(2, SIDE),
            pltpu.VMEM(box, BF16),
            pltpu.SemaphoreType.DMA,
            pltpu.SemaphoreType.DMA,
        ],
        flags, *kept[:4], back, piece, *old, up, cosine, sine,
    )[0]


def turn_tables():
    positions = jnp.arange(TOKENS, dtype=F32)
    exponent = jnp.arange(HEAD_SIZE // 2, dtype=F32) * (2.0 / HEAD_SIZE)
    angles = positions[:, None] * jnp.exp(-math.log(10000.0) * exponent)[None, :]
    cosine, sine = jnp.cos(angles), jnp.sin(angles)
    return (
        jnp.concatenate([cosine, cosine], axis=1),
        jnp.concatenate([-sine, sine], axis=1),
    )


def pick_table():
    place = jnp.arange(SIDE)[:, None, None]
    row = jnp.arange(HEAD_SIZE)[None, :, None]
    column = jnp.arange(2 * HEAD_SIZE)[None, None, :]
    keys = (row < KV_PART) & (column == place * KV_PART + row)
    values = (
        (row >= KV_PART)
        & (row < 2 * KV_PART)
        & (column == HEAD_SIZE + place * KV_PART + row - KV_PART)
    )
    return (keys | values).astype(BF16)


def shards(
    tokens,
    cotangent,
    sequence_job,
    section_layer_list,
    section_norm_gain,
    query_matrix,
    key_matrix,
    value_matrix,
    output_matrix,
    adapter_down_all,
    adapter_up_all,
):
    segments = lax.axis_size(SEG)
    replicas = lax.axis_size("dp")
    segment_index = lax.axis_index(SEG)
    gain = section_norm_gain.astype(F32)
    query_w = query_matrix[0]
    out_w = output_matrix[0]
    width, columns = query_w.shape
    piece_width = adapter_down_all.shape[1]
    jobs_width = ADAPTER_JOBS * ADAPTER_RANK
    cosine, sine = turn_tables()
    pick = pick_table()

    active = section_layer_list > 0
    places = jnp.arange(segments, dtype=jnp.int32)
    rank = jnp.sum(active[None, :] & (places[None, :] < places[:, None]), axis=1)
    layers = jnp.sum(active.astype(jnp.int32))
    turns = max(segments - 1, 1)
    wanted = jnp.arange(turns, dtype=jnp.int32)
    owners = jnp.sum(
        jnp.where(active[None, :] & (rank[None, :] == wanted[:, None]), places[None, :], 0), axis=1
    ).astype(jnp.int32)
    mine = (owners == segment_index).astype(jnp.int32)
    last = (layers == wanted + 1).astype(jnp.int32)
    ending = cotangent[0]

    *kept, back_ending, side_w, up = start(
        sequence_job, tokens[0], ending, gain, query_w, key_matrix[0].T, value_matrix[0].T, out_w,
        adapter_down_all[0], adapter_up_all[0], pick, cosine, sine,
    )
    nothing = (
        jnp.zeros((TOKENS, piece_width), BF16),
        jnp.zeros((ADAPTER_RANK, TOKENS), F32),
        jnp.zeros((ADAPTER_RANK, columns), F32),
    )

    def beyond(turn, hidden, kept):
        def onward(operand):
            hidden, kept = operand
            hidden, *kept = advance(
                owners[turn][None], hidden, *kept[:4][:3], gain, query_w, side_w, out_w, up, pick,
                cosine, sine, segments,
            )
            gradient, back, old = beyond(turn + 1, hidden, kept)
            flags = jnp.stack([owners[turn + 1], mine[turn + 1], last[turn + 1]])
            gradient, back, *old = retreat(
                flags, ending, gradient, hidden, gain, kept, back, old, query_w, side_w, out_w, up,
                pick, cosine, sine, segments,
            )
            return gradient, back, tuple(old)

        nowhere = (jnp.zeros((ROWS, width), BF16), back_ending, nothing)
        if turn + 1 == turns:
            return nowhere
        return lax.cond(layers > turn + 1, onward, lambda operand: nowhere, (hidden, tuple(kept)))

    _, back, old = beyond(0, tokens[0], kept)
    applied = jnp.sum(jnp.where(places == segment_index, section_layer_list, 0)) > 0
    flags = jnp.stack([owners[0], mine[0], applied.astype(jnp.int32), sequence_job[0]])
    box = end(flags, kept, back, old, up, cosine, sine, replicas)
    box = box.reshape(replicas * ADAPTER_RANK, box.shape[2])
    spots = box[:, columns + piece_width :]
    grad_up = dot(spots, box[:, :columns], ((0,), (0,)))
    grad_down = dot(box[:, columns : columns + piece_width], spots, ((0,), (0,)))
    return (grad_down[None], grad_up[None])


def solution(mesh):
    split = Mesh(
        mesh.devices.reshape(mesh.shape["segment"], SIDE, SIDE, mesh.shape["dp"]),
        (SEG, Z, X, "dp"),
    )
    return jax.shard_map(
        shards,
        mesh=split,
        in_specs=(
            P("dp", TENSOR, None),
            P("dp", TENSOR, None),
            P("dp"),
            P(),
            P(SEG, None),
            P(SEG, None, TENSOR),
            P(SEG, None, TENSOR),
            P(SEG, None, TENSOR),
            P(SEG, TENSOR, None),
            P(SEG, TENSOR, None),
            P(SEG, None, TENSOR),
        ),
        out_specs=(P(SEG, TENSOR, None), P(SEG, None, TENSOR)),
        check_vma=False,
    )
```

```python
import functools
import math

import jax
import jax.numpy as jnp
import numpy as np
from jax import lax
from jax.experimental import pallas as pl
from jax.experimental.pallas import tpu as pltpu
from jax.sharding import Mesh
from jax.sharding import PartitionSpec as P

HEAD_SIZE = 128
ADAPTER_RANK = 16
ADAPTER_JOBS = 32
ADAPTER_SCALE = 2.0
EPSILON = 1e-05
SIDE = 4
ROWS = 16
TOKENS = SIDE * SIDE * ROWS
KV_PART = 32
LOW_LANE = 2 * KV_PART
GATHER_CHUNKS = 4
SCATTER_CHUNKS = 4
SEG, Z, X = "segment", "tensor_0", "tensor_1"
TENSOR = (Z, X)
MESH = pl.DeviceIdType.MESH
BF16, F32 = jnp.bfloat16, jnp.float32
VMEM_LIMIT = 60 * 1024 * 1024


def dot(a, b, dims=((1,), (0,))):
    return lax.dot_general(a, b, (dims, ((), ())), preferred_element_type=F32)


def step_of(axis, offset):
    return lax.rem(lax.axis_index(axis) + (offset + SIDE), SIDE)


def remote(src, dst, send_sem, recv_sem, axis, offset):
    return pltpu.make_async_remote_copy(
        src_ref=src,
        dst_ref=dst,
        send_sem=send_sem,
        recv_sem=recv_sem,
        device_id={axis: step_of(axis, offset)},
        device_id_type=MESH,
    )


NEAR = [(Z, 1), (Z, -1), (X, 1), (X, -1)]


def greet(partners, planes):
    barrier = pltpu.get_barrier_semaphore()
    for axis, offset in partners:
        pl.semaphore_signal(
            barrier, inc=1, device_id={axis: step_of(axis, offset)}, device_id_type=MESH
        )
    mine = lax.axis_index(SEG)
    for distance in range(1, planes):
        there = lax.rem(mine + distance, planes)
        pl.semaphore_signal(barrier, inc=1, device_id={SEG: there}, device_id_type=MESH)
    pl.semaphore_wait(barrier, len(partners) + planes - 1)


def order_of(chunk):
    return (Z, X) if chunk % 2 == 0 else (X, Z)


def blocks(ref, axis, place, columns):
    if axis == Z:
        return ref.at[place, :, :, columns]
    return ref.at[:, place, :, columns]


def gather_stages(held, start, size, order, send, recv, started):
    first, second = order
    me = {Z: lax.axis_index(Z), X: lax.axis_index(X)}
    whole = pl.ds(start, size)
    halves = (pl.ds(start, size // 2), pl.ds(start + size // 2, size // 2))

    def go(slot, src, axis, offset):
        copy = remote(src, src, send.at[slot], recv.at[slot], axis, offset)
        copy.start()
        started.append(copy)

    def arrived(slot, where, axis, offset):
        remote(where, where, send.at[slot], recv.at[slot], axis, offset).wait_recv()

    def one(offset, columns):
        place = step_of(first, offset)
        z, x = (place, me[X]) if first == Z else (me[Z], place)
        return held.at[z, x, :, columns]

    def group(offset, columns):
        return blocks(held, second, step_of(second, offset), columns)

    def stage0():
        go(0, one(0, whole), first, 1)
        go(1, one(0, whole), first, -1)

    def stage1():
        arrived(0, one(-1, whole), first, 1)
        go(2, one(-1, halves[0]), first, 1)
        arrived(1, one(1, whole), first, -1)
        go(3, one(1, halves[1]), first, -1)

    def stage2():
        arrived(2, one(2, halves[0]), first, 1)
        arrived(3, one(2, halves[1]), first, -1)
        go(4, group(0, whole), second, 1)
        go(5, group(0, whole), second, -1)

    def stage3():
        arrived(4, group(-1, whole), second, 1)
        go(6, group(-1, halves[0]), second, 1)
        arrived(5, group(1, whole), second, -1)
        go(7, group(1, halves[1]), second, -1)

    def stage4():
        arrived(6, group(2, halves[0]), second, 1)
        arrived(7, group(2, halves[1]), second, -1)

    return stage0, stage1, stage2, stage3, stage4


def gather_chunks(held, send, recv, started):
    size = held.shape[-1] // GATHER_CHUNKS
    return [
        gather_stages(
            held, chunk * size, size, order_of(chunk), send.at[chunk], recv.at[chunk], started
        )
        for chunk in range(GATHER_CHUNKS)
    ]


def gather_scratch(width, chunks=GATHER_CHUNKS):
    return [
        pltpu.VMEM((SIDE, SIDE, ROWS, width), BF16),
        pltpu.SemaphoreType.DMA((chunks, 8)),
        pltpu.SemaphoreType.DMA((chunks, 8)),
    ]


def load_columns(source, target, sem, chunks):
    size = target.shape[1] // chunks
    loads = []
    for chunk in range(chunks):
        at = pl.ds(chunk * size, size)
        copy = pltpu.make_async_copy(source.at[:, at], target.at[:, at], sem.at[chunk])
        copy.start()
        loads.append(copy)
    return loads


def load_rows(source, target, sem, chunks):
    size = target.shape[0] // chunks
    loads = []
    for chunk in range(chunks):
        at = pl.ds(chunk * size, size)
        copy = pltpu.make_async_copy(source.at[at], target.at[at], sem.at[chunk])
        copy.start()
        loads.append(copy)
    return loads


def inverse_of(stream):
    return lax.rsqrt(jnp.mean(stream * stream, axis=-1, keepdims=True) + EPSILON)


def turn_of(layers, turn):
    owner, count = jnp.int32(0), jnp.int32(0)
    for section in range(layers.shape[0]):
        here = (layers[section] > 0).astype(jnp.int32)
        owner = jnp.where((here > 0) & (count == turn), section, owner)
        count += here
    return owner, owner == lax.axis_index(SEG), count


def over_tiles(first, extent, body):
    tile = min(512, extent)

    def step(i, carry):
        body(pl.multiple_of(first + i * tile, tile), tile)
        return carry

    lax.fori_loop(0, extent // tile, step, 0)


def rows_of(held, at, tile):
    return held[:, :, :, pl.ds(at, tile)].reshape(TOKENS, tile)


def scatter_sum(part, mid, land1, land2, land3, land4, send, recv, term, finish, started):
    width = part.shape[-1]
    size = width // SCATTER_CHUNKS
    half = size // 2
    me = {Z: lax.axis_index(Z), X: lax.axis_index(X)}

    def columns(chunk, part_of=None):
        if part_of is None:
            return pl.ds(chunk * size, size)
        return pl.ds(chunk * size + part_of * half, half)

    def go(chunk, slot, src, dst, axis, offset):
        copy = remote(src, dst, send.at[chunk, slot], recv.at[chunk, slot], axis, offset)
        copy.start()
        started.append(copy)

    def arrived(chunk, slot, where, axis, offset):
        remote(where, where, send.at[chunk, slot], recv.at[chunk, slot], axis, offset).wait_recv()

    def add_into(target, landed):
        target[...] = (target[...].astype(F32) + landed[...].astype(F32)).astype(BF16)

    def stage0(chunk):
        first, _ = order_of(chunk)
        part[:, :, :, columns(chunk)] = (
            term(chunk * size, size).astype(BF16).reshape(SIDE, SIDE, ROWS, size)
        )
        far = step_of(first, 2)
        go(chunk, 0, blocks(part, first, far, columns(chunk, 0)), land1.at[chunk, 0], first, 1)
        go(chunk, 1, blocks(part, first, far, columns(chunk, 1)), land1.at[chunk, 1], first, -1)

    def stage1(chunk):
        first, _ = order_of(chunk)
        for slot, offset in ((0, 1), (1, -1)):
            arrived(chunk, slot, land1.at[chunk, slot], first, offset)
            near = step_of(first, offset)
            add_into(blocks(part, first, near, columns(chunk, slot)), land1.at[chunk, slot])
            go(
                chunk,
                2 + slot,
                blocks(part, first, near, columns(chunk)),
                land2.at[chunk, slot],
                first,
                offset,
            )

    def stage2(chunk):
        first, second = order_of(chunk)
        arrived(chunk, 2, land2.at[chunk, 0], first, 1)
        arrived(chunk, 3, land2.at[chunk, 1], first, -1)
        own = blocks(part, first, me[first], columns(chunk))
        mid[chunk] = (
            own[...].astype(F32) + land2[chunk, 0].astype(F32) + land2[chunk, 1].astype(F32)
        ).astype(BF16)
        far = step_of(second, 2)
        go(chunk, 4, mid.at[chunk, far, :, pl.ds(0, half)], land3.at[chunk, 0], second, 1)
        go(chunk, 5, mid.at[chunk, far, :, pl.ds(half, half)], land3.at[chunk, 1], second, -1)

    def stage3(chunk):
        _, second = order_of(chunk)
        for slot, offset in ((0, 1), (1, -1)):
            arrived(chunk, 4 + slot, land3.at[chunk, slot], second, offset)
            near = step_of(second, offset)
            add_into(mid.at[chunk, near, :, pl.ds(slot * half, half)], land3.at[chunk, slot])
            go(chunk, 6 + slot, mid.at[chunk, near], land4.at[chunk, slot], second, offset)

    def stage4(chunk):
        _, second = order_of(chunk)
        arrived(chunk, 6, land4.at[chunk, 0], second, 1)
        arrived(chunk, 7, land4.at[chunk, 1], second, -1)
        total = (
            mid[chunk, me[second]].astype(F32)
            + land4[chunk, 0].astype(F32)
            + land4[chunk, 1].astype(F32)
        )
        finish(chunk, chunk * size, size, total)

    return stage0, stage1, stage2, stage3, stage4


def sum_and_spread(sums, spreads, summed=None, later=None):
    pairs = [(0, 1), (2, 3)]

    def total(stage, pair):
        for chunk in pairs[pair]:
            sums[stage](chunk)

    def across(stage, pair):
        for chunk in pairs[pair]:
            spreads[chunk][stage]()

    total(0, 0)
    for stage in range(4):
        total(stage, 1)
        if stage == 0 and later is not None:
            later()
        total(stage + 1, 0)
    across(0, 0)
    total(4, 1)
    across(0, 1)
    if summed is not None:
        summed()
    across(1, 0)
    across(1, 1)


def scatter_scratch(width):
    size = width // SCATTER_CHUNKS
    return [
        pltpu.VMEM((SIDE, SIDE, ROWS, width), BF16),
        pltpu.VMEM((SCATTER_CHUNKS, SIDE, ROWS, size), BF16),
        pltpu.VMEM((SCATTER_CHUNKS, 2, SIDE, ROWS, size // 2), BF16),
        pltpu.VMEM((SCATTER_CHUNKS, 2, SIDE, ROWS, size), BF16),
        pltpu.VMEM((SCATTER_CHUNKS, 2, ROWS, size // 2), BF16),
        pltpu.VMEM((SCATTER_CHUNKS, 2, ROWS, size), BF16),
        pltpu.SemaphoreType.DMA((SCATTER_CHUNKS, 8)),
        pltpu.SemaphoreType.DMA((SCATTER_CHUNKS, 8)),
    ]


def plane_step(planes, offset):
    return lax.rem(lax.axis_index(SEG) + (planes + offset), planes)


def spread_stages(all_planes, start, size, send, recv, started):
    planes = all_planes.shape[0]
    columns = pl.ds(start, size)

    def copy_of(origin, distance):
        rows = all_planes.at[plane_step(planes, origin), :, columns]
        return pltpu.make_async_remote_copy(
            src_ref=rows,
            dst_ref=rows,
            send_sem=send.at[distance],
            recv_sem=recv.at[distance],
            device_id={SEG: plane_step(planes, distance)},
            device_id_type=MESH,
        )

    def stage0():
        for distance in range(1, planes):
            copy = copy_of(0, distance)
            copy.start()
            started.append(copy)

    def stage1():
        for distance in range(1, planes):
            copy_of(-distance, distance).wait_recv()

    return stage0, stage1


def spread_chunks(all_planes, chunks, send, recv, started):
    size = all_planes.shape[-1] // chunks
    return [
        spread_stages(all_planes, chunk * size, size, send.at[chunk], recv.at[chunk], started)
        for chunk in range(chunks)
    ]


def turned(value, cosine, sine):
    return value * cosine + pltpu.roll(value, HEAD_SIZE // 2, 1) * sine


def turned_back(value, cosine, sine):
    return value * cosine + pltpu.roll(value * sine, HEAD_SIZE // 2, 1)


def probabilities(query, key):
    scores = dot(query, key, ((1,), (1,))) * (1.0 / math.sqrt(HEAD_SIZE))
    row = lax.broadcasted_iota(jnp.int32, scores.shape, 0)
    column = lax.broadcasted_iota(jnp.int32, scores.shape, 1)
    weights = jnp.exp(jnp.where(row >= column, scores, -1e30))
    return weights / jnp.sum(weights, axis=-1, keepdims=True)


def trade_start(trade, send, recv, source, target):
    copies = []
    for distance in range(1, SIDE):
        copy = remote(
            source(distance), target(distance), send.at[distance], recv.at[distance], X, distance
        )
        copy.start()
        copies.append(copy)
    return copies


def project_sums(held, first, extent, query_w, side_w, query_sum, side_sum):
    def body(at, tile):
        rows = rows_of(held, at, tile)
        query_sum[...] += dot(rows, query_w[pl.ds(at, tile), :])
        side_sum[...] += dot(rows, side_w[:, pl.ds(at, tile)], ((1,), (1,)))

    over_tiles(first, extent, body)


HALF = TOKENS // 2


def two_halves(first, second):
    lane = lax.broadcasted_iota(jnp.int32, first.shape, 1)
    return jnp.where(lane < LOW_LANE, first, second)


def pick(half, place):
    shape = (HEAD_SIZE, 2 * HEAD_SIZE)
    row = lax.broadcasted_iota(jnp.int32, shape, 0) - half * LOW_LANE
    column = lax.broadcasted_iota(jnp.int32, shape, 1) - place * KV_PART
    keys = (row >= 0) & (row < KV_PART) & (column == row)
    values = (row >= KV_PART) & (row < LOW_LANE) & (column == row + HEAD_SIZE - KV_PART)
    return jnp.where(keys | values, 1.0, 0.0).astype(BF16)


def project_start(side_sum, trade, send, recv, side_out):
    mine = lax.axis_index(X)
    side = side_sum[...]
    side_out[...] = side.astype(BF16)
    trade[mine] = two_halves(side[:HALF], pltpu.roll(side[HALF:], LOW_LANE, 1)).astype(BF16)
    return trade_start(
        trade, send, recv, lambda distance: trade.at[mine], lambda distance: trade.at[mine]
    )


def project_local(held, query_sum, side_out, up, cosine, sine, query_out, piece_out):
    query = query_sum[...] + ADAPTER_SCALE * dot(side_out[...], up[...])
    for head in range(query.shape[1] // HEAD_SIZE):
        lanes = slice(head * HEAD_SIZE, (head + 1) * HEAD_SIZE)
        query_out[:, lanes] = turned(query[:, lanes], cosine[...], sine[...]).astype(BF16)
    piece = held.shape[-1] // (SIDE * SIDE)
    first = (lax.axis_index(Z) * SIDE + lax.axis_index(X)) * piece
    piece_out[...] = rows_of(held, pl.multiple_of(first, piece), piece)


def project_end(trade, send, recv, copies, cosine, sine, key_out, value_out):
    for distance in range(1, SIDE):
        there = trade.at[step_of(X, -distance)]
        remote(there, there, send.at[distance], recv.at[distance], X, distance).wait_recv()
    for copy in copies:
        copy.wait_send()
    for half in range(2):
        rows = slice(half * HALF, (half + 1) * HALF)
        both = dot(trade[0], pick(half, 0))
        for place in range(1, SIDE):
            both += dot(trade[place], pick(half, place))
        key_out[rows] = turned(both[:, :HEAD_SIZE], cosine[rows], sine[rows]).astype(BF16)
        value_out[rows] = both[:, HEAD_SIZE:].astype(BF16)


def back_sums(held, first, extent, out_w, back_sum):
    def body(at, tile):
        back_sum[...] += dot(rows_of(held, at, tile), out_w[:, pl.ds(at, tile)], ((1,), (1,)))

    over_tiles(first, extent, body)


def start_kernel(
    only, job, layers, hidden, ending, gain, query_hbm, key_hbm, value_hbm, out_hbm, down, up_table, cosine, sine,
    query_out, key_out, value_out, side_out, piece_out, back_out, side_w, up_out,
    held, send, recv, held_down, send_down, recv_down,
    query_w, q_sem, s_sem, out_w, o_sem, query_sum, side_sum, back_sum, trade, trade_send, trade_recv,
    *second,
):
    size = held.shape[-1] // GATHER_CHUNKS
    narrow = [
        pltpu.make_async_copy(key_hbm, side_w.at[pl.ds(0, KV_PART)], s_sem.at[0]),
        pltpu.make_async_copy(value_hbm, side_w.at[pl.ds(KV_PART, KV_PART)], s_sem.at[1]),
    ]
    for copy in narrow:
        copy.start()
    query_loads = load_rows(query_hbm, query_w, q_sem, GATHER_CHUNKS)
    out_loads = load_columns(out_hbm, out_w, o_sem, GATHER_CHUNKS)
    z, x = lax.axis_index(Z), lax.axis_index(X)
    stream = hidden[...].astype(F32)
    normed = stream * inverse_of(stream) * gain[...].astype(F32)
    if only:
        held_back, send_back, recv_back = second
        held_back[z, x] = ending[...]
    else:
        _, mine_here, _ = turn_of(layers, 0)
        normed = jnp.where(mine_here, normed, ending[...].astype(F32))
    held[z, x] = normed.astype(BF16)
    tables = (ADAPTER_RANK, down.shape[1])
    picked = (
        lax.broadcasted_iota(jnp.int32, tables, 1)
        == lax.broadcasted_iota(jnp.int32, tables, 0) + job[0] * ADAPTER_RANK
    ).astype(BF16)
    held_down[z, x] = dot(picked, down[...], ((1,), (1,))).astype(BF16)
    greet(NEAR + [(X, 2)], 1)
    started = []
    first = gather_stages(
        held_down, 0, held_down.shape[-1], (Z, X), send_down.at[0], recv_down.at[0], started
    )
    ahead = gather_chunks(held, send, recv, started)
    behind = gather_chunks(held_back, send_back, recv_back, started) if only else []
    for chunk in [first, *ahead, *behind]:
        chunk[0]()
    up_out[...] = jnp.zeros_like(up_out)
    up_out[pl.ds(LOW_LANE, ADAPTER_RANK), :] = dot(picked, up_table[...]).astype(BF16)
    tail = HEAD_SIZE - LOW_LANE - ADAPTER_RANK
    side_w[pl.ds(LOW_LANE + ADAPTER_RANK, tail), :] = jnp.zeros((tail, side_w.shape[1]), BF16)
    query_sum[...] = jnp.zeros_like(query_sum)
    side_sum[...] = jnp.zeros_like(side_sum)
    back_sum[...] = jnp.zeros_like(back_sum)
    for chunk in [first, *ahead, *behind]:
        chunk[1]()
    for chunk in [first, *ahead]:
        chunk[2]()
    for chunk in [first, *ahead]:
        chunk[3]()
    for chunk in behind:
        chunk[2]()
    first[4]()
    piece = held_down.shape[-1]
    for place in range(SIDE * SIDE):
        side_w[pl.ds(LOW_LANE, ADAPTER_RANK), pl.ds(place * piece, piece)] = held_down[
            place // SIDE, place % SIDE
        ]
    for copy in narrow:
        copy.wait()
    for place, chunk in enumerate(ahead):
        chunk[4]()
        query_loads[place].wait()
        project_sums(held, place * size, size, query_w, side_w, query_sum, side_sum)
    copies = project_start(side_sum, trade, trade_send, trade_recv, side_out)
    if not only:
        for place in range(GATHER_CHUNKS):
            out_loads[place].wait()
            back_sums(held, place * size, size, out_w, back_sum)
    for chunk in behind:
        chunk[3]()
    project_local(held, query_sum, side_out, up_out, cosine, sine, query_out, piece_out)
    project_end(trade, trade_send, trade_recv, copies, cosine, sine, key_out, value_out)
    for place, chunk in enumerate(behind):
        chunk[4]()
        out_loads[place].wait()
        back_sums(held_back, place * size, size, out_w, back_sum)
    back_out[...] = back_sum[...].astype(BF16)
    for copy in started:
        copy.wait_send()


def advance_kernel(
    turn, layers, hidden, query, key, value, gain, query_hbm, side_hbm, out_hbm, up, cosine, sine,
    hidden_out, query_out, key_out, value_out, side_out, piece_out,
    part, mid, land1, land2, land3, land4, send, recv,
    held, send_held, recv_held,
    query_w, q_sem, side_w, s_sem, out_w, o_sem, attended, planes, p_send, p_recv,
    query_sum, side_sum, trade, trade_send, trade_recv,
):
    width = part.shape[-1]
    size = width // SCATTER_CHUNKS
    owner, _, _ = turn_of(layers, turn)
    out_loads = load_columns(out_hbm, out_w, o_sem, SCATTER_CHUNKS)
    query_loads, side_loads = [], []

    def later():
        query_loads.extend(load_rows(query_hbm, query_w, q_sem, GATHER_CHUNKS))
        side_loads.extend(load_columns(side_hbm, side_w, s_sem, GATHER_CHUNKS))

    for head in range(query.shape[1] // HEAD_SIZE):
        lanes = slice(head * HEAD_SIZE, (head + 1) * HEAD_SIZE)
        weights = probabilities(query[:, lanes], key[...]).astype(BF16)
        attended[:, lanes] = dot(weights, value[...]).astype(BF16)
    query_sum[...] = jnp.zeros_like(query_sum)
    side_sum[...] = jnp.zeros_like(side_sum)
    greet(NEAR + [(X, 2)], planes.shape[0])
    mine = lax.axis_index(SEG)
    started = []

    def term(first, extent):
        out_loads[first // size].wait()
        return dot(attended[...], out_w[:, pl.ds(first, extent)])

    def finish(chunk, first, extent, total):
        cols = pl.ds(first, extent)
        planes[mine, :, cols] = (hidden[:, cols].astype(F32) + total).astype(BF16)

    sum_and_spread(
        scatter_sum(part, mid, land1, land2, land3, land4, send, recv, term, finish, started),
        spread_chunks(planes, SCATTER_CHUNKS, p_send, p_recv, started),
        later=later,
    )
    following = planes[owner]
    hidden_out[...] = following
    stream = following.astype(F32)
    held[lax.axis_index(Z), lax.axis_index(X)] = (
        stream * inverse_of(stream) * gain[...].astype(F32)
    ).astype(BF16)
    ahead = gather_chunks(held, send_held, recv_held, started)
    for stage in range(4):
        for chunk in ahead:
            chunk[stage]()
    size = width // GATHER_CHUNKS
    for place, chunk in enumerate(ahead):
        chunk[4]()
        query_loads[place].wait()
        side_loads[place].wait()
        project_sums(held, place * size, size, query_w, side_w, query_sum, side_sum)
    copies = project_start(side_sum, trade, trade_send, trade_recv, side_out)
    project_local(held, query_sum, side_out, up, cosine, sine, query_out, piece_out)
    project_end(trade, trade_send, trade_recv, copies, cosine, sine, key_out, value_out)
    for copy in started:
        copy.wait_send()


def attention_reverse(query, key, value, back, cosine, sine, query_grad_ref, pair_grad_ref=None):
    scale = 1.0 / math.sqrt(HEAD_SIZE)
    key_grad = jnp.zeros((TOKENS, HEAD_SIZE), F32)
    value_grad = jnp.zeros((TOKENS, HEAD_SIZE), F32)
    for head in range(query.shape[1] // HEAD_SIZE):
        lanes = slice(head * HEAD_SIZE, (head + 1) * HEAD_SIZE)
        weights = probabilities(query[:, lanes], key[...])
        out_grad = back[:, lanes]
        weight_grad = dot(out_grad, value[...], ((1,), (1,)))
        mean = jnp.sum(weight_grad * weights, axis=-1, keepdims=True)
        score_grad = (weights * (weight_grad - mean) * scale).astype(BF16)
        query_grad = turned_back(dot(score_grad, key[...]), cosine[...], sine[...])
        query_grad_ref[:, lanes] = query_grad.astype(BF16)
        if pair_grad_ref is not None:
            value_grad += dot(weights.astype(BF16), out_grad, ((0,), (0,)))
            key_grad += dot(score_grad, query[:, lanes], ((0,), (0,)))
    if pair_grad_ref is not None:
        pair_grad_ref[:, :HEAD_SIZE] = turned_back(key_grad, cosine[...], sine[...]).astype(BF16)
        pair_grad_ref[:, HEAD_SIZE:] = value_grad.astype(BF16)


LOW_ROWS = slice(LOW_LANE, LOW_LANE + ADAPTER_RANK)


def adapter_shares(query_grad, side, up):
    low = ADAPTER_SCALE * dot(up, query_grad, ((1,), (1,)))
    grad_up = ADAPTER_SCALE * dot(side, query_grad, ((0,), (0,)))
    return low[LOW_ROWS], grad_up[LOW_ROWS]


def retreat_kernel(
    turn, layers, ending, gradient, hidden, gain, query, key, value, side, back, piece,
    old_piece, old_low, old_up, query_hbm, side_hbm, out_hbm, up, cosine, sine,
    gradient_out, back_out, piece_out, low_out, up_out,
    part, mid, land1, land2, land3, land4, send, recv,
    held, send_held, recv_held,
    query_w, q_sem, side_w, s_sem, out_w, o_sem, query_grad, pair_grad, side_grad,
    trade, trade_send, trade_recv, planes, p_send, p_recv, means, m_send, m_recv, back_sum,
):
    width = part.shape[-1]
    size = width // SCATTER_CHUNKS
    query_loads = load_rows(query_hbm, query_w, q_sem, SCATTER_CHUNKS)
    side_loads = load_columns(side_hbm, side_w, s_sem, SCATTER_CHUNKS)
    out_loads = []

    def later():
        out_loads.extend(load_columns(out_hbm, out_w, o_sem, GATHER_CHUNKS))

    attention_reverse(query, key, value, back, cosine, sine, query_grad, pair_grad)
    for place in range(SIDE):
        trade[0, place] = (
            dot(pair_grad[:HALF], pick(0, place), ((1,), (1,)))
            + dot(pair_grad[HALF:], pick(1, place), ((1,), (1,)))
        ).astype(BF16)
    greet(NEAR + [(X, 2)], planes.shape[0])
    copies = trade_start(
        trade,
        trade_send,
        trade_recv,
        lambda distance: trade.at[0, step_of(X, distance)],
        lambda distance: trade.at[1, distance],
    )
    owner, mine_here, count = turn_of(layers, turn)
    low, grad_up = adapter_shares(query_grad[...], side[...], up[...])
    low_out[...] = jnp.where(mine_here, low, old_low[...])
    up_out[...] = jnp.where(mine_here, grad_up, old_up[...])
    piece_out[...] = jnp.where(mine_here, piece[...].astype(F32), old_piece[...].astype(F32)).astype(BF16)
    back_sum[...] = jnp.zeros_like(back_sum)
    stream = hidden[...].astype(F32)
    inverse = inverse_of(stream)
    total = trade[0, lax.axis_index(X)].astype(F32)
    for distance in range(1, SIDE):
        there = trade.at[1, distance]
        remote(there, there, trade_send.at[distance], trade_recv.at[distance], X, distance).wait_recv()
        total += trade[1, distance].astype(F32)
    wide_low = ADAPTER_SCALE * dot(query_grad[...], up[...], ((1,), (1,)))
    side_grad[:HALF] = two_halves(total, wide_low[:HALF]).astype(BF16)
    side_grad[HALF:] = two_halves(pltpu.roll(total, LOW_LANE, 1), wide_low[HALF:]).astype(BF16)
    mine = lax.axis_index(SEG)
    started = []
    sums = []

    def term(first, extent):
        query_loads[first // size].wait()
        side_loads[first // size].wait()
        at = pl.ds(first, extent)
        return dot(query_grad[...], query_w[at, :], ((1,), (1,))) + dot(side_grad[...], side_w[:, at])

    def finish(chunk, first, extent, total):
        cols = pl.ds(first, extent)
        gained = total * gain[:, cols].astype(F32)
        sums.append(jnp.sum(gained * hidden[:, cols].astype(F32), axis=-1, keepdims=True))
        planes[mine, :, cols] = (inverse * gained).astype(BF16)

    mean_spread = spread_stages(means, 0, means.shape[-1], m_send, m_recv, started)

    def summed():
        means[mine] = jnp.broadcast_to(sum(sums) / width, means.shape[1:])
        mean_spread[0]()

    sum_and_spread(
        scatter_sum(part, mid, land1, land2, land3, land4, send, recv, term, finish, started),
        spread_chunks(planes, SCATTER_CHUNKS, p_send, p_recv, started),
        summed,
        later,
    )
    for stage in mean_spread[1:]:
        stage()
    mean = means[owner][:, :1]
    before = jnp.where(count == turn + 1, ending[...].astype(F32), gradient[...].astype(F32))
    following = (
        before + planes[owner].astype(F32) - stream * (inverse * inverse * inverse * mean)
    ).astype(BF16)
    gradient_out[...] = following
    held[lax.axis_index(Z), lax.axis_index(X)] = following
    ahead = gather_chunks(held, send_held, recv_held, started)
    for stage in range(4):
        for chunk in ahead:
            chunk[stage]()
    size = width // GATHER_CHUNKS
    for place, chunk in enumerate(ahead):
        chunk[4]()
        out_loads[place].wait()
        back_sums(held, place * size, size, out_w, back_sum)
    back_out[...] = back_sum[...].astype(BF16)
    for copy in copies + started:
        copy.wait_send()


def end_kernel(
    job, layers, query, key, value, side, back, piece, old_piece, old_low, old_up, up, cosine, sine,
    box_out,
    query_grad, lows_z, lows_x, low_send, low_recv, box, box_send, box_recv,
):
    attention_reverse(query, key, value, back, cosine, sine, query_grad)
    _, mine_here, _ = turn_of(layers, 0)
    low, grad_up = adapter_shares(query_grad[...], side[...], up[...])
    z, x = lax.axis_index(Z), lax.axis_index(X)
    lows_z[z] = jnp.where(mine_here, low, old_low[...])
    replicas = box.shape[0]
    barrier = pltpu.get_barrier_semaphore()
    around = [(axis, distance) for axis in TENSOR for distance in range(1, SIDE)]
    for axis, offset in around:
        pl.semaphore_signal(
            barrier, inc=1, device_id={axis: step_of(axis, offset)}, device_id_type=MESH
        )
    replica = lax.axis_index("dp")
    if replicas > 1:
        pl.semaphore_signal(barrier, inc=1, device_id={"dp": 1 - replica}, device_id_type=MESH)
    pl.semaphore_wait(barrier, len(around) + replicas - 1)
    copies = []

    def share(lows, axis, place, row):
        for distance in range(1, SIDE):
            copy = remote(
                lows.at[place], lows.at[place], low_send.at[row, distance], low_recv.at[row, distance],
                axis, distance,
            )
            copy.start()
            copies.append(copy)

    def shared(lows, axis, row):
        for distance in range(1, SIDE):
            there = lows.at[step_of(axis, -distance)]
            remote(
                there, there, low_send.at[row, distance], low_recv.at[row, distance], axis, distance
            ).wait_recv()
        return lows[0] + lows[1] + lows[2] + lows[3]

    share(lows_z, Z, z, 0)
    columns, width = query.shape[1], piece.shape[1]
    applied = jnp.int32(0)
    for section in range(layers.shape[0]):
        applied += jnp.where(section == lax.axis_index(SEG), layers[section], 0)
    active = applied > 0
    grad_up = jnp.where(mine_here, grad_up, old_up[...])
    box[replica, :, pl.ds(0, columns)] = jnp.where(active, grad_up, 0.0).astype(BF16)
    spot = box.shape[2] - columns - width
    jobs = (ADAPTER_RANK, spot)
    box[replica, :, pl.ds(columns + width, spot)] = (
        lax.broadcasted_iota(jnp.int32, jobs, 1)
        == lax.broadcasted_iota(jnp.int32, jobs, 0) + job[0] * ADAPTER_RANK
    ).astype(BF16)
    chosen = jnp.where(mine_here, piece[...].astype(F32), old_piece[...].astype(F32)).astype(BF16)
    lows_x[x] = shared(lows_z, Z, 0)
    share(lows_x, X, x, 1)
    low = shared(lows_x, X, 1).astype(BF16)
    box[replica, :, pl.ds(columns, width)] = jnp.where(active, dot(low, chosen), 0.0).astype(BF16)
    if replicas > 1:
        copy = pltpu.make_async_remote_copy(
            src_ref=box.at[replica],
            dst_ref=box.at[replica],
            send_sem=box_send,
            recv_sem=box_recv,
            device_id={"dp": 1 - replica},
            device_id_type=MESH,
        )
        copy.start()
        there = box.at[1 - replica]
        pltpu.make_async_remote_copy(
            src_ref=there,
            dst_ref=there,
            send_sem=box_send,
            recv_sem=box_recv,
            device_id={"dp": 1 - replica},
            device_id_type=MESH,
        ).wait_recv()
        copy.wait_send()
    for copy in copies:
        copy.wait_send()
    box_out[...] = box[...]


ANYWHERE = pl.BlockSpec(memory_space=pl.ANY)
SCALAR = pl.BlockSpec(memory_space=pltpu.SMEM)
INSIDE = pl.BlockSpec(memory_space=pltpu.VMEM)
SPECS = {"s": SCALAR, "a": ANYWHERE, "v": INSIDE}


def shaped(shape, dtype=BF16):
    return jax.ShapeDtypeStruct(shape, dtype)


def call(kernel, number, places, outputs, scratch, *operands):
    return pl.pallas_call(
        kernel,
        out_shape=tuple(outputs),
        in_specs=[SPECS[place] for place in places],
        out_specs=tuple(INSIDE for _ in outputs),
        scratch_shapes=scratch,
        compiler_params=pltpu.CompilerParams(
            collective_id=number, has_side_effects=True, vmem_limit_bytes=VMEM_LIMIT
        ),
        name=getattr(kernel, "func", kernel).__name__,
    )(*operands)


def dma(*shape):
    return pltpu.SemaphoreType.DMA(shape)


def projections(width, columns):
    return [
        shaped((TOKENS, columns)),
        shaped((TOKENS, HEAD_SIZE)),
        shaped((TOKENS, HEAD_SIZE)),
        shaped((TOKENS, HEAD_SIZE)),
        shaped((TOKENS, width // (SIDE * SIDE))),
    ]


def start(only, job, layers, hidden, ending, gain, query_w, key_w, value_w, out_w, down, up_table, cosine, sine):
    width, columns = query_w.shape
    return call(
        functools.partial(start_kernel, only), 1 + only, "ssvvv" + "aaaa" + "vvvv",
        [
            *projections(width, columns),
            shaped((TOKENS, columns)),
            shaped((HEAD_SIZE, width)),
            shaped((HEAD_SIZE, columns)),
        ],
        [
            *gather_scratch(width),
            *gather_scratch(down.shape[0], 1),
            pltpu.VMEM((width, columns), BF16),
            dma(GATHER_CHUNKS),
            dma(2),
            pltpu.VMEM((columns, width), BF16),
            dma(GATHER_CHUNKS),
            pltpu.VMEM((TOKENS, columns), F32),
            pltpu.VMEM((TOKENS, HEAD_SIZE), F32),
            pltpu.VMEM((TOKENS, columns), F32),
            pltpu.VMEM((SIDE, HALF, HEAD_SIZE), BF16),
            dma(SIDE),
            dma(SIDE),
            *(gather_scratch(width) if only else []),
        ],
        job, layers, hidden, ending, gain, query_w, key_w, value_w, out_w, down, up_table, cosine, sine,
    )


def advance(turn, layers, hidden, query, key, value, gain, query_w, side_w, out_w, up, cosine, sine):
    width, columns = query_w.shape
    planes = layers.shape[0]
    return call(
        functools.partial(advance_kernel, turn), 10 + turn, "svvvvv" + "aaa" + "vvv",
        [shaped((ROWS, width)), *projections(width, columns)],
        [
            *scatter_scratch(width),
            *gather_scratch(width),
            pltpu.VMEM((width, columns), BF16),
            dma(GATHER_CHUNKS),
            pltpu.VMEM((HEAD_SIZE, width), BF16),
            dma(GATHER_CHUNKS),
            pltpu.VMEM((columns, width), BF16),
            dma(SCATTER_CHUNKS),
            pltpu.VMEM((TOKENS, columns), BF16),
            pltpu.VMEM((planes, ROWS, width), BF16),
            dma(SCATTER_CHUNKS, 4),
            dma(SCATTER_CHUNKS, 4),
            pltpu.VMEM((TOKENS, columns), F32),
            pltpu.VMEM((TOKENS, HEAD_SIZE), F32),
            pltpu.VMEM((SIDE, HALF, HEAD_SIZE), BF16),
            dma(SIDE),
            dma(SIDE),
        ],
        layers, hidden, query, key, value, gain, query_w, side_w, out_w, up, cosine, sine,
    )


def retreat(
    turn, layers, ending, gradient, hidden, gain, kept, back, old,
    query_w, side_w, out_w, up, cosine, sine,
):
    width, columns = query_w.shape
    planes = layers.shape[0]
    query, key, value, side, piece = kept
    return call(
        functools.partial(retreat_kernel, turn), 20 + turn, "s" + "v" * 13 + "aaa" + "vvv",
        [
            shaped((ROWS, width)),
            shaped((TOKENS, columns)),
            shaped(piece.shape),
            shaped((ADAPTER_RANK, TOKENS), F32),
            shaped((ADAPTER_RANK, columns), F32),
        ],
        [
            *scatter_scratch(width),
            *gather_scratch(width),
            pltpu.VMEM((width, columns), BF16),
            dma(SCATTER_CHUNKS),
            pltpu.VMEM((HEAD_SIZE, width), BF16),
            dma(SCATTER_CHUNKS),
            pltpu.VMEM((columns, width), BF16),
            dma(GATHER_CHUNKS),
            pltpu.VMEM((TOKENS, columns), BF16),
            pltpu.VMEM((TOKENS, 2 * HEAD_SIZE), BF16),
            pltpu.VMEM((TOKENS, HEAD_SIZE), BF16),
            pltpu.VMEM((2, SIDE, HALF, HEAD_SIZE), BF16),
            dma(SIDE),
            dma(SIDE),
            pltpu.VMEM((planes, ROWS, width), BF16),
            dma(SCATTER_CHUNKS, 4),
            dma(SCATTER_CHUNKS, 4),
            pltpu.VMEM((planes, ROWS, 2 * HEAD_SIZE), F32),
            dma(4),
            dma(4),
            pltpu.VMEM((TOKENS, columns), F32),
        ],
        layers, ending, gradient, hidden, gain, *kept[:4], back, piece, *old,
        query_w, side_w, out_w, up, cosine, sine,
    )


def end(job, layers, kept, back, old, up, cosine, sine, replicas):
    query, key, value, side, piece = kept
    columns, width = query.shape[1], piece.shape[1]
    box = (replicas, ADAPTER_RANK, columns + width + ADAPTER_JOBS * ADAPTER_RANK)
    return call(
        end_kernel, 4, "ss" + "v" * 12,
        [shaped(box)],
        [
            pltpu.VMEM((TOKENS, columns), BF16),
            pltpu.VMEM((SIDE, ADAPTER_RANK, TOKENS), F32),
            pltpu.VMEM((SIDE, ADAPTER_RANK, TOKENS), F32),
            dma(2, SIDE),
            dma(2, SIDE),
            pltpu.VMEM(box, BF16),
            pltpu.SemaphoreType.DMA,
            pltpu.SemaphoreType.DMA,
        ],
        job, layers, *kept[:4], back, piece, *old, up, cosine, sine,
    )[0]


def placed_kernel(box, down_out, up_out):
    columns, width = up_out.shape[1], down_out.shape[0]
    spots = box[:, columns + width :]
    down_out[...] = dot(box[:, columns : columns + width], spots, ((0,), (0,)))
    up_out[...] = dot(spots, box[:, :columns], ((0,), (0,)))


def placed(box, columns, width):
    jobs = ADAPTER_JOBS * ADAPTER_RANK
    return pl.pallas_call(
        placed_kernel,
        out_shape=(shaped((width, jobs), F32), shaped((jobs, columns), F32)),
        in_specs=[INSIDE],
        out_specs=(INSIDE, INSIDE),
    )(box)


def turn_tables():
    exponent = np.arange(HEAD_SIZE // 2) * (2.0 / HEAD_SIZE)
    angles = np.arange(TOKENS)[:, None] * np.exp(-math.log(10000.0) * exponent)[None, :]
    cosine, sine = np.cos(angles), np.sin(angles)
    return (
        jnp.asarray(np.concatenate([cosine, cosine], axis=1), F32),
        jnp.asarray(np.concatenate([-sine, sine], axis=1), F32),
    )


def shards(
    tokens,
    cotangent,
    sequence_job,
    section_layer_list,
    section_norm_gain,
    query_matrix,
    key_matrix,
    value_matrix,
    output_matrix,
    adapter_down_all,
    adapter_up_all,
):
    segments = lax.axis_size(SEG)
    replicas = lax.axis_size("dp")
    gain = section_norm_gain
    query_w = query_matrix[0]
    out_w = output_matrix[0]
    width, columns = query_w.shape
    piece_width = adapter_down_all.shape[1]
    cosine, sine = turn_tables()
    turns = max(segments - 1, 1)
    layers = section_layer_list
    count = jnp.sum((layers > 0).astype(jnp.int32))
    ending = cotangent[0]

    def first(only):
        return lambda: start(
            only, sequence_job, layers, tokens[0], ending, gain, query_w, key_matrix[0].T,
            value_matrix[0].T, out_w, adapter_down_all[0], adapter_up_all[0], cosine, sine,
        )

    if turns == 1:
        *kept, back_ending, side_w, up = first(True)()
    else:
        *kept, back_ending, side_w, up = lax.cond(count > 1, first(False), first(True))
    nothing = (
        jnp.zeros((TOKENS, piece_width), BF16),
        jnp.zeros((ADAPTER_RANK, TOKENS), F32),
        jnp.zeros((ADAPTER_RANK, columns), F32),
    )

    def beyond(turn, hidden, kept):
        def onward(operand):
            hidden, kept = operand
            hidden, *kept = advance(
                turn, layers, hidden, *kept[:3], gain, query_w, side_w, out_w, up, cosine, sine
            )
            gradient, back, old = beyond(turn + 1, hidden, kept)
            gradient, back, *old = retreat(
                turn + 1, layers, ending, gradient, hidden, gain, kept, back, old,
                query_w, side_w, out_w, up, cosine, sine,
            )
            return gradient, back, tuple(old)

        nowhere = (jnp.zeros((ROWS, width), BF16), back_ending, nothing)
        if turn + 1 == turns:
            return nowhere
        return lax.cond(count > turn + 1, onward, lambda operand: nowhere, (hidden, tuple(kept)))

    _, back, old = beyond(0, tokens[0], kept)
    box = end(sequence_job, layers, kept, back, old, up, cosine, sine, replicas)
    grad_down, grad_up = placed(box.reshape(replicas * ADAPTER_RANK, box.shape[2]), columns, piece_width)
    return (grad_down[None], grad_up[None])


def solution(mesh):
    split = Mesh(
        mesh.devices.reshape(mesh.shape["segment"], SIDE, SIDE, mesh.shape["dp"]),
        (SEG, Z, X, "dp"),
    )
    return jax.shard_map(
        shards,
        mesh=split,
        in_specs=(
            P("dp", TENSOR, None),
            P("dp", TENSOR, None),
            P("dp"),
            P(),
            P(SEG, None),
            P(SEG, None, TENSOR),
            P(SEG, None, TENSOR),
            P(SEG, None, TENSOR),
            P(SEG, TENSOR, None),
            P(SEG, TENSOR, None),
            P(SEG, None, TENSOR),
        ),
        out_specs=(P(SEG, TENSOR, None), P(SEG, None, TENSOR)),
        check_vma=False,
    )
```

```python
import functools
import math

import jax
import jax.numpy as jnp
import numpy as np
from jax import lax
from jax.experimental import pallas as pl
from jax.experimental.pallas import tpu as pltpu
from jax.sharding import Mesh
from jax.sharding import PartitionSpec as P

HEAD_SIZE = 128
ADAPTER_RANK = 16
ADAPTER_JOBS = 32
ADAPTER_SCALE = 2.0
EPSILON = 1e-05
SIDE = 4
ROWS = 16
TOKENS = SIDE * SIDE * ROWS
KV_PART = 32
LOW_LANE = 2 * KV_PART
GATHER_CHUNKS = 4
SCATTER_PARTS = (8, 8, 8, 8)
SCATTER_CHUNKS = len(SCATTER_PARTS)
SEG, Z, X = "segment", "tensor_0", "tensor_1"
TENSOR = (Z, X)
MESH = pl.DeviceIdType.MESH
BF16, F32 = jnp.bfloat16, jnp.float32
VMEM_LIMIT = 60 * 1024 * 1024


def dot(a, b, dims=((1,), (0,))):
    return lax.dot_general(a, b, (dims, ((), ())), preferred_element_type=F32)


def step_of(axis, offset):
    return lax.rem(lax.axis_index(axis) + (offset + SIDE), SIDE)


def remote(src, dst, send_sem, recv_sem, axis, offset):
    return pltpu.make_async_remote_copy(
        src_ref=src,
        dst_ref=dst,
        send_sem=send_sem,
        recv_sem=recv_sem,
        device_id={axis: step_of(axis, offset)},
        device_id_type=MESH,
    )


NEAR = [(Z, 1), (Z, -1), (X, 1), (X, -1)]


def greet(partners, planes):
    barrier = pltpu.get_barrier_semaphore()
    for axis, offset in partners:
        pl.semaphore_signal(
            barrier, inc=1, device_id={axis: step_of(axis, offset)}, device_id_type=MESH
        )
    mine = lax.axis_index(SEG)
    for distance in range(1, planes):
        there = lax.rem(mine + distance, planes)
        pl.semaphore_signal(barrier, inc=1, device_id={SEG: there}, device_id_type=MESH)


def await_greeting(partners, planes):
    pl.semaphore_wait(pltpu.get_barrier_semaphore(), len(partners) + planes - 1)


def order_of(chunk):
    return (Z, X) if chunk % 2 == 0 else (X, Z)


def blocks(ref, axis, place, columns):
    if axis == Z:
        return ref.at[place, :, :, columns]
    return ref.at[:, place, :, columns]


def gather_stages(held, start, size, order, send, recv, started):
    first, second = order
    me = {Z: lax.axis_index(Z), X: lax.axis_index(X)}
    whole = pl.ds(start, size)
    halves = (pl.ds(start, size // 2), pl.ds(start + size // 2, size // 2))

    def go(slot, src, axis, offset):
        copy = remote(src, src, send.at[slot], recv.at[slot], axis, offset)
        copy.start()
        started.append(copy)

    def arrived(slot, where, axis, offset):
        remote(where, where, send.at[slot], recv.at[slot], axis, offset).wait_recv()

    def one(offset, columns):
        place = step_of(first, offset)
        z, x = (place, me[X]) if first == Z else (me[Z], place)
        return held.at[z, x, :, columns]

    def group(offset, columns):
        return blocks(held, second, step_of(second, offset), columns)

    def stage0():
        go(0, one(0, whole), first, 1)
        go(1, one(0, whole), first, -1)

    def stage1():
        arrived(0, one(-1, whole), first, 1)
        go(2, one(-1, halves[0]), first, 1)
        arrived(1, one(1, whole), first, -1)
        go(3, one(1, halves[1]), first, -1)

    def stage2():
        arrived(2, one(2, halves[0]), first, 1)
        arrived(3, one(2, halves[1]), first, -1)
        go(4, group(0, whole), second, 1)
        go(5, group(0, whole), second, -1)

    def stage3():
        arrived(4, group(-1, whole), second, 1)
        go(6, group(-1, halves[0]), second, 1)
        arrived(5, group(1, whole), second, -1)
        go(7, group(1, halves[1]), second, -1)

    def stage4():
        arrived(6, group(2, halves[0]), second, 1)
        arrived(7, group(2, halves[1]), second, -1)

    return stage0, stage1, stage2, stage3, stage4


def gather_chunks(held, send, recv, started):
    size = held.shape[-1] // GATHER_CHUNKS
    return [
        gather_stages(
            held, chunk * size, size, order_of(chunk), send.at[chunk], recv.at[chunk], started
        )
        for chunk in range(GATHER_CHUNKS)
    ]


def gather_scratch(width, chunks=GATHER_CHUNKS):
    return [
        pltpu.VMEM((SIDE, SIDE, ROWS, width), BF16),
        pltpu.SemaphoreType.DMA((chunks, 8)),
        pltpu.SemaphoreType.DMA((chunks, 8)),
    ]


def even_spans(width):
    size = width // GATHER_CHUNKS
    return [(chunk * size, size) for chunk in range(GATHER_CHUNKS)]


def load_columns(source, target, sem, parts):
    loads = []
    for chunk, part in enumerate(parts):
        at = pl.ds(*part)
        copy = pltpu.make_async_copy(source.at[:, at], target.at[:, at], sem.at[chunk])
        copy.start()
        loads.append(copy)
    return loads


def load_rows(source, target, sem, parts):
    loads = []
    for chunk, part in enumerate(parts):
        at = pl.ds(*part)
        copy = pltpu.make_async_copy(source.at[at], target.at[at], sem.at[chunk])
        copy.start()
        loads.append(copy)
    return loads


def inverse_of(stream):
    return lax.rsqrt(jnp.mean(stream * stream, axis=-1, keepdims=True) + EPSILON)


def turn_of(layers, turn):
    owner, count = jnp.int32(0), jnp.int32(0)
    for section in range(layers.shape[0]):
        here = (layers[section] > 0).astype(jnp.int32)
        owner = jnp.where((here > 0) & (count == turn), section, owner)
        count += here
    return owner, owner == lax.axis_index(SEG), count


def over_tiles(first, extent, body):
    tile = min(512, extent)

    def step(i, carry):
        body(pl.multiple_of(first + i * tile, tile), tile)
        return carry

    lax.fori_loop(0, extent // tile, step, 0)


def rows_of(held, at, tile):
    return held[:, :, :, pl.ds(at, tile)].reshape(TOKENS, tile)


def spans(width):
    unit = width // sum(SCATTER_PARTS)
    starts = [unit * sum(SCATTER_PARTS[:chunk]) for chunk in range(SCATTER_CHUNKS)]
    return [(start, unit * part) for start, part in zip(starts, SCATTER_PARTS)]


def scatter_sum(part, mid, land1, land2, land3, land4, send, recv, term, finish, started):
    chunk_spans = spans(part.shape[-1])
    me = {Z: lax.axis_index(Z), X: lax.axis_index(X)}

    def columns(chunk, part_of=None):
        start, size = chunk_spans[chunk]
        if part_of is None:
            return pl.ds(start, size)
        return pl.ds(start + part_of * (size // 2), size // 2)

    def whole(ref, chunk, *places):
        index = (chunk, *places, *[slice(None)] * (len(ref.shape) - 2 - len(places)))
        return ref.at[(*index, pl.ds(0, chunk_spans[chunk][1]))]

    def halved(ref, chunk, *places, at=0):
        half = chunk_spans[chunk][1] // 2
        index = (chunk, *places, *[slice(None)] * (len(ref.shape) - 2 - len(places)))
        return ref.at[(*index, pl.ds(at * half, half))]

    def go(chunk, slot, src, dst, axis, offset):
        copy = remote(src, dst, send.at[chunk, slot], recv.at[chunk, slot], axis, offset)
        copy.start()
        started.append(copy)

    def arrived(chunk, slot, where, axis, offset):
        remote(where, where, send.at[chunk, slot], recv.at[chunk, slot], axis, offset).wait_recv()

    def add_into(target, landed):
        target[...] = (target[...].astype(F32) + landed[...].astype(F32)).astype(BF16)

    def stage0(chunk):
        first, _ = order_of(chunk)
        start, size = chunk_spans[chunk]
        part[:, :, :, columns(chunk)] = (
            term(chunk, start, size).astype(BF16).reshape(SIDE, SIDE, ROWS, size)
        )
        far = step_of(first, 2)
        go(chunk, 0, blocks(part, first, far, columns(chunk, 0)), halved(land1, chunk, 0), first, 1)
        go(chunk, 1, blocks(part, first, far, columns(chunk, 1)), halved(land1, chunk, 1), first, -1)

    def stage1(chunk):
        first, _ = order_of(chunk)
        for slot, offset in ((0, 1), (1, -1)):
            arrived(chunk, slot, halved(land1, chunk, slot), first, offset)
            near = step_of(first, offset)
            add_into(blocks(part, first, near, columns(chunk, slot)), halved(land1, chunk, slot))
            go(
                chunk,
                2 + slot,
                blocks(part, first, near, columns(chunk)),
                whole(land2, chunk, slot),
                first,
                offset,
            )

    def stage2(chunk):
        first, second = order_of(chunk)
        arrived(chunk, 2, whole(land2, chunk, 0), first, 1)
        arrived(chunk, 3, whole(land2, chunk, 1), first, -1)
        own = blocks(part, first, me[first], columns(chunk))
        whole(mid, chunk)[...] = (
            own[...].astype(F32) + whole(land2, chunk, 0)[...].astype(F32) + whole(land2, chunk, 1)[...].astype(F32)
        ).astype(BF16)
        far = step_of(second, 2)
        go(chunk, 4, whole(mid, chunk, far), whole(land3, chunk, 0), second, 2)
        for slot, offset in ((0, 1), (1, -1)):
            near = step_of(second, offset)
            go(chunk, 6 + slot, whole(mid, chunk, near), whole(land4, chunk, slot), second, offset)

    def stage3(chunk):
        _, second = order_of(chunk)
        arrived(chunk, 6, whole(land4, chunk, 0), second, 1)
        arrived(chunk, 7, whole(land4, chunk, 1), second, -1)
        arrived(chunk, 4, whole(land3, chunk, 0), second, 2)
        total = (
            whole(mid, chunk, me[second])[...].astype(F32)
            + whole(land4, chunk, 0)[...].astype(F32)
            + whole(land4, chunk, 1)[...].astype(F32)
            + whole(land3, chunk, 0)[...].astype(F32)
        )
        finish(chunk, *chunk_spans[chunk], total)

    return stage0, stage1, stage2, stage3


def sum_and_spread(sums, spreads, summed=None, later=None):
    pairs = [(chunk, chunk + 1) for chunk in range(0, SCATTER_CHUNKS, 2)]
    for turn in range(len(pairs) + len(sums) - 1):
        for stage in range(len(sums)):
            pair = turn - stage
            if 0 <= pair < len(pairs):
                for chunk in pairs[pair]:
                    sums[stage](chunk)
                if stage == len(sums) - 1:
                    for chunk in pairs[pair]:
                        spreads[chunk][0]()
        if turn == 1 and later is not None:
            later()
    if summed is not None:
        summed()
    for spread in spreads:
        spread[1]()


def scatter_scratch(width):
    size = max(size for _, size in spans(width))
    return [
        pltpu.VMEM((SIDE, SIDE, ROWS, width), BF16),
        pltpu.VMEM((SCATTER_CHUNKS, SIDE, ROWS, size), BF16),
        pltpu.VMEM((SCATTER_CHUNKS, 2, SIDE, ROWS, size // 2), BF16),
        pltpu.VMEM((SCATTER_CHUNKS, 2, SIDE, ROWS, size), BF16),
        pltpu.VMEM((SCATTER_CHUNKS, 1, ROWS, size), BF16),
        pltpu.VMEM((SCATTER_CHUNKS, 2, ROWS, size), BF16),
        pltpu.SemaphoreType.DMA((SCATTER_CHUNKS, 8)),
        pltpu.SemaphoreType.DMA((SCATTER_CHUNKS, 8)),
    ]


def far_first(count):
    return sorted(range(1, count), key=lambda distance: -min(distance, count - distance))


def plane_step(planes, offset):
    return lax.rem(lax.axis_index(SEG) + (planes + offset), planes)


def spread_stages(all_planes, start, size, send, recv, started):
    planes = all_planes.shape[0]
    columns = pl.ds(start, size)

    def copy_of(origin, distance):
        rows = all_planes.at[plane_step(planes, origin), :, columns]
        return pltpu.make_async_remote_copy(
            src_ref=rows,
            dst_ref=rows,
            send_sem=send.at[distance],
            recv_sem=recv.at[distance],
            device_id={SEG: plane_step(planes, distance)},
            device_id_type=MESH,
        )

    def stage0():
        for distance in far_first(planes):
            copy = copy_of(0, distance)
            copy.start()
            started.append(copy)

    def stage1():
        for distance in range(1, planes):
            copy_of(-distance, distance).wait_recv()

    return stage0, stage1


def spread_chunks(all_planes, send, recv, started):
    return [
        spread_stages(all_planes, start, size, send.at[chunk], recv.at[chunk], started)
        for chunk, (start, size) in enumerate(spans(all_planes.shape[-1]))
    ]


def turned(value, cosine, sine):
    return value * cosine + pltpu.roll(value, HEAD_SIZE // 2, 1) * sine


def turned_back(value, cosine, sine):
    return value * cosine + pltpu.roll(value * sine, HEAD_SIZE // 2, 1)


def probabilities(query, key):
    scores = dot(query, key, ((1,), (1,))) * (1.0 / math.sqrt(HEAD_SIZE))
    row = lax.broadcasted_iota(jnp.int32, scores.shape, 0)
    column = lax.broadcasted_iota(jnp.int32, scores.shape, 1)
    weights = jnp.exp(jnp.where(row >= column, scores, -1e30))
    return weights / jnp.sum(weights, axis=-1, keepdims=True)


def trade_start(trade, send, recv, source, target):
    copies = []
    for distance in far_first(SIDE):
        copy = remote(
            source(distance), target(distance), send.at[distance], recv.at[distance], X, distance
        )
        copy.start()
        copies.append(copy)
    return copies


def project_sums(held, first, extent, query_w, side_w, query_sum, side_sum):
    def body(at, tile):
        rows = rows_of(held, at, tile)
        query_sum[...] += dot(rows, query_w[pl.ds(at, tile), :])
        side_sum[...] += dot(rows, side_w[:, pl.ds(at, tile)], ((1,), (1,)))

    over_tiles(first, extent, body)


HALF = TOKENS // 2


def two_halves(first, second):
    lane = lax.broadcasted_iota(jnp.int32, first.shape, 1)
    return jnp.where(lane < LOW_LANE, first, second)


def pick(half, place):
    shape = (HEAD_SIZE, 2 * HEAD_SIZE)
    row = lax.broadcasted_iota(jnp.int32, shape, 0) - half * LOW_LANE
    column = lax.broadcasted_iota(jnp.int32, shape, 1) - place * KV_PART
    keys = (row >= 0) & (row < KV_PART) & (column == row)
    values = (row >= KV_PART) & (row < LOW_LANE) & (column == row + HEAD_SIZE - KV_PART)
    return jnp.where(keys | values, 1.0, 0.0).astype(BF16)


def project_start(side_sum, trade, send, recv, side_out):
    mine = lax.axis_index(X)
    side = side_sum[...]
    side_out[...] = side.astype(BF16)
    trade[mine] = two_halves(side[:HALF], pltpu.roll(side[HALF:], LOW_LANE, 1)).astype(BF16)
    return trade_start(
        trade, send, recv, lambda distance: trade.at[mine], lambda distance: trade.at[mine]
    )


def project_local(held, query_sum, side_out, up, cosine, sine, query_out, piece_out):
    query = query_sum[...] + ADAPTER_SCALE * dot(side_out[...], up[...])
    for head in range(query.shape[1] // HEAD_SIZE):
        lanes = slice(head * HEAD_SIZE, (head + 1) * HEAD_SIZE)
        query_out[:, lanes] = turned(query[:, lanes], cosine[...], sine[...]).astype(BF16)
    piece = held.shape[-1] // (SIDE * SIDE)
    first = (lax.axis_index(Z) * SIDE + lax.axis_index(X)) * piece
    piece_out[...] = rows_of(held, pl.multiple_of(first, piece), piece)


def project_end(trade, send, recv, copies, cosine, sine, key_out, value_out):
    for distance in range(1, SIDE):
        there = trade.at[step_of(X, -distance)]
        remote(there, there, send.at[distance], recv.at[distance], X, distance).wait_recv()
    for copy in copies:
        copy.wait_send()
    for half in range(2):
        rows = slice(half * HALF, (half + 1) * HALF)
        both = dot(trade[0], pick(half, 0))
        for place in range(1, SIDE):
            both += dot(trade[place], pick(half, place))
        key_out[rows] = turned(both[:, :HEAD_SIZE], cosine[rows], sine[rows]).astype(BF16)
        value_out[rows] = both[:, HEAD_SIZE:].astype(BF16)


def back_sums(held, first, extent, out_w, back_sum):
    def body(at, tile):
        back_sum[...] += dot(rows_of(held, at, tile), out_w[:, pl.ds(at, tile)], ((1,), (1,)))

    over_tiles(first, extent, body)


def start_kernel(
    only, job, layers, hidden, ending, gain, query_hbm, key_hbm, value_hbm, out_hbm, down, up_table, cosine, sine,
    query_out, key_out, value_out, side_out, piece_out, back_out, side_w, up_out,
    held, send, recv, held_down, send_down, recv_down,
    query_w, q_sem, s_sem, out_w, o_sem, query_sum, side_sum, back_sum, trade, trade_send, trade_recv,
    *second,
):
    greet(NEAR + [(X, 2), (Z, 2)], 1)
    size = held.shape[-1] // GATHER_CHUNKS
    narrow = [
        pltpu.make_async_copy(key_hbm, side_w.at[pl.ds(0, KV_PART)], s_sem.at[0]),
        pltpu.make_async_copy(value_hbm, side_w.at[pl.ds(KV_PART, KV_PART)], s_sem.at[1]),
    ]
    for copy in narrow:
        copy.start()
    query_loads = load_rows(query_hbm, query_w, q_sem, even_spans(held.shape[-1]))
    out_loads = load_columns(out_hbm, out_w, o_sem, even_spans(held.shape[-1]))
    z, x = lax.axis_index(Z), lax.axis_index(X)
    stream = hidden[...].astype(F32)
    normed = stream * inverse_of(stream) * gain[...].astype(F32)
    if only:
        held_back, send_back, recv_back = second
        held_back[z, x] = ending[...]
    else:
        _, mine_here, _ = turn_of(layers, 0)
        normed = jnp.where(mine_here, normed, ending[...].astype(F32))
    held[z, x] = normed.astype(BF16)
    tables = (ADAPTER_RANK, down.shape[1])
    picked = (
        lax.broadcasted_iota(jnp.int32, tables, 1)
        == lax.broadcasted_iota(jnp.int32, tables, 0) + job[0] * ADAPTER_RANK
    ).astype(BF16)
    held_down[z, x] = dot(picked, down[...], ((1,), (1,))).astype(BF16)
    await_greeting(NEAR + [(X, 2), (Z, 2)], 1)
    started = []
    first = gather_stages(
        held_down, 0, held_down.shape[-1], (Z, X), send_down.at[0], recv_down.at[0], started
    )
    ahead = gather_chunks(held, send, recv, started)
    behind = gather_chunks(held_back, send_back, recv_back, started) if only else []
    for chunk in [first, *ahead, *behind]:
        chunk[0]()
    up_out[...] = jnp.zeros_like(up_out)
    up_out[pl.ds(LOW_LANE, ADAPTER_RANK), :] = dot(picked, up_table[...]).astype(BF16)
    tail = HEAD_SIZE - LOW_LANE - ADAPTER_RANK
    side_w[pl.ds(LOW_LANE + ADAPTER_RANK, tail), :] = jnp.zeros((tail, side_w.shape[1]), BF16)
    query_sum[...] = jnp.zeros_like(query_sum)
    side_sum[...] = jnp.zeros_like(side_sum)
    back_sum[...] = jnp.zeros_like(back_sum)
    for chunk in [first, *ahead, *behind]:
        chunk[1]()
    for chunk in [first, *ahead]:
        chunk[2]()
    for chunk in [first, *ahead]:
        chunk[3]()
    for chunk in behind:
        chunk[2]()
    first[4]()
    piece = held_down.shape[-1]
    for place in range(SIDE * SIDE):
        side_w[pl.ds(LOW_LANE, ADAPTER_RANK), pl.ds(place * piece, piece)] = held_down[
            place // SIDE, place % SIDE
        ]
    for copy in narrow:
        copy.wait()
    for place, chunk in enumerate(ahead):
        chunk[4]()
        query_loads[place].wait()
        project_sums(held, place * size, size, query_w, side_w, query_sum, side_sum)
    copies = project_start(side_sum, trade, trade_send, trade_recv, side_out)
    if not only:
        for place in range(GATHER_CHUNKS):
            out_loads[place].wait()
            back_sums(held, place * size, size, out_w, back_sum)
    for chunk in behind:
        chunk[3]()
    project_local(held, query_sum, side_out, up_out, cosine, sine, query_out, piece_out)
    project_end(trade, trade_send, trade_recv, copies, cosine, sine, key_out, value_out)
    for place, chunk in enumerate(behind):
        chunk[4]()
        out_loads[place].wait()
        back_sums(held_back, place * size, size, out_w, back_sum)
    back_out[...] = back_sum[...].astype(BF16)
    for copy in started:
        copy.wait_send()


def advance_kernel(
    turn, layers, hidden, query, key, value, gain, query_hbm, side_hbm, out_hbm, up, cosine, sine,
    hidden_out, query_out, key_out, value_out, side_out, piece_out,
    part, mid, land1, land2, land3, land4, send, recv,
    held, send_held, recv_held,
    query_w, q_sem, side_w, s_sem, out_w, o_sem, attended, planes, p_send, p_recv,
    query_sum, side_sum, trade, trade_send, trade_recv,
):
    width = part.shape[-1]
    greet(NEAR + [(X, 2), (Z, 2)], planes.shape[0])
    owner, _, _ = turn_of(layers, turn)
    out_loads = load_columns(out_hbm, out_w, o_sem, spans(part.shape[-1]))
    query_loads, side_loads = [], []

    def later():
        query_loads.extend(load_rows(query_hbm, query_w, q_sem, even_spans(held.shape[-1])))
        side_loads.extend(load_columns(side_hbm, side_w, s_sem, even_spans(held.shape[-1])))

    for head in range(query.shape[1] // HEAD_SIZE):
        lanes = slice(head * HEAD_SIZE, (head + 1) * HEAD_SIZE)
        weights = probabilities(query[:, lanes], key[...]).astype(BF16)
        attended[:, lanes] = dot(weights, value[...]).astype(BF16)
    query_sum[...] = jnp.zeros_like(query_sum)
    side_sum[...] = jnp.zeros_like(side_sum)
    await_greeting(NEAR + [(X, 2), (Z, 2)], planes.shape[0])
    mine = lax.axis_index(SEG)
    started = []

    def term(chunk, first, extent):
        out_loads[chunk].wait()
        return dot(attended[...], out_w[:, pl.ds(first, extent)])

    def finish(chunk, first, extent, total):
        cols = pl.ds(first, extent)
        planes[mine, :, cols] = (hidden[:, cols].astype(F32) + total).astype(BF16)

    sum_and_spread(
        scatter_sum(part, mid, land1, land2, land3, land4, send, recv, term, finish, started),
        spread_chunks(planes, p_send, p_recv, started),
        later=later,
    )
    following = planes[owner]
    hidden_out[...] = following
    stream = following.astype(F32)
    held[lax.axis_index(Z), lax.axis_index(X)] = (
        stream * inverse_of(stream) * gain[...].astype(F32)
    ).astype(BF16)
    ahead = gather_chunks(held, send_held, recv_held, started)
    for stage in range(4):
        for chunk in ahead:
            chunk[stage]()
    size = width // GATHER_CHUNKS
    for place, chunk in enumerate(ahead):
        chunk[4]()
        query_loads[place].wait()
        side_loads[place].wait()
        project_sums(held, place * size, size, query_w, side_w, query_sum, side_sum)
    copies = project_start(side_sum, trade, trade_send, trade_recv, side_out)
    project_local(held, query_sum, side_out, up, cosine, sine, query_out, piece_out)
    project_end(trade, trade_send, trade_recv, copies, cosine, sine, key_out, value_out)
    for copy in started:
        copy.wait_send()


def attention_reverse(query, key, value, back, cosine, sine, query_grad_ref, pair_grad_ref=None):
    scale = 1.0 / math.sqrt(HEAD_SIZE)
    key_grad = jnp.zeros((TOKENS, HEAD_SIZE), F32)
    value_grad = jnp.zeros((TOKENS, HEAD_SIZE), F32)
    for head in range(query.shape[1] // HEAD_SIZE):
        lanes = slice(head * HEAD_SIZE, (head + 1) * HEAD_SIZE)
        weights = probabilities(query[:, lanes], key[...])
        out_grad = back[:, lanes]
        weight_grad = dot(out_grad, value[...], ((1,), (1,)))
        mean = jnp.sum(weight_grad * weights, axis=-1, keepdims=True)
        score_grad = (weights * (weight_grad - mean) * scale).astype(BF16)
        query_grad = turned_back(dot(score_grad, key[...]), cosine[...], sine[...])
        query_grad_ref[:, lanes] = query_grad.astype(BF16)
        if pair_grad_ref is not None:
            value_grad += dot(weights.astype(BF16), out_grad, ((0,), (0,)))
            key_grad += dot(score_grad, query[:, lanes], ((0,), (0,)))
    if pair_grad_ref is not None:
        pair_grad_ref[:, :HEAD_SIZE] = turned_back(key_grad, cosine[...], sine[...]).astype(BF16)
        pair_grad_ref[:, HEAD_SIZE:] = value_grad.astype(BF16)


LOW_ROWS = slice(LOW_LANE, LOW_LANE + ADAPTER_RANK)


def adapter_shares(query_grad, side, up):
    low = ADAPTER_SCALE * dot(up, query_grad, ((1,), (1,)))
    grad_up = ADAPTER_SCALE * dot(side, query_grad, ((0,), (0,)))
    return low[LOW_ROWS], grad_up[LOW_ROWS]


def retreat_kernel(
    turn, layers, ending, gradient, hidden, gain, query, key, value, side, back, piece,
    old_piece, old_low, old_up, query_hbm, side_hbm, out_hbm, up, cosine, sine,
    gradient_out, back_out, piece_out, low_out, up_out,
    part, mid, land1, land2, land3, land4, send, recv,
    held, send_held, recv_held,
    query_w, q_sem, side_w, s_sem, out_w, o_sem, query_grad, pair_grad, side_grad,
    trade, trade_send, trade_recv, planes, p_send, p_recv, means, m_send, m_recv, back_sum,
):
    width = part.shape[-1]
    greet(NEAR + [(X, 2), (Z, 2)], planes.shape[0])
    query_loads = load_rows(query_hbm, query_w, q_sem, spans(part.shape[-1]))
    side_loads = load_columns(side_hbm, side_w, s_sem, spans(part.shape[-1]))
    out_loads = []

    def later():
        out_loads.extend(load_columns(out_hbm, out_w, o_sem, even_spans(held.shape[-1])))

    attention_reverse(query, key, value, back, cosine, sine, query_grad, pair_grad)
    for place in range(SIDE):
        trade[0, place] = (
            dot(pair_grad[:HALF], pick(0, place), ((1,), (1,)))
            + dot(pair_grad[HALF:], pick(1, place), ((1,), (1,)))
        ).astype(BF16)
    await_greeting(NEAR + [(X, 2), (Z, 2)], planes.shape[0])
    copies = trade_start(
        trade,
        trade_send,
        trade_recv,
        lambda distance: trade.at[0, step_of(X, distance)],
        lambda distance: trade.at[1, distance],
    )
    owner, mine_here, count = turn_of(layers, turn)
    low, grad_up = adapter_shares(query_grad[...], side[...], up[...])
    low_out[...] = jnp.where(mine_here, low, old_low[...])
    up_out[...] = jnp.where(mine_here, grad_up, old_up[...])
    piece_out[...] = jnp.where(mine_here, piece[...].astype(F32), old_piece[...].astype(F32)).astype(BF16)
    back_sum[...] = jnp.zeros_like(back_sum)
    stream = hidden[...].astype(F32)
    inverse = inverse_of(stream)
    total = trade[0, lax.axis_index(X)].astype(F32)
    for distance in range(1, SIDE):
        there = trade.at[1, distance]
        remote(there, there, trade_send.at[distance], trade_recv.at[distance], X, distance).wait_recv()
        total += trade[1, distance].astype(F32)
    wide_low = ADAPTER_SCALE * dot(query_grad[...], up[...], ((1,), (1,)))
    side_grad[:HALF] = two_halves(total, wide_low[:HALF]).astype(BF16)
    side_grad[HALF:] = two_halves(pltpu.roll(total, LOW_LANE, 1), wide_low[HALF:]).astype(BF16)
    mine = lax.axis_index(SEG)
    started = []
    sums = []

    def term(chunk, first, extent):
        query_loads[chunk].wait()
        side_loads[chunk].wait()
        at = pl.ds(first, extent)
        return dot(query_grad[...], query_w[at, :], ((1,), (1,))) + dot(side_grad[...], side_w[:, at])

    def finish(chunk, first, extent, total):
        cols = pl.ds(first, extent)
        gained = total * gain[:, cols].astype(F32)
        sums.append(jnp.sum(gained * hidden[:, cols].astype(F32), axis=-1, keepdims=True))
        planes[mine, :, cols] = (inverse * gained).astype(BF16)

    mean_spread = spread_stages(means, 0, means.shape[-1], m_send, m_recv, started)

    def summed():
        means[mine] = jnp.broadcast_to(sum(sums) / width, means.shape[1:])
        mean_spread[0]()

    sum_and_spread(
        scatter_sum(part, mid, land1, land2, land3, land4, send, recv, term, finish, started),
        spread_chunks(planes, p_send, p_recv, started),
        summed,
        later,
    )
    for stage in mean_spread[1:]:
        stage()
    mean = means[owner][:, :1]
    before = jnp.where(count == turn + 1, ending[...].astype(F32), gradient[...].astype(F32))
    following = (
        before + planes[owner].astype(F32) - stream * (inverse * inverse * inverse * mean)
    ).astype(BF16)
    gradient_out[...] = following
    held[lax.axis_index(Z), lax.axis_index(X)] = following
    ahead = gather_chunks(held, send_held, recv_held, started)
    for stage in range(4):
        for chunk in ahead:
            chunk[stage]()
    size = width // GATHER_CHUNKS
    for place, chunk in enumerate(ahead):
        chunk[4]()
        out_loads[place].wait()
        back_sums(held, place * size, size, out_w, back_sum)
    back_out[...] = back_sum[...].astype(BF16)
    for copy in copies + started:
        copy.wait_send()


def end_kernel(
    job, layers, query, key, value, side, back, piece, old_piece, old_low, old_up, up, cosine, sine,
    box_out,
    query_grad, lows_z, lows_x, low_send, low_recv, box, box_send, box_recv,
):
    replicas = box.shape[0]
    barrier = pltpu.get_barrier_semaphore()
    around = [(axis, distance) for axis in TENSOR for distance in range(1, SIDE)]
    for axis, offset in around:
        pl.semaphore_signal(
            barrier, inc=1, device_id={axis: step_of(axis, offset)}, device_id_type=MESH
        )
    replica = lax.axis_index("dp")
    if replicas > 1:
        pl.semaphore_signal(barrier, inc=1, device_id={"dp": 1 - replica}, device_id_type=MESH)
    attention_reverse(query, key, value, back, cosine, sine, query_grad)
    _, mine_here, _ = turn_of(layers, 0)
    low, grad_up = adapter_shares(query_grad[...], side[...], up[...])
    z, x = lax.axis_index(Z), lax.axis_index(X)
    lows_z[z] = jnp.where(mine_here, low, old_low[...])
    pl.semaphore_wait(barrier, len(around) + replicas - 1)
    columns, width = query.shape[1], piece.shape[1]
    copies = []

    def share(lows, axis, place, row):
        for distance in far_first(SIDE):
            copy = remote(
                lows.at[place], lows.at[place], low_send.at[row, distance], low_recv.at[row, distance],
                axis, distance,
            )
            copy.start()
            copies.append(copy)

    def shared(lows, axis, row):
        for distance in range(1, SIDE):
            there = lows.at[step_of(axis, -distance)]
            remote(
                there, there, low_send.at[row, distance], low_recv.at[row, distance], axis, distance
            ).wait_recv()
        return lows[0] + lows[1] + lows[2] + lows[3]

    share(lows_z, Z, z, 0)
    columns, width = query.shape[1], piece.shape[1]
    applied = jnp.int32(0)
    for section in range(layers.shape[0]):
        applied += jnp.where(section == lax.axis_index(SEG), layers[section], 0)
    active = applied > 0
    grad_up = jnp.where(mine_here, grad_up, old_up[...])
    box[replica, :, pl.ds(0, columns)] = jnp.where(active, grad_up, 0.0).astype(BF16)
    spot = box.shape[2] - columns - width
    jobs = (ADAPTER_RANK, spot)
    box[replica, :, pl.ds(columns + width, spot)] = (
        lax.broadcasted_iota(jnp.int32, jobs, 1)
        == lax.broadcasted_iota(jnp.int32, jobs, 0) + job[0] * ADAPTER_RANK
    ).astype(BF16)
    chosen = jnp.where(mine_here, piece[...].astype(F32), old_piece[...].astype(F32)).astype(BF16)
    lows_x[x] = shared(lows_z, Z, 0)
    share(lows_x, X, x, 1)
    low = shared(lows_x, X, 1).astype(BF16)
    box[replica, :, pl.ds(columns, width)] = jnp.where(active, dot(low, chosen), 0.0).astype(BF16)
    if replicas > 1:
        copy = pltpu.make_async_remote_copy(
            src_ref=box.at[replica],
            dst_ref=box.at[replica],
            send_sem=box_send,
            recv_sem=box_recv,
            device_id={"dp": 1 - replica},
            device_id_type=MESH,
        )
        copy.start()
        there = box.at[1 - replica]
        pltpu.make_async_remote_copy(
            src_ref=there,
            dst_ref=there,
            send_sem=box_send,
            recv_sem=box_recv,
            device_id={"dp": 1 - replica},
            device_id_type=MESH,
        ).wait_recv()
        copy.wait_send()
    for copy in copies:
        copy.wait_send()
    box_out[...] = box[...]


ANYWHERE = pl.BlockSpec(memory_space=pl.ANY)
SCALAR = pl.BlockSpec(memory_space=pltpu.SMEM)
INSIDE = pl.BlockSpec(memory_space=pltpu.VMEM)
SPECS = {"s": SCALAR, "a": ANYWHERE, "v": INSIDE}


def shaped(shape, dtype=BF16):
    return jax.ShapeDtypeStruct(shape, dtype)


def call(kernel, number, places, outputs, scratch, *operands):
    return pl.pallas_call(
        kernel,
        out_shape=tuple(outputs),
        in_specs=[SPECS[place] for place in places],
        out_specs=tuple(INSIDE for _ in outputs),
        scratch_shapes=scratch,
        compiler_params=pltpu.CompilerParams(
            collective_id=number, has_side_effects=True, vmem_limit_bytes=VMEM_LIMIT
        ),
        name=getattr(kernel, "func", kernel).__name__,
    )(*operands)


def dma(*shape):
    return pltpu.SemaphoreType.DMA(shape)


def projections(width, columns):
    return [
        shaped((TOKENS, columns)),
        shaped((TOKENS, HEAD_SIZE)),
        shaped((TOKENS, HEAD_SIZE)),
        shaped((TOKENS, HEAD_SIZE)),
        shaped((TOKENS, width // (SIDE * SIDE))),
    ]


def start(only, job, layers, hidden, ending, gain, query_w, key_w, value_w, out_w, down, up_table, cosine, sine):
    width, columns = query_w.shape
    return call(
        functools.partial(start_kernel, only), 1 + only, "ssvvv" + "aaaa" + "vvvv",
        [
            *projections(width, columns),
            shaped((TOKENS, columns)),
            shaped((HEAD_SIZE, width)),
            shaped((HEAD_SIZE, columns)),
        ],
        [
            *gather_scratch(width),
            *gather_scratch(down.shape[0], 1),
            pltpu.VMEM((width, columns), BF16),
            dma(GATHER_CHUNKS),
            dma(2),
            pltpu.VMEM((columns, width), BF16),
            dma(GATHER_CHUNKS),
            pltpu.VMEM((TOKENS, columns), F32),
            pltpu.VMEM((TOKENS, HEAD_SIZE), F32),
            pltpu.VMEM((TOKENS, columns), F32),
            pltpu.VMEM((SIDE, HALF, HEAD_SIZE), BF16),
            dma(SIDE),
            dma(SIDE),
            *(gather_scratch(width) if only else []),
        ],
        job, layers, hidden, ending, gain, query_w, key_w, value_w, out_w, down, up_table, cosine, sine,
    )


def advance(turn, layers, hidden, query, key, value, gain, query_w, side_w, out_w, up, cosine, sine):
    width, columns = query_w.shape
    planes = layers.shape[0]
    return call(
        functools.partial(advance_kernel, turn), 10 + turn, "svvvvv" + "aaa" + "vvv",
        [shaped((ROWS, width)), *projections(width, columns)],
        [
            *scatter_scratch(width),
            *gather_scratch(width),
            pltpu.VMEM((width, columns), BF16),
            dma(GATHER_CHUNKS),
            pltpu.VMEM((HEAD_SIZE, width), BF16),
            dma(GATHER_CHUNKS),
            pltpu.VMEM((columns, width), BF16),
            dma(SCATTER_CHUNKS),
            pltpu.VMEM((TOKENS, columns), BF16),
            pltpu.VMEM((planes, ROWS, width), BF16),
            dma(SCATTER_CHUNKS, 4),
            dma(SCATTER_CHUNKS, 4),
            pltpu.VMEM((TOKENS, columns), F32),
            pltpu.VMEM((TOKENS, HEAD_SIZE), F32),
            pltpu.VMEM((SIDE, HALF, HEAD_SIZE), BF16),
            dma(SIDE),
            dma(SIDE),
        ],
        layers, hidden, query, key, value, gain, query_w, side_w, out_w, up, cosine, sine,
    )


def retreat(
    turn, layers, ending, gradient, hidden, gain, kept, back, old,
    query_w, side_w, out_w, up, cosine, sine,
):
    width, columns = query_w.shape
    planes = layers.shape[0]
    query, key, value, side, piece = kept
    return call(
        functools.partial(retreat_kernel, turn), 20 + turn, "s" + "v" * 13 + "aaa" + "vvv",
        [
            shaped((ROWS, width)),
            shaped((TOKENS, columns)),
            shaped(piece.shape),
            shaped((ADAPTER_RANK, TOKENS), F32),
            shaped((ADAPTER_RANK, columns), F32),
        ],
        [
            *scatter_scratch(width),
            *gather_scratch(width),
            pltpu.VMEM((width, columns), BF16),
            dma(SCATTER_CHUNKS),
            pltpu.VMEM((HEAD_SIZE, width), BF16),
            dma(SCATTER_CHUNKS),
            pltpu.VMEM((columns, width), BF16),
            dma(GATHER_CHUNKS),
            pltpu.VMEM((TOKENS, columns), BF16),
            pltpu.VMEM((TOKENS, 2 * HEAD_SIZE), BF16),
            pltpu.VMEM((TOKENS, HEAD_SIZE), BF16),
            pltpu.VMEM((2, SIDE, HALF, HEAD_SIZE), BF16),
            dma(SIDE),
            dma(SIDE),
            pltpu.VMEM((planes, ROWS, width), BF16),
            dma(SCATTER_CHUNKS, 4),
            dma(SCATTER_CHUNKS, 4),
            pltpu.VMEM((planes, ROWS, 2 * HEAD_SIZE), F32),
            dma(4),
            dma(4),
            pltpu.VMEM((TOKENS, columns), F32),
        ],
        layers, ending, gradient, hidden, gain, *kept[:4], back, piece, *old,
        query_w, side_w, out_w, up, cosine, sine,
    )


def end(job, layers, kept, back, old, up, cosine, sine, replicas):
    query, key, value, side, piece = kept
    columns, width = query.shape[1], piece.shape[1]
    box = (replicas, ADAPTER_RANK, columns + width + ADAPTER_JOBS * ADAPTER_RANK)
    return call(
        end_kernel, 4, "ss" + "v" * 12,
        [shaped(box)],
        [
            pltpu.VMEM((TOKENS, columns), BF16),
            pltpu.VMEM((SIDE, ADAPTER_RANK, TOKENS), F32),
            pltpu.VMEM((SIDE, ADAPTER_RANK, TOKENS), F32),
            dma(2, SIDE),
            dma(2, SIDE),
            pltpu.VMEM(box, BF16),
            pltpu.SemaphoreType.DMA,
            pltpu.SemaphoreType.DMA,
        ],
        job, layers, *kept[:4], back, piece, *old, up, cosine, sine,
    )[0]


def placed_kernel(box, down_out, up_out):
    columns, width = up_out.shape[1], down_out.shape[0]
    spots = box[:, columns + width :]
    down_out[...] = dot(box[:, columns : columns + width], spots, ((0,), (0,)))
    up_out[...] = dot(spots, box[:, :columns], ((0,), (0,)))


def placed(box, columns, width):
    jobs = ADAPTER_JOBS * ADAPTER_RANK
    return pl.pallas_call(
        placed_kernel,
        out_shape=(shaped((width, jobs), F32), shaped((jobs, columns), F32)),
        in_specs=[INSIDE],
        out_specs=(INSIDE, INSIDE),
    )(box)


def turn_tables():
    exponent = np.arange(HEAD_SIZE // 2) * (2.0 / HEAD_SIZE)
    angles = np.arange(TOKENS)[:, None] * np.exp(-math.log(10000.0) * exponent)[None, :]
    cosine, sine = np.cos(angles), np.sin(angles)
    return (
        jnp.asarray(np.concatenate([cosine, cosine], axis=1), F32),
        jnp.asarray(np.concatenate([-sine, sine], axis=1), F32),
    )


def shards(
    tokens,
    cotangent,
    sequence_job,
    section_layer_list,
    section_norm_gain,
    query_matrix,
    key_matrix,
    value_matrix,
    output_matrix,
    adapter_down_all,
    adapter_up_all,
):
    segments = lax.axis_size(SEG)
    replicas = lax.axis_size("dp")
    gain = section_norm_gain
    query_w = query_matrix[0]
    out_w = output_matrix[0]
    width, columns = query_w.shape
    piece_width = adapter_down_all.shape[1]
    cosine, sine = turn_tables()
    turns = max(segments - 1, 1)
    layers = section_layer_list
    count = jnp.sum((layers > 0).astype(jnp.int32))
    ending = cotangent[0]

    def first(only):
        return lambda: start(
            only, sequence_job, layers, tokens[0], ending, gain, query_w, key_matrix[0].T,
            value_matrix[0].T, out_w, adapter_down_all[0], adapter_up_all[0], cosine, sine,
        )

    if turns == 1:
        *kept, back_ending, side_w, up = first(True)()
    else:
        *kept, back_ending, side_w, up = lax.cond(count > 1, first(False), first(True))
    nothing = (
        jnp.zeros((TOKENS, piece_width), BF16),
        jnp.zeros((ADAPTER_RANK, TOKENS), F32),
        jnp.zeros((ADAPTER_RANK, columns), F32),
    )

    def beyond(turn, hidden, kept):
        def onward(operand):
            hidden, kept = operand
            hidden, *kept = advance(
                turn, layers, hidden, *kept[:3], gain, query_w, side_w, out_w, up, cosine, sine
            )
            gradient, back, old = beyond(turn + 1, hidden, kept)
            gradient, back, *old = retreat(
                turn + 1, layers, ending, gradient, hidden, gain, kept, back, old,
                query_w, side_w, out_w, up, cosine, sine,
            )
            return gradient, back, tuple(old)

        nowhere = (jnp.zeros((ROWS, width), BF16), back_ending, nothing)
        if turn + 1 == turns:
            return nowhere
        return lax.cond(count > turn + 1, onward, lambda operand: nowhere, (hidden, tuple(kept)))

    _, back, old = beyond(0, tokens[0], kept)
    box = end(sequence_job, layers, kept, back, old, up, cosine, sine, replicas)
    grad_down, grad_up = placed(box.reshape(replicas * ADAPTER_RANK, box.shape[2]), columns, piece_width)
    return (grad_down[None], grad_up[None])


def solution(mesh):
    split = Mesh(
        mesh.devices.reshape(mesh.shape["segment"], SIDE, SIDE, mesh.shape["dp"]),
        (SEG, Z, X, "dp"),
    )
    return jax.shard_map(
        shards,
        mesh=split,
        in_specs=(
            P("dp", TENSOR, None),
            P("dp", TENSOR, None),
            P("dp"),
            P(),
            P(SEG, None),
            P(SEG, None, TENSOR),
            P(SEG, None, TENSOR),
            P(SEG, None, TENSOR),
            P(SEG, TENSOR, None),
            P(SEG, TENSOR, None),
            P(SEG, None, TENSOR),
        ),
        out_specs=(P(SEG, TENSOR, None), P(SEG, None, TENSOR)),
        check_vma=False,
    )
```

```python
import functools
import math

import jax
import jax.numpy as jnp
import numpy as np
from jax import lax
from jax.experimental import pallas as pl
from jax.experimental.pallas import tpu as pltpu
from jax.sharding import Mesh
from jax.sharding import PartitionSpec as P

HEAD_SIZE = 128
ADAPTER_RANK = 16
ADAPTER_JOBS = 32
ADAPTER_SCALE = 2.0
EPSILON = 1e-05
SIDE = 4
ROWS = 16
TOKENS = SIDE * SIDE * ROWS
KV_PART = 32
LOW_LANE = 2 * KV_PART
GATHER_CHUNKS = 4
SCATTER_PARTS = (8, 8, 8, 8)
SCATTER_CHUNKS = len(SCATTER_PARTS)
SEG, Z, X = "segment", "tensor_0", "tensor_1"
TENSOR = (Z, X)
MESH = pl.DeviceIdType.MESH
BF16, F32 = jnp.bfloat16, jnp.float32
VMEM_LIMIT = 60 * 1024 * 1024


def dot(a, b, dims=((1,), (0,))):
    return lax.dot_general(a, b, (dims, ((), ())), preferred_element_type=F32)


def step_of(axis, offset):
    return lax.rem(lax.axis_index(axis) + (offset + SIDE), SIDE)


def remote(src, dst, send_sem, recv_sem, axis, offset):
    return pltpu.make_async_remote_copy(
        src_ref=src,
        dst_ref=dst,
        send_sem=send_sem,
        recv_sem=recv_sem,
        device_id={axis: step_of(axis, offset)},
        device_id_type=MESH,
    )


NEAR = [(Z, 1), (Z, -1), (X, 1), (X, -1)]


def greet(partners, planes):
    barrier = pltpu.get_barrier_semaphore()
    for axis, offset in partners:
        pl.semaphore_signal(
            barrier, inc=1, device_id={axis: step_of(axis, offset)}, device_id_type=MESH
        )
    mine = lax.axis_index(SEG)
    for distance in range(1, planes):
        there = lax.rem(mine + distance, planes)
        pl.semaphore_signal(barrier, inc=1, device_id={SEG: there}, device_id_type=MESH)


def await_greeting(partners, planes):
    pl.semaphore_wait(pltpu.get_barrier_semaphore(), len(partners) + planes - 1)


def order_of(chunk):
    return (Z, X) if chunk % 2 == 0 else (X, Z)


def blocks(ref, axis, place, columns):
    if axis == Z:
        return ref.at[place, :, :, columns]
    return ref.at[:, place, :, columns]


def gather_stages(held, start, size, order, send, recv, started):
    first, second = order
    me = {Z: lax.axis_index(Z), X: lax.axis_index(X)}
    whole = pl.ds(start, size)
    halves = (pl.ds(start, size // 2), pl.ds(start + size // 2, size // 2))

    def go(slot, src, axis, offset):
        copy = remote(src, src, send.at[slot], recv.at[slot], axis, offset)
        copy.start()
        started.append(copy)

    def arrived(slot, where, axis, offset):
        remote(where, where, send.at[slot], recv.at[slot], axis, offset).wait_recv()

    def one(offset, columns):
        place = step_of(first, offset)
        z, x = (place, me[X]) if first == Z else (me[Z], place)
        return held.at[z, x, :, columns]

    def group(offset, columns):
        return blocks(held, second, step_of(second, offset), columns)

    def stage0():
        go(0, one(0, whole), first, 1)
        go(1, one(0, whole), first, -1)

    def stage1():
        arrived(0, one(-1, whole), first, 1)
        go(2, one(-1, halves[0]), first, 1)
        arrived(1, one(1, whole), first, -1)
        go(3, one(1, halves[1]), first, -1)

    def stage2():
        arrived(2, one(2, halves[0]), first, 1)
        arrived(3, one(2, halves[1]), first, -1)
        go(4, group(0, whole), second, 1)
        go(5, group(0, whole), second, -1)

    def stage3():
        arrived(4, group(-1, whole), second, 1)
        go(6, group(-1, halves[0]), second, 1)
        arrived(5, group(1, whole), second, -1)
        go(7, group(1, halves[1]), second, -1)

    def stage4():
        arrived(6, group(2, halves[0]), second, 1)
        arrived(7, group(2, halves[1]), second, -1)

    return stage0, stage1, stage2, stage3, stage4


def gather_chunks(held, send, recv, started):
    size = held.shape[-1] // GATHER_CHUNKS
    return [
        gather_stages(
            held, chunk * size, size, order_of(chunk), send.at[chunk], recv.at[chunk], started
        )
        for chunk in range(GATHER_CHUNKS)
    ]


def gather_scratch(width, chunks=GATHER_CHUNKS):
    return [
        pltpu.VMEM((SIDE, SIDE, ROWS, width), BF16),
        pltpu.SemaphoreType.DMA((chunks, 8)),
        pltpu.SemaphoreType.DMA((chunks, 8)),
    ]


def even_spans(width):
    size = width // GATHER_CHUNKS
    return [(chunk * size, size) for chunk in range(GATHER_CHUNKS)]


def load_columns(source, target, sem, parts):
    loads = []
    for chunk, part in enumerate(parts):
        at = pl.ds(*part)
        copy = pltpu.make_async_copy(source.at[:, at], target.at[:, at], sem.at[chunk])
        copy.start()
        loads.append(copy)
    return loads


def load_rows(source, target, sem, parts):
    loads = []
    for chunk, part in enumerate(parts):
        at = pl.ds(*part)
        copy = pltpu.make_async_copy(source.at[at], target.at[at], sem.at[chunk])
        copy.start()
        loads.append(copy)
    return loads


def inverse_of(stream):
    return lax.rsqrt(jnp.mean(stream * stream, axis=-1, keepdims=True) + EPSILON)


def turn_of(layers, turn):
    owner, count = jnp.int32(0), jnp.int32(0)
    for section in range(layers.shape[0]):
        here = (layers[section] > 0).astype(jnp.int32)
        owner = jnp.where((here > 0) & (count == turn), section, owner)
        count += here
    return owner, owner == lax.axis_index(SEG), count


def over_tiles(first, extent, body):
    tile = min(512, extent)

    def step(i, carry):
        body(pl.multiple_of(first + i * tile, tile), tile)
        return carry

    lax.fori_loop(0, extent // tile, step, 0)


def rows_of(held, at, tile):
    return held[:, :, :, pl.ds(at, tile)].reshape(TOKENS, tile)


def spans(width):
    unit = width // sum(SCATTER_PARTS)
    starts = [unit * sum(SCATTER_PARTS[:chunk]) for chunk in range(SCATTER_CHUNKS)]
    return [(start, unit * part) for start, part in zip(starts, SCATTER_PARTS)]


def scatter_sum(part, mid, land1, land2, land3, land4, send, recv, term, finish, started):
    chunk_spans = spans(part.shape[-1])
    me = {Z: lax.axis_index(Z), X: lax.axis_index(X)}

    def columns(chunk, part_of=None):
        start, size = chunk_spans[chunk]
        if part_of is None:
            return pl.ds(start, size)
        return pl.ds(start + part_of * (size // 2), size // 2)

    def whole(ref, chunk, *places):
        index = (chunk, *places, *[slice(None)] * (len(ref.shape) - 2 - len(places)))
        return ref.at[(*index, pl.ds(0, chunk_spans[chunk][1]))]

    def halved(ref, chunk, *places, at=0):
        half = chunk_spans[chunk][1] // 2
        index = (chunk, *places, *[slice(None)] * (len(ref.shape) - 2 - len(places)))
        return ref.at[(*index, pl.ds(at * half, half))]

    def go(chunk, slot, src, dst, axis, offset):
        copy = remote(src, dst, send.at[chunk, slot], recv.at[chunk, slot], axis, offset)
        copy.start()
        started.append(copy)

    def arrived(chunk, slot, where, axis, offset):
        remote(where, where, send.at[chunk, slot], recv.at[chunk, slot], axis, offset).wait_recv()

    def add_into(target, landed):
        target[...] = (target[...].astype(F32) + landed[...].astype(F32)).astype(BF16)

    def stage0(chunk):
        first, _ = order_of(chunk)
        start, size = chunk_spans[chunk]
        part[:, :, :, columns(chunk)] = (
            term(chunk, start, size).astype(BF16).reshape(SIDE, SIDE, ROWS, size)
        )
        far = step_of(first, 2)
        go(chunk, 0, blocks(part, first, far, columns(chunk, 0)), halved(land1, chunk, 0), first, 1)
        go(chunk, 1, blocks(part, first, far, columns(chunk, 1)), halved(land1, chunk, 1), first, -1)

    def stage1(chunk):
        first, _ = order_of(chunk)
        for slot, offset in ((0, 1), (1, -1)):
            arrived(chunk, slot, halved(land1, chunk, slot), first, offset)
            near = step_of(first, offset)
            add_into(blocks(part, first, near, columns(chunk, slot)), halved(land1, chunk, slot))
            go(
                chunk,
                2 + slot,
                blocks(part, first, near, columns(chunk)),
                whole(land2, chunk, slot),
                first,
                offset,
            )

    def stage2(chunk):
        first, second = order_of(chunk)
        arrived(chunk, 2, whole(land2, chunk, 0), first, 1)
        arrived(chunk, 3, whole(land2, chunk, 1), first, -1)
        own = blocks(part, first, me[first], columns(chunk))
        whole(mid, chunk)[...] = (
            own[...].astype(F32) + whole(land2, chunk, 0)[...].astype(F32) + whole(land2, chunk, 1)[...].astype(F32)
        ).astype(BF16)
        far = step_of(second, 2)
        go(chunk, 4, whole(mid, chunk, far), whole(land3, chunk, 0), second, 2)
        for slot, offset in ((0, 1), (1, -1)):
            near = step_of(second, offset)
            go(chunk, 6 + slot, whole(mid, chunk, near), whole(land4, chunk, slot), second, offset)

    def stage3(chunk):
        _, second = order_of(chunk)
        arrived(chunk, 6, whole(land4, chunk, 0), second, 1)
        arrived(chunk, 7, whole(land4, chunk, 1), second, -1)
        arrived(chunk, 4, whole(land3, chunk, 0), second, 2)
        total = (
            whole(mid, chunk, me[second])[...].astype(F32)
            + whole(land4, chunk, 0)[...].astype(F32)
            + whole(land4, chunk, 1)[...].astype(F32)
            + whole(land3, chunk, 0)[...].astype(F32)
        )
        finish(chunk, *chunk_spans[chunk], total)

    return stage0, stage1, stage2, stage3


def sum_and_spread(sums, spreads, summed=None, later=None):
    pairs = [(chunk, chunk + 1) for chunk in range(0, SCATTER_CHUNKS, 2)]
    for turn in range(len(pairs) + len(sums) - 1):
        for stage in range(len(sums)):
            pair = turn - stage
            if 0 <= pair < len(pairs):
                for chunk in pairs[pair]:
                    sums[stage](chunk)
                if stage == len(sums) - 1:
                    for chunk in pairs[pair]:
                        spreads[chunk][0]()
        if turn == 1 and later is not None:
            later()
    if summed is not None:
        summed()
    for spread in spreads:
        spread[1]()


def scatter_scratch(width):
    size = max(size for _, size in spans(width))
    return [
        pltpu.VMEM((SIDE, SIDE, ROWS, width), BF16),
        pltpu.VMEM((SCATTER_CHUNKS, SIDE, ROWS, size), BF16),
        pltpu.VMEM((SCATTER_CHUNKS, 2, SIDE, ROWS, size // 2), BF16),
        pltpu.VMEM((SCATTER_CHUNKS, 2, SIDE, ROWS, size), BF16),
        pltpu.VMEM((SCATTER_CHUNKS, 1, ROWS, size), BF16),
        pltpu.VMEM((SCATTER_CHUNKS, 2, ROWS, size), BF16),
        pltpu.SemaphoreType.DMA((SCATTER_CHUNKS, 8)),
        pltpu.SemaphoreType.DMA((SCATTER_CHUNKS, 8)),
    ]


def far_first(count):
    return sorted(range(1, count), key=lambda distance: -min(distance, count - distance))


def plane_step(planes, offset):
    return lax.rem(lax.axis_index(SEG) + (planes + offset), planes)


def spread_stages(all_planes, start, size, send, recv, started):
    planes = all_planes.shape[0]
    columns = pl.ds(start, size)

    def copy_of(origin, distance):
        rows = all_planes.at[plane_step(planes, origin), :, columns]
        return pltpu.make_async_remote_copy(
            src_ref=rows,
            dst_ref=rows,
            send_sem=send.at[distance],
            recv_sem=recv.at[distance],
            device_id={SEG: plane_step(planes, distance)},
            device_id_type=MESH,
        )

    def stage0():
        for distance in far_first(planes):
            copy = copy_of(0, distance)
            copy.start()
            started.append(copy)

    def stage1():
        for distance in range(1, planes):
            copy_of(-distance, distance).wait_recv()

    return stage0, stage1


def spread_chunks(all_planes, send, recv, started):
    return [
        spread_stages(all_planes, start, size, send.at[chunk], recv.at[chunk], started)
        for chunk, (start, size) in enumerate(spans(all_planes.shape[-1]))
    ]


def turned(value, cosine, sine):
    return value * cosine + pltpu.roll(value, HEAD_SIZE // 2, 1) * sine


def turned_back(value, cosine, sine):
    return value * cosine + pltpu.roll(value * sine, HEAD_SIZE // 2, 1)


def probabilities(query, key):
    scores = dot(query, key, ((1,), (1,))) * (1.0 / math.sqrt(HEAD_SIZE))
    row = lax.broadcasted_iota(jnp.int32, scores.shape, 0)
    column = lax.broadcasted_iota(jnp.int32, scores.shape, 1)
    weights = jnp.exp(jnp.where(row >= column, scores, -1e30))
    return weights / jnp.sum(weights, axis=-1, keepdims=True)


def trade_start(trade, send, recv, source, target):
    copies = []
    for distance in far_first(SIDE):
        copy = remote(
            source(distance), target(distance), send.at[distance], recv.at[distance], X, distance
        )
        copy.start()
        copies.append(copy)
    return copies


def project_sums(held, first, extent, query_w, side_w, query_sum, side_sum):
    def body(at, tile):
        rows = rows_of(held, at, tile)
        query_sum[...] += dot(rows, query_w[pl.ds(at, tile), :])
        side_sum[...] += dot(rows, side_w[:, pl.ds(at, tile)], ((1,), (1,)))

    over_tiles(first, extent, body)


HALF = TOKENS // 2


def two_halves(first, second):
    lane = lax.broadcasted_iota(jnp.int32, first.shape, 1)
    return jnp.where(lane < LOW_LANE, first, second)


def pick(half, place):
    shape = (HEAD_SIZE, 2 * HEAD_SIZE)
    row = lax.broadcasted_iota(jnp.int32, shape, 0) - half * LOW_LANE
    column = lax.broadcasted_iota(jnp.int32, shape, 1) - place * KV_PART
    keys = (row >= 0) & (row < KV_PART) & (column == row)
    values = (row >= KV_PART) & (row < LOW_LANE) & (column == row + HEAD_SIZE - KV_PART)
    return jnp.where(keys | values, 1.0, 0.0).astype(BF16)


def project_start(side_sum, trade, send, recv, side_out):
    mine = lax.axis_index(X)
    side = side_sum[...]
    side_out[...] = side.astype(BF16)
    trade[mine] = two_halves(side[:HALF], pltpu.roll(side[HALF:], LOW_LANE, 1)).astype(BF16)
    return trade_start(
        trade, send, recv, lambda distance: trade.at[mine], lambda distance: trade.at[mine]
    )


def project_local(held, query_sum, side_out, up, cosine, sine, query_out, piece_out):
    query = query_sum[...] + ADAPTER_SCALE * dot(side_out[...], up[...])
    for head in range(query.shape[1] // HEAD_SIZE):
        lanes = slice(head * HEAD_SIZE, (head + 1) * HEAD_SIZE)
        query_out[:, lanes] = turned(query[:, lanes], cosine[...], sine[...]).astype(BF16)
    piece = held.shape[-1] // (SIDE * SIDE)
    first = (lax.axis_index(Z) * SIDE + lax.axis_index(X)) * piece
    piece_out[...] = rows_of(held, pl.multiple_of(first, piece), piece)


def project_end(trade, send, recv, copies, cosine, sine, key_out, value_out):
    for distance in range(1, SIDE):
        there = trade.at[step_of(X, -distance)]
        remote(there, there, send.at[distance], recv.at[distance], X, distance).wait_recv()
    for copy in copies:
        copy.wait_send()
    for half in range(2):
        rows = slice(half * HALF, (half + 1) * HALF)
        both = dot(trade[0], pick(half, 0))
        for place in range(1, SIDE):
            both += dot(trade[place], pick(half, place))
        key_out[rows] = turned(both[:, :HEAD_SIZE], cosine[rows], sine[rows]).astype(BF16)
        value_out[rows] = both[:, HEAD_SIZE:].astype(BF16)


def back_sums(held, first, extent, out_w, back_sum):
    def body(at, tile):
        back_sum[...] += dot(rows_of(held, at, tile), out_w[:, pl.ds(at, tile)], ((1,), (1,)))

    over_tiles(first, extent, body)


def start_kernel(
    only, job, layers, hidden, ending, gain, query_hbm, key_hbm, value_hbm, out_hbm, down, up_table, cosine, sine,
    query_out, key_out, value_out, side_out, piece_out, back_out, side_w, up_out,
    held, send, recv, held_down, send_down, recv_down,
    query_w, q_sem, s_sem, out_w, o_sem, query_sum, side_sum, back_sum, trade, trade_send, trade_recv,
    *second,
):
    greet(NEAR + [(X, 2), (Z, 2)], 1)
    size = held.shape[-1] // GATHER_CHUNKS
    narrow = [
        pltpu.make_async_copy(key_hbm, side_w.at[pl.ds(0, KV_PART)], s_sem.at[0]),
        pltpu.make_async_copy(value_hbm, side_w.at[pl.ds(KV_PART, KV_PART)], s_sem.at[1]),
    ]
    for copy in narrow:
        copy.start()
    query_loads = load_rows(query_hbm, query_w, q_sem, even_spans(held.shape[-1]))
    out_loads = load_columns(out_hbm, out_w, o_sem, even_spans(held.shape[-1]))
    z, x = lax.axis_index(Z), lax.axis_index(X)
    stream = hidden[...].astype(F32)
    normed = stream * inverse_of(stream) * gain[...].astype(F32)
    if only:
        held_back, send_back, recv_back = second
        held_back[z, x] = ending[...]
    else:
        _, mine_here, _ = turn_of(layers, 0)
        normed = jnp.where(mine_here, normed, ending[...].astype(F32))
    held[z, x] = normed.astype(BF16)
    tables = (ADAPTER_RANK, down.shape[1])
    picked = (
        lax.broadcasted_iota(jnp.int32, tables, 1)
        == lax.broadcasted_iota(jnp.int32, tables, 0) + job[0] * ADAPTER_RANK
    ).astype(BF16)
    held_down[z, x] = dot(picked, down[...], ((1,), (1,))).astype(BF16)
    await_greeting(NEAR + [(X, 2), (Z, 2)], 1)
    started = []
    first = gather_stages(
        held_down, 0, held_down.shape[-1], (Z, X), send_down.at[0], recv_down.at[0], started
    )
    ahead = gather_chunks(held, send, recv, started)
    behind = gather_chunks(held_back, send_back, recv_back, started) if only else []
    for chunk in [first, *ahead, *behind]:
        chunk[0]()
    up_out[...] = jnp.zeros_like(up_out)
    up_out[pl.ds(LOW_LANE, ADAPTER_RANK), :] = dot(picked, up_table[...]).astype(BF16)
    tail = HEAD_SIZE - LOW_LANE - ADAPTER_RANK
    side_w[pl.ds(LOW_LANE + ADAPTER_RANK, tail), :] = jnp.zeros((tail, side_w.shape[1]), BF16)
    query_sum[...] = jnp.zeros_like(query_sum)
    side_sum[...] = jnp.zeros_like(side_sum)
    back_sum[...] = jnp.zeros_like(back_sum)
    for chunk in [first, *ahead, *behind]:
        chunk[1]()
    for chunk in [first, *ahead]:
        chunk[2]()
    for chunk in [first, *ahead]:
        chunk[3]()
    for chunk in behind:
        chunk[2]()
    first[4]()
    piece = held_down.shape[-1]
    for place in range(SIDE * SIDE):
        side_w[pl.ds(LOW_LANE, ADAPTER_RANK), pl.ds(place * piece, piece)] = held_down[
            place // SIDE, place % SIDE
        ]
    for copy in narrow:
        copy.wait()
    for place, chunk in enumerate(ahead):
        chunk[4]()
        query_loads[place].wait()
        project_sums(held, place * size, size, query_w, side_w, query_sum, side_sum)
    copies = project_start(side_sum, trade, trade_send, trade_recv, side_out)
    if not only:
        for place in range(GATHER_CHUNKS):
            out_loads[place].wait()
            back_sums(held, place * size, size, out_w, back_sum)
    for chunk in behind:
        chunk[3]()
    project_local(held, query_sum, side_out, up_out, cosine, sine, query_out, piece_out)
    project_end(trade, trade_send, trade_recv, copies, cosine, sine, key_out, value_out)
    for place, chunk in enumerate(behind):
        chunk[4]()
        out_loads[place].wait()
        back_sums(held_back, place * size, size, out_w, back_sum)
    back_out[...] = back_sum[...].astype(BF16)
    for copy in started:
        copy.wait_send()


def advance_kernel(
    turn, layers, hidden, query, key, value, gain, query_hbm, side_hbm, out_hbm, up, cosine, sine,
    hidden_out, query_out, key_out, value_out, side_out, piece_out,
    part, mid, land1, land2, land3, land4, send, recv,
    held, send_held, recv_held,
    query_w, q_sem, side_w, s_sem, out_w, o_sem, attended, planes, p_send, p_recv,
    query_sum, side_sum, trade, trade_send, trade_recv,
):
    width = part.shape[-1]
    greet(NEAR + [(X, 2), (Z, 2)], planes.shape[0])
    owner, _, _ = turn_of(layers, turn)
    out_loads = load_columns(out_hbm, out_w, o_sem, spans(part.shape[-1]))
    query_loads, side_loads = [], []

    def later():
        query_loads.extend(load_rows(query_hbm, query_w, q_sem, even_spans(held.shape[-1])))
        side_loads.extend(load_columns(side_hbm, side_w, s_sem, even_spans(held.shape[-1])))

    for head in range(query.shape[1] // HEAD_SIZE):
        lanes = slice(head * HEAD_SIZE, (head + 1) * HEAD_SIZE)
        weights = probabilities(query[:, lanes], key[...]).astype(BF16)
        attended[:, lanes] = dot(weights, value[...]).astype(BF16)
    query_sum[...] = jnp.zeros_like(query_sum)
    side_sum[...] = jnp.zeros_like(side_sum)
    await_greeting(NEAR + [(X, 2), (Z, 2)], planes.shape[0])
    mine = lax.axis_index(SEG)
    started = []

    def term(chunk, first, extent):
        out_loads[chunk].wait()
        return dot(attended[...], out_w[:, pl.ds(first, extent)])

    def finish(chunk, first, extent, total):
        cols = pl.ds(first, extent)
        planes[mine, :, cols] = (hidden[:, cols].astype(F32) + total).astype(BF16)

    sum_and_spread(
        scatter_sum(part, mid, land1, land2, land3, land4, send, recv, term, finish, started),
        spread_chunks(planes, p_send, p_recv, started),
        later=later,
    )
    following = planes[owner]
    hidden_out[...] = following
    stream = following.astype(F32)
    held[lax.axis_index(Z), lax.axis_index(X)] = (
        stream * inverse_of(stream) * gain[...].astype(F32)
    ).astype(BF16)
    ahead = gather_chunks(held, send_held, recv_held, started)
    for stage in range(4):
        for chunk in ahead:
            chunk[stage]()
    size = width // GATHER_CHUNKS
    for place, chunk in enumerate(ahead):
        chunk[4]()
        query_loads[place].wait()
        side_loads[place].wait()
        project_sums(held, place * size, size, query_w, side_w, query_sum, side_sum)
    copies = project_start(side_sum, trade, trade_send, trade_recv, side_out)
    project_local(held, query_sum, side_out, up, cosine, sine, query_out, piece_out)
    project_end(trade, trade_send, trade_recv, copies, cosine, sine, key_out, value_out)
    for copy in started:
        copy.wait_send()


def attention_reverse(query, key, value, back, cosine, sine, query_grad_ref, pair_grad_ref=None):
    scale = 1.0 / math.sqrt(HEAD_SIZE)
    key_grad = jnp.zeros((TOKENS, HEAD_SIZE), F32)
    value_grad = jnp.zeros((TOKENS, HEAD_SIZE), F32)
    for head in range(query.shape[1] // HEAD_SIZE):
        lanes = slice(head * HEAD_SIZE, (head + 1) * HEAD_SIZE)
        weights = probabilities(query[:, lanes], key[...])
        out_grad = back[:, lanes]
        weight_grad = dot(out_grad, value[...], ((1,), (1,)))
        mean = jnp.sum(weight_grad * weights, axis=-1, keepdims=True)
        score_grad = (weights * (weight_grad - mean) * scale).astype(BF16)
        query_grad = turned_back(dot(score_grad, key[...]), cosine[...], sine[...])
        query_grad_ref[:, lanes] = query_grad.astype(BF16)
        if pair_grad_ref is not None:
            value_grad += dot(weights.astype(BF16), out_grad, ((0,), (0,)))
            key_grad += dot(score_grad, query[:, lanes], ((0,), (0,)))
    if pair_grad_ref is not None:
        pair_grad_ref[:, :HEAD_SIZE] = turned_back(key_grad, cosine[...], sine[...]).astype(BF16)
        pair_grad_ref[:, HEAD_SIZE:] = value_grad.astype(BF16)


LOW_ROWS = slice(LOW_LANE, LOW_LANE + ADAPTER_RANK)


def adapter_shares(query_grad, side, up):
    low = ADAPTER_SCALE * dot(up, query_grad, ((1,), (1,)))
    grad_up = ADAPTER_SCALE * dot(side, query_grad, ((0,), (0,)))
    return low[LOW_ROWS], grad_up[LOW_ROWS]


def retreat_kernel(
    turn, layers, ending, gradient, hidden, gain, query, key, value, side, back, piece,
    old_piece, old_low, old_up, query_hbm, side_hbm, out_hbm, up, cosine, sine,
    gradient_out, back_out, piece_out, low_out, up_out,
    part, mid, land1, land2, land3, land4, send, recv,
    held, send_held, recv_held,
    query_w, q_sem, side_w, s_sem, out_w, o_sem, query_grad, pair_grad, side_grad,
    trade, trade_send, trade_recv, planes, p_send, p_recv, means, m_send, m_recv, back_sum,
):
    width = part.shape[-1]
    greet(NEAR + [(X, 2), (Z, 2)], planes.shape[0])
    query_loads = load_rows(query_hbm, query_w, q_sem, spans(part.shape[-1]))
    side_loads = load_columns(side_hbm, side_w, s_sem, spans(part.shape[-1]))
    out_loads = []

    def later():
        out_loads.extend(load_columns(out_hbm, out_w, o_sem, even_spans(held.shape[-1])))

    attention_reverse(query, key, value, back, cosine, sine, query_grad, pair_grad)
    for place in range(SIDE):
        trade[0, place] = (
            dot(pair_grad[:HALF], pick(0, place), ((1,), (1,)))
            + dot(pair_grad[HALF:], pick(1, place), ((1,), (1,)))
        ).astype(BF16)
    await_greeting(NEAR + [(X, 2), (Z, 2)], planes.shape[0])
    copies = trade_start(
        trade,
        trade_send,
        trade_recv,
        lambda distance: trade.at[0, step_of(X, distance)],
        lambda distance: trade.at[1, distance],
    )
    owner, mine_here, count = turn_of(layers, turn)
    low, grad_up = adapter_shares(query_grad[...], side[...], up[...])
    low_out[...] = jnp.where(mine_here, low, old_low[...])
    up_out[...] = jnp.where(mine_here, grad_up, old_up[...])
    piece_out[...] = jnp.where(mine_here, piece[...].astype(F32), old_piece[...].astype(F32)).astype(BF16)
    back_sum[...] = jnp.zeros_like(back_sum)
    stream = hidden[...].astype(F32)
    inverse = inverse_of(stream)
    total = trade[0, lax.axis_index(X)].astype(F32)
    for distance in range(1, SIDE):
        there = trade.at[1, distance]
        remote(there, there, trade_send.at[distance], trade_recv.at[distance], X, distance).wait_recv()
        total += trade[1, distance].astype(F32)
    wide_low = ADAPTER_SCALE * dot(query_grad[...], up[...], ((1,), (1,)))
    side_grad[:HALF] = two_halves(total, wide_low[:HALF]).astype(BF16)
    side_grad[HALF:] = two_halves(pltpu.roll(total, LOW_LANE, 1), wide_low[HALF:]).astype(BF16)
    mine = lax.axis_index(SEG)
    started = []
    sums = []

    def term(chunk, first, extent):
        query_loads[chunk].wait()
        side_loads[chunk].wait()
        at = pl.ds(first, extent)
        return dot(query_grad[...], query_w[at, :], ((1,), (1,))) + dot(side_grad[...], side_w[:, at])

    def finish(chunk, first, extent, total):
        cols = pl.ds(first, extent)
        gained = total * gain[:, cols].astype(F32)
        sums.append(jnp.sum(gained * hidden[:, cols].astype(F32), axis=-1, keepdims=True))
        planes[mine, :, cols] = (inverse * gained).astype(BF16)

    mean_spread = spread_stages(means, 0, means.shape[-1], m_send, m_recv, started)

    def summed():
        means[mine] = jnp.broadcast_to(sum(sums) / width, means.shape[1:])
        mean_spread[0]()

    sum_and_spread(
        scatter_sum(part, mid, land1, land2, land3, land4, send, recv, term, finish, started),
        spread_chunks(planes, p_send, p_recv, started),
        summed,
        later,
    )
    for stage in mean_spread[1:]:
        stage()
    mean = means[owner][:, :1]
    before = jnp.where(count == turn + 1, ending[...].astype(F32), gradient[...].astype(F32))
    following = (
        before + planes[owner].astype(F32) - stream * (inverse * inverse * inverse * mean)
    ).astype(BF16)
    gradient_out[...] = following
    held[lax.axis_index(Z), lax.axis_index(X)] = following
    ahead = gather_chunks(held, send_held, recv_held, started)
    for stage in range(4):
        for chunk in ahead:
            chunk[stage]()
    size = width // GATHER_CHUNKS
    for place, chunk in enumerate(ahead):
        chunk[4]()
        out_loads[place].wait()
        back_sums(held, place * size, size, out_w, back_sum)
    back_out[...] = back_sum[...].astype(BF16)
    for copy in copies + started:
        copy.wait_send()


def end_kernel(
    only, job, layers, query, key, value, side, back, piece, *rest
):
    if not only:
        old_piece, old_low, old_up, *rest = rest
    up, cosine, sine, box_out, query_grad, lows_z, lows_x, low_send, low_recv, box, box_send, box_recv = rest
    replicas = box.shape[0]
    barrier = pltpu.get_barrier_semaphore()
    around = [(axis, distance) for axis in TENSOR for distance in range(1, SIDE)]
    for axis, offset in around:
        pl.semaphore_signal(
            barrier, inc=1, device_id={axis: step_of(axis, offset)}, device_id_type=MESH
        )
    replica = lax.axis_index("dp")
    if replicas > 1:
        pl.semaphore_signal(barrier, inc=1, device_id={"dp": 1 - replica}, device_id_type=MESH)
    attention_reverse(query, key, value, back, cosine, sine, query_grad)
    _, mine_here, _ = turn_of(layers, 0)
    low, grad_up = adapter_shares(query_grad[...], side[...], up[...])
    z, x = lax.axis_index(Z), lax.axis_index(X)
    lows_z[z] = low if only else jnp.where(mine_here, low, old_low[...])
    pl.semaphore_wait(barrier, len(around) + replicas - 1)
    columns, width = query.shape[1], piece.shape[1]
    copies = []

    def share(lows, axis, place, row):
        for distance in far_first(SIDE):
            copy = remote(
                lows.at[place], lows.at[place], low_send.at[row, distance], low_recv.at[row, distance],
                axis, distance,
            )
            copy.start()
            copies.append(copy)

    def shared(lows, axis, row):
        for distance in range(1, SIDE):
            there = lows.at[step_of(axis, -distance)]
            remote(
                there, there, low_send.at[row, distance], low_recv.at[row, distance], axis, distance
            ).wait_recv()
        return lows[0] + lows[1] + lows[2] + lows[3]

    share(lows_z, Z, z, 0)
    columns, width = query.shape[1], piece.shape[1]
    applied = jnp.int32(0)
    for section in range(layers.shape[0]):
        applied += jnp.where(section == lax.axis_index(SEG), layers[section], 0)
    active = applied > 0
    if not only:
        grad_up = jnp.where(mine_here, grad_up, old_up[...])
    box[replica, :, pl.ds(0, columns)] = jnp.where(active, grad_up, 0.0).astype(BF16)
    spot = box.shape[2] - columns - width
    jobs = (ADAPTER_RANK, spot)
    box[replica, :, pl.ds(columns + width, spot)] = (
        lax.broadcasted_iota(jnp.int32, jobs, 1)
        == lax.broadcasted_iota(jnp.int32, jobs, 0) + job[0] * ADAPTER_RANK
    ).astype(BF16)
    chosen = piece[...]
    if not only:
        chosen = jnp.where(mine_here, chosen.astype(F32), old_piece[...].astype(F32)).astype(BF16)
    lows_x[x] = shared(lows_z, Z, 0)
    share(lows_x, X, x, 1)
    low = shared(lows_x, X, 1).astype(BF16)
    box[replica, :, pl.ds(columns, width)] = jnp.where(active, dot(low, chosen), 0.0).astype(BF16)
    if replicas > 1:
        copy = pltpu.make_async_remote_copy(
            src_ref=box.at[replica],
            dst_ref=box.at[replica],
            send_sem=box_send,
            recv_sem=box_recv,
            device_id={"dp": 1 - replica},
            device_id_type=MESH,
        )
        copy.start()
        there = box.at[1 - replica]
        pltpu.make_async_remote_copy(
            src_ref=there,
            dst_ref=there,
            send_sem=box_send,
            recv_sem=box_recv,
            device_id={"dp": 1 - replica},
            device_id_type=MESH,
        ).wait_recv()
        copy.wait_send()
    for copy in copies:
        copy.wait_send()
    box_out[...] = box[...]


ANYWHERE = pl.BlockSpec(memory_space=pl.ANY)
SCALAR = pl.BlockSpec(memory_space=pltpu.SMEM)
INSIDE = pl.BlockSpec(memory_space=pltpu.VMEM)
SPECS = {"s": SCALAR, "a": ANYWHERE, "v": INSIDE}


def shaped(shape, dtype=BF16):
    return jax.ShapeDtypeStruct(shape, dtype)


def call(kernel, number, places, outputs, scratch, *operands):
    return pl.pallas_call(
        kernel,
        out_shape=tuple(outputs),
        in_specs=[SPECS[place] for place in places],
        out_specs=tuple(INSIDE for _ in outputs),
        scratch_shapes=scratch,
        compiler_params=pltpu.CompilerParams(
            collective_id=number, has_side_effects=True, vmem_limit_bytes=VMEM_LIMIT
        ),
        name=getattr(kernel, "func", kernel).__name__,
    )(*operands)


def dma(*shape):
    return pltpu.SemaphoreType.DMA(shape)


def projections(width, columns):
    return [
        shaped((TOKENS, columns)),
        shaped((TOKENS, HEAD_SIZE)),
        shaped((TOKENS, HEAD_SIZE)),
        shaped((TOKENS, HEAD_SIZE)),
        shaped((TOKENS, width // (SIDE * SIDE))),
    ]


def start(only, job, layers, hidden, ending, gain, query_w, key_w, value_w, out_w, down, up_table, cosine, sine):
    width, columns = query_w.shape
    return call(
        functools.partial(start_kernel, only), 1 + only, "ssvvv" + "aaaa" + "vvvv",
        [
            *projections(width, columns),
            shaped((TOKENS, columns)),
            shaped((HEAD_SIZE, width)),
            shaped((HEAD_SIZE, columns)),
        ],
        [
            *gather_scratch(width),
            *gather_scratch(down.shape[0], 1),
            pltpu.VMEM((width, columns), BF16),
            dma(GATHER_CHUNKS),
            dma(2),
            pltpu.VMEM((columns, width), BF16),
            dma(GATHER_CHUNKS),
            pltpu.VMEM((TOKENS, columns), F32),
            pltpu.VMEM((TOKENS, HEAD_SIZE), F32),
            pltpu.VMEM((TOKENS, columns), F32),
            pltpu.VMEM((SIDE, HALF, HEAD_SIZE), BF16),
            dma(SIDE),
            dma(SIDE),
            *(gather_scratch(width) if only else []),
        ],
        job, layers, hidden, ending, gain, query_w, key_w, value_w, out_w, down, up_table, cosine, sine,
    )


def advance(turn, layers, hidden, query, key, value, gain, query_w, side_w, out_w, up, cosine, sine):
    width, columns = query_w.shape
    planes = layers.shape[0]
    return call(
        functools.partial(advance_kernel, turn), 10 + turn, "svvvvv" + "aaa" + "vvv",
        [shaped((ROWS, width)), *projections(width, columns)],
        [
            *scatter_scratch(width),
            *gather_scratch(width),
            pltpu.VMEM((width, columns), BF16),
            dma(GATHER_CHUNKS),
            pltpu.VMEM((HEAD_SIZE, width), BF16),
            dma(GATHER_CHUNKS),
            pltpu.VMEM((columns, width), BF16),
            dma(SCATTER_CHUNKS),
            pltpu.VMEM((TOKENS, columns), BF16),
            pltpu.VMEM((planes, ROWS, width), BF16),
            dma(SCATTER_CHUNKS, 4),
            dma(SCATTER_CHUNKS, 4),
            pltpu.VMEM((TOKENS, columns), F32),
            pltpu.VMEM((TOKENS, HEAD_SIZE), F32),
            pltpu.VMEM((SIDE, HALF, HEAD_SIZE), BF16),
            dma(SIDE),
            dma(SIDE),
        ],
        layers, hidden, query, key, value, gain, query_w, side_w, out_w, up, cosine, sine,
    )


def retreat(
    turn, layers, ending, gradient, hidden, gain, kept, back, old,
    query_w, side_w, out_w, up, cosine, sine,
):
    width, columns = query_w.shape
    planes = layers.shape[0]
    query, key, value, side, piece = kept
    return call(
        functools.partial(retreat_kernel, turn), 20 + turn, "s" + "v" * 13 + "aaa" + "vvv",
        [
            shaped((ROWS, width)),
            shaped((TOKENS, columns)),
            shaped(piece.shape),
            shaped((ADAPTER_RANK, TOKENS), F32),
            shaped((ADAPTER_RANK, columns), F32),
        ],
        [
            *scatter_scratch(width),
            *gather_scratch(width),
            pltpu.VMEM((width, columns), BF16),
            dma(SCATTER_CHUNKS),
            pltpu.VMEM((HEAD_SIZE, width), BF16),
            dma(SCATTER_CHUNKS),
            pltpu.VMEM((columns, width), BF16),
            dma(GATHER_CHUNKS),
            pltpu.VMEM((TOKENS, columns), BF16),
            pltpu.VMEM((TOKENS, 2 * HEAD_SIZE), BF16),
            pltpu.VMEM((TOKENS, HEAD_SIZE), BF16),
            pltpu.VMEM((2, SIDE, HALF, HEAD_SIZE), BF16),
            dma(SIDE),
            dma(SIDE),
            pltpu.VMEM((planes, ROWS, width), BF16),
            dma(SCATTER_CHUNKS, 4),
            dma(SCATTER_CHUNKS, 4),
            pltpu.VMEM((planes, ROWS, 2 * HEAD_SIZE), F32),
            dma(4),
            dma(4),
            pltpu.VMEM((TOKENS, columns), F32),
        ],
        layers, ending, gradient, hidden, gain, *kept[:4], back, piece, *old,
        query_w, side_w, out_w, up, cosine, sine,
    )


def end(job, layers, kept, back, old, up, cosine, sine, replicas):
    query, key, value, side, piece = kept
    columns, width = query.shape[1], piece.shape[1]
    box = (replicas, ADAPTER_RANK, columns + width + ADAPTER_JOBS * ADAPTER_RANK)
    return call(
        functools.partial(end_kernel, not old), 4 if old else 5, "ss" + "v" * (9 + len(old)),
        [shaped(box)],
        [
            pltpu.VMEM((TOKENS, columns), BF16),
            pltpu.VMEM((SIDE, ADAPTER_RANK, TOKENS), F32),
            pltpu.VMEM((SIDE, ADAPTER_RANK, TOKENS), F32),
            dma(2, SIDE),
            dma(2, SIDE),
            pltpu.VMEM(box, BF16),
            pltpu.SemaphoreType.DMA,
            pltpu.SemaphoreType.DMA,
        ],
        job, layers, *kept[:4], back, piece, *old, up, cosine, sine,
    )[0]


def placed_kernel(box, down_out, up_out):
    columns, width = up_out.shape[1], down_out.shape[0]
    spots = box[:, columns + width :]
    down_out[...] = dot(box[:, columns : columns + width], spots, ((0,), (0,)))
    up_out[...] = dot(spots, box[:, :columns], ((0,), (0,)))


def placed(box, columns, width):
    jobs = ADAPTER_JOBS * ADAPTER_RANK
    return pl.pallas_call(
        placed_kernel,
        out_shape=(shaped((width, jobs), F32), shaped((jobs, columns), F32)),
        in_specs=[INSIDE],
        out_specs=(INSIDE, INSIDE),
    )(box)


def turn_tables():
    exponent = np.arange(HEAD_SIZE // 2) * (2.0 / HEAD_SIZE)
    angles = np.arange(TOKENS)[:, None] * np.exp(-math.log(10000.0) * exponent)[None, :]
    cosine, sine = np.cos(angles), np.sin(angles)
    return (
        jnp.asarray(np.concatenate([cosine, cosine], axis=1), F32),
        jnp.asarray(np.concatenate([-sine, sine], axis=1), F32),
    )


def shards(
    tokens,
    cotangent,
    sequence_job,
    section_layer_list,
    section_norm_gain,
    query_matrix,
    key_matrix,
    value_matrix,
    output_matrix,
    adapter_down_all,
    adapter_up_all,
):
    segments = lax.axis_size(SEG)
    replicas = lax.axis_size("dp")
    gain = section_norm_gain
    query_w = query_matrix[0]
    out_w = output_matrix[0]
    width, columns = query_w.shape
    piece_width = adapter_down_all.shape[1]
    cosine, sine = turn_tables()
    turns = max(segments - 1, 1)
    layers = section_layer_list
    count = jnp.sum((layers > 0).astype(jnp.int32))
    ending = cotangent[0]

    def first(only):
        return lambda: start(
            only, sequence_job, layers, tokens[0], ending, gain, query_w, key_matrix[0].T,
            value_matrix[0].T, out_w, adapter_down_all[0], adapter_up_all[0], cosine, sine,
        )

    nothing = (
        jnp.zeros((TOKENS, piece_width), BF16),
        jnp.zeros((ADAPTER_RANK, TOKENS), F32),
        jnp.zeros((ADAPTER_RANK, columns), F32),
    )

    def beyond(turn, hidden, kept, back_ending, side_w, up):
        def onward(operand):
            hidden, kept = operand
            hidden, *kept = advance(
                turn, layers, hidden, *kept[:3], gain, query_w, side_w, out_w, up, cosine, sine
            )
            gradient, back, old = beyond(turn + 1, hidden, kept, back_ending, side_w, up)
            gradient, back, *old = retreat(
                turn + 1, layers, ending, gradient, hidden, gain, kept, back, old,
                query_w, side_w, out_w, up, cosine, sine,
            )
            return gradient, back, tuple(old)

        if turn == 0:
            return onward((hidden, tuple(kept)))
        nowhere = (jnp.zeros((ROWS, width), BF16), back_ending, nothing)
        if turn + 1 == turns:
            return nowhere
        return lax.cond(count > turn + 1, onward, lambda operand: nowhere, (hidden, tuple(kept)))

    def several():
        *kept, back, side_w, up = first(False)()
        _, back, old = beyond(0, tokens[0], kept, back, side_w, up)
        return end(sequence_job, layers, kept, back, old, up, cosine, sine, replicas)

    def single():
        *kept, back, _, up = first(True)()
        return end(sequence_job, layers, kept, back, (), up, cosine, sine, replicas)

    box = single() if turns == 1 else lax.cond(count > 1, several, single)
    grad_down, grad_up = placed(box.reshape(replicas * ADAPTER_RANK, box.shape[2]), columns, piece_width)
    return (grad_down[None], grad_up[None])


def solution(mesh):
    split = Mesh(
        mesh.devices.reshape(mesh.shape["segment"], SIDE, SIDE, mesh.shape["dp"]),
        (SEG, Z, X, "dp"),
    )
    return jax.shard_map(
        shards,
        mesh=split,
        in_specs=(
            P("dp", TENSOR, None),
            P("dp", TENSOR, None),
            P("dp"),
            P(),
            P(SEG, None),
            P(SEG, None, TENSOR),
            P(SEG, None, TENSOR),
            P(SEG, None, TENSOR),
            P(SEG, TENSOR, None),
            P(SEG, TENSOR, None),
            P(SEG, None, TENSOR),
        ),
        out_specs=(P(SEG, TENSOR, None), P(SEG, None, TENSOR)),
        check_vma=False,
    )
```
